128 devices in a mesh: tiles: 128 (over x, z, y, core).
Axes of the slice: x: 4, y: 4, z: 4, core: 2. Of those that a mesh axis runs over, the one named last changes fastest.
Arguments:
- primal_start: float32 [256, 512, 1024], P('tiles'), may hold values from 0 to 1
- cost: bfloat16 [256, 512, 1024], P('tiles'), may hold values from -4 to 4
- mask: int32 [256, 64, 8], P('tiles'), may hold values 0 or 1
- tile_adv: int32 [256], P('tiles'), may hold values from -1 to 127, as said below
- tile_slot: int32 [256], P('tiles'), may hold values from -1 to 127
- adv_dual: float32 [128, 512], P('tiles'), may hold values from 0 to 2
- slot_dual: float32 [128, 1024], P('tiles'), may hold values from 0 to 2
- spend_limit: float32 [128, 512], P('tiles'), may hold values from 204 to 921
- capacity: float32 [128, 1024], P('tiles'), may hold values from 64 to 384
Outputs:
- primal: float32 [256, 512, 1024], P('tiles')
- adv_out: float32 [128, 512], P('tiles')
- slot_out: float32 [128, 1024], P('tiles')
The draws below stay inside these ranges and needn't reach their ends.
Inputs may be any that keep to these rules, and one draw needn't show every extreme that they name: -1 marks an empty tile slot; tile_adv and tile_slot are -1 at the same slots. Each device's 2 slots hold 1 to 2 tiles, in its first slots, and some device holds exactly 2.
All inputs are finite; a program needn't handle non-finite values. No bound on the sum of `mask` on one device may be relied on, other than what follows from the above.
Results may differ from the reference program's by a relative error of at most 0.0003.
Values sent between devices are 32-bit elements; how exact they have to be, the bound alone decides.
No kernel may reach another device: no remote copies, remote signals or barrier semaphores. Data moves between devices by JAX's collectives and lax.ppermute only.
A program may use at most 64 MiB of HBM per device.

```python
import jax
import jax.numpy as jnp
from jax import lax

ROWS = 512
COLS = 1024
MB_ROWS = 8
MB_COLS = 128
ITERS = 2
CAP = 2
TILE_SLOTS = 256
ADV_BLOCKS = 128
SLOT_BLOCKS = 128
MASK_R = 64
MASK_C = 8


def tile_layout(key):
    base = jax.random.fold_in(key, 11)
    subkeys = jax.random.split(base, 6)
    owners = TILE_SLOTS // CAP
    drawn = jax.random.randint(subkeys[0], (owners,), 0, 5)
    counts = jnp.where(drawn < 3, 1, jnp.where(drawn < 4, min(2, CAP), CAP))
    fuller = jax.random.randint(subkeys[1], (), 0, owners)
    counts = jnp.where(jnp.arange(owners) == fuller, CAP, counts)
    places = jnp.arange(CAP)
    occupied = (places[None, :] < counts[:, None]).reshape(TILE_SLOTS)
    adv_drawn = jax.random.randint(subkeys[2], (TILE_SLOTS,), 0, ADV_BLOCKS)
    hot_blocks = jax.random.randint(subkeys[3], (4,), 0, SLOT_BLOCKS)
    choose = jax.random.randint(subkeys[4], (TILE_SLOTS,), 0, 8)
    spread = jax.random.randint(subkeys[5], (TILE_SLOTS,), 0, SLOT_BLOCKS)
    slot_drawn = jnp.where(choose < 4, hot_blocks[jnp.minimum(choose, 3)], spread)
    adv_ids = jnp.where(occupied, adv_drawn, -1).astype(jnp.int32)
    slot_ids = jnp.where(occupied, slot_drawn, -1).astype(jnp.int32)
    return (adv_ids, slot_ids)


def draw_tile_adv(key, part):
    return tile_layout(key)[0]


def draw_tile_slot(key, part):
    return tile_layout(key)[1]


def place_ends(array, key, low, high):
    index_at = [jax.random.randint(jax.random.fold_in(key, axis), (), 0, length) for axis, length in enumerate(array.shape)]
    main_axis = array.shape.index(max(array.shape))
    beside = index_at[:main_axis] + [(index_at[main_axis] + 1) % array.shape[main_axis]] + index_at[main_axis + 1:]
    return array.at[tuple(index_at)].set(low).at[tuple(beside)].set(high)


def levels(stream_key, shape, pieces, low, high):
    def one(axis_at, parts):
        draws = jax.random.uniform(jax.random.fold_in(jax.random.fold_in(stream_key, 6), axis_at), (parts,), jnp.float32, low / len(pieces), high / len(pieces))
        return jnp.repeat(jnp.exp(draws), shape[axis_at] // parts).reshape((-1,) + (1,) * (len(shape) - axis_at - 1))

    gain = one(*pieces[0])
    for cut in pieces[1:]:
        gain = gain * one(*cut)
    return gain


def bell_draw(rng, extent, scale, bound, cuts=(), kind=jnp.bfloat16):
    entries = scale * jax.random.normal(rng, extent, jnp.float32)
    if cuts:
        entries = entries * levels(rng, extent, cuts, -0.22, 0.18)
    return jnp.clip(entries, -bound, bound).astype(kind)


def setup_inputs(seed: int = 0) -> dict:
    streams_of = jax.random.split(jax.random.key(seed), 10)
    return {
        "primal_start": jnp.clip(1.0 * jax.random.uniform(streams_of[0], (TILE_SLOTS, ROWS, COLS), jnp.float32) ** levels(streams_of[0], (TILE_SLOTS, ROWS, COLS), ((0, 128),), -0.2, 0.2), 0.0, 1.0),
        "cost": bell_draw(streams_of[1], (TILE_SLOTS, ROWS, COLS), 1.0, 4.0, ((0, 128),)),
        "mask": place_ends((jax.random.randint(streams_of[2], (TILE_SLOTS, MASK_R, MASK_C), 0, 4) < 3).astype(jnp.int32), jax.random.fold_in(streams_of[2], 1), 0, 1),
        "tile_adv": draw_tile_adv(jax.random.fold_in(streams_of[9], 71), 0),
        "tile_slot": draw_tile_slot(jax.random.fold_in(streams_of[9], 71), 0),
        "adv_dual": jnp.clip(2.0 * jax.random.uniform(streams_of[5], (ADV_BLOCKS, ROWS), jnp.float32) ** levels(streams_of[5], (ADV_BLOCKS, ROWS), ((0, 128),), -0.2, 0.2), 0.0, 2.0),
        "slot_dual": jnp.clip(2.0 * jax.random.uniform(streams_of[6], (SLOT_BLOCKS, COLS), jnp.float32) ** levels(streams_of[6], (SLOT_BLOCKS, COLS), ((0, 128),), -0.2, 0.2), 0.0, 2.0),
        "spend_limit": jnp.clip(204.0 + 717.0 * jax.random.uniform(streams_of[7], (ADV_BLOCKS, ROWS), jnp.float32) ** levels(streams_of[7], (ADV_BLOCKS, ROWS), ((0, 128),), -0.2, 0.2), 204.0, 921.0),
        "capacity": jnp.clip(64.0 + 320.0 * jax.random.uniform(streams_of[8], (SLOT_BLOCKS, COLS), jnp.float32) ** levels(streams_of[8], (SLOT_BLOCKS, COLS), ((0, 128),), -0.2, 0.2), 64.0, 384.0),
    }


tau_step = 0.5


def expand_mask(blocks):
    values = blocks.astype(jnp.float32)
    rows_in = values.shape[-2]
    cols_in = values.shape[-1]
    shaped = jnp.broadcast_to(values[..., :, None, :, None], values.shape[:-2] + (rows_in, MB_ROWS, cols_in, MB_COLS))
    return shaped.reshape(values.shape[:-2] + (rows_in * MB_ROWS, cols_in * MB_COLS))


def reference(primal_start, cost, mask, tile_adv, tile_slot, adv_dual, slot_dual, spend_limit, capacity):
    highest = lax.Precision.HIGHEST
    adv_onehot = (tile_adv[:, None] == jnp.arange(ADV_BLOCKS, dtype=jnp.int32)[None, :]).astype(jnp.float32)
    slot_onehot = (tile_slot[:, None] == jnp.arange(SLOT_BLOCKS, dtype=jnp.int32)[None, :]).astype(jnp.float32)
    present = (tile_adv >= 0).astype(jnp.float32)
    primal = primal_start
    for sweep_index in range(ITERS):
        adv_rows = jnp.dot(adv_onehot, adv_dual, precision=highest)
        slot_cols = jnp.dot(slot_onehot, slot_dual, precision=highest)
        first_sweep = sweep_index == 0

        def tile_step(items):
            previous, price, blocks, alive_flag, adv_row, slot_col = items
            weight = expand_mask(blocks) * alive_flag
            if first_sweep:
                previous = weight * previous
            update = weight * jnp.clip(previous - tau_step * (price.astype(jnp.float32) + adv_row[:, None] + slot_col[None, :]), 0.0, 1.0)
            extended = 2.0 * update - previous
            return update, jnp.sum(extended, axis=1), jnp.sum(extended, axis=0)

        primal, row_sums, col_sums = lax.map(tile_step, (primal, cost, mask, present, adv_rows, slot_cols))
        row_use = jnp.dot(adv_onehot.T, row_sums, precision=highest)
        col_use = jnp.dot(slot_onehot.T, col_sums, precision=highest)
        adv_dual = jnp.maximum(adv_dual + (row_use - spend_limit) / COLS, 0.0)
        slot_dual = jnp.maximum(slot_dual + (col_use - capacity) / ROWS, 0.0)
    return primal, adv_dual, slot_dual
```

```python
import functools

import jax
import jax.numpy as jnp
from jax import lax
from jax.experimental import pallas as pl
from jax.experimental.pallas import tpu as pltpu
from jax.sharding import PartitionSpec as P

DEV = 128
XZ = 16
YC = 8
L = 128
AR = 4
SR = 8
REC = AR + SR + 1
TS = 2 * (AR + SR)
MSG = TS + SR + AR
RB = 128
NRB = 4

XZ_GROUPS = [[j * YC + q for j in range(XZ)] for q in range(YC)]
YC_GROUPS = [[j * YC + q for q in range(YC)] for j in range(XZ)]

VMEM_WHOLE = pl.BlockSpec(memory_space=pltpu.VMEM)
SMEM_WHOLE = pl.BlockSpec(memory_space=pltpu.SMEM)


def spread_rows(row, buf):
    for b in range(NRB):
        block = jnp.broadcast_to(row[b : b + 1, :], (L, L))
        buf[b * L : (b + 1) * L, :] = block.T


def sweep_block(w_ref, t, rb, p_ref, c_ref, out_ref, a_buf, s_buf, r_buf, col_buf, first):
    def step(g, cols):
        r0 = pl.multiple_of(g * 16, 16)
        cols = list(cols)
        racc = [None, None]
        for cb in range(SR):
            lanes = pl.ds(cb * L, L)
            c16 = c_ref[0, pl.ds(r0, 16), lanes].astype(jnp.float32)
            s = s_buf[pl.ds(cb * 8, 8), :]
            for h in range(2):
                rows = pl.ds(pl.multiple_of(r0 + 8 * h, 8), 8)
                w = w_ref[t * 512 + (rb * 16 + g * 2 + h) * SR + cb]
                p = p_ref[0, rows, lanes]
                if first:
                    p = p * w
                arow = a_buf[pl.ds(pl.multiple_of(rb * RB + r0 + 8 * h, 8), 8), :]
                v = p - 0.5 * ((c16[8 * h : 8 * h + 8] + arow) + s)
                u = jnp.minimum(jnp.maximum(v, 0.0), w)
                out_ref[0, rows, lanes] = u
                e = (u + u) - p
                racc[h] = e if racc[h] is None else racc[h] + e
                cols[cb] = cols[cb] + e
        for h in range(2):
            r_buf[pl.ds(pl.multiple_of(r0 + 8 * h, 8), 8), :] = racc[h]
        return tuple(cols)

    cols = tuple(col_buf[pl.ds(cb * 8, 8), :] for cb in range(SR))
    cols = lax.fori_loop(0, RB // 16, step, cols)
    for cb in range(SR):
        col_buf[pl.ds(cb * 8, 8), :] = cols[cb]


def begin_tile(arow, srow, a_buf, s_buf, col_buf):
    spread_rows(arow, a_buf)
    for cb in range(SR):
        s_buf[cb * 8 : (cb + 1) * 8, :] = jnp.broadcast_to(srow[cb : cb + 1, :], (8, L))
    col_buf[...] = jnp.zeros_like(col_buf)


def keep_sums(t, rb, r_buf, col_buf, sums):
    sums[pl.ds(t * AR + rb, 1), :] = jnp.sum(r_buf[...].T, axis=0, keepdims=True)

    @pl.when(rb == NRB - 1)
    def _():
        rows = [jnp.sum(col_buf[cb * 8 : (cb + 1) * 8, :], axis=0, keepdims=True) for cb in range(SR)]
        sums[pl.ds(pl.multiple_of(8 + t * SR, 8), SR), :] = jnp.concatenate(rows, axis=0)


def first_kernel(adv_id, slot_id, w_ref, rec, own_adv, own_slot, limit, cap, p_ref, c_ref, out_ref, msg, a_buf, s_buf, r_buf, col_buf, sums):
    t = pl.program_id(0)
    rb = pl.program_id(1)

    @pl.when(rb == 0)
    def _():
        a = jnp.maximum(adv_id[t], 0) * REC
        s = jnp.maximum(slot_id[t], 0) * REC + AR
        begin_tile(rec[pl.ds(a, AR), :], rec[pl.ds(s, SR), :], a_buf, s_buf, col_buf)

    sweep_block(w_ref, t, rb, p_ref, c_ref, out_ref, a_buf, s_buf, r_buf, col_buf, True)
    keep_sums(t, rb, r_buf, col_buf, sums)

    @pl.when((t == 1) & (rb == NRB - 1))
    def _():
        data = jnp.concatenate(
            [sums[...], own_slot[...] * 512.0 - cap[...], own_adv[...] * 1024.0 - limit[...]], axis=0
        )
        for j in range(XZ):
            msg[j * MSG : (j + 1) * MSG, :] = data


def second_kernel(w_ref, rec, p_ref, c_ref, out_ref, msg, own, a_buf, s_buf, r_buf, col_buf, sums, dual):
    t = pl.program_id(0)
    rb = pl.program_id(1)

    @pl.when((t == 0) & (rb == 0))
    def _():
        total = rec[0:MSG, :]
        for q in range(1, YC):
            total = total + rec[q * MSG : (q + 1) * MSG, :]
        dual[0:8, :] = jnp.maximum(total[0:8] * (1.0 / 1024), 0.0)
        dual[8:32, :] = jnp.maximum(total[8:32] * (1.0 / 512), 0.0)
        dual[32:36, :] = jnp.maximum(total[32:36] * (1.0 / 1024), 0.0)
        own[...] = dual[24:36, :]

    @pl.when(rb == 0)
    def _():
        begin_tile(
            dual[pl.ds(t * AR, AR), :], dual[pl.ds(pl.multiple_of(8 + t * SR, 8), SR), :], a_buf, s_buf, col_buf
        )

    sweep_block(w_ref, t, rb, p_ref, c_ref, out_ref, a_buf, s_buf, r_buf, col_buf, False)
    keep_sums(t, rb, r_buf, col_buf, sums)

    @pl.when((t == 1) & (rb == NRB - 1))
    def _():
        data = sums[...]
        for j in range(XZ):
            msg[j * TS : (j + 1) * TS, :] = data


def scatter(ids, yc, rec, size, acc_a, acc_s):
    acc_a[...] = jnp.zeros_like(acc_a)
    acc_s[...] = jnp.zeros_like(acc_s)
    for j in range(XZ):
        dev = j * YC + yc
        for k in range(2):
            a = ids[dev * 4 + k]
            a = pl.multiple_of(jnp.where(a < 0, DEV, a) * 8, 8)
            acc_a[pl.ds(a, AR), :] += rec[j * size + AR * k : j * size + AR * (k + 1), :]
            s = ids[dev * 4 + 2 + k]
            s = pl.multiple_of(jnp.where(s < 0, DEV, s) * 8, 8)
            acc_s[pl.ds(s, SR), :] += rec[j * size + 8 + SR * k : j * size + 8 + SR * (k + 1), :]
        if size == MSG:
            d = pl.multiple_of(dev * 8, 8)
            acc_s[pl.ds(d, SR), :] += rec[j * size + 24 : j * size + 32, :]
            acc_a[pl.ds(d, AR), :] += rec[j * size + 32 : j * size + 36, :]


def users_kernel(ids, me, rec, out, acc_a, acc_s):
    scatter(ids, me[1], rec, MSG, acc_a, acc_s)
    for q in range(YC):
        dev = me[0] * YC + q
        o = q * MSG
        for k in range(2):
            a = ids[dev * 4 + k]
            a = pl.multiple_of(jnp.where(a < 0, DEV, a) * 8, 8)
            out[o + AR * k : o + AR * (k + 1), :] = acc_a[pl.ds(a, AR), :]
            s = ids[dev * 4 + 2 + k]
            s = pl.multiple_of(jnp.where(s < 0, DEV, s) * 8, 8)
            out[o + 8 + SR * k : o + 8 + SR * (k + 1), :] = acc_s[pl.ds(s, SR), :]
        d = pl.multiple_of(dev * 8, 8)
        out[o + 24 : o + 32, :] = acc_s[pl.ds(d, SR), :]
        out[o + 32 : o + 36, :] = acc_a[pl.ds(d, AR), :]


def owners_kernel(ids, me, rec, out, acc_a, acc_s):
    scatter(ids, me[1], rec, TS, acc_a, acc_s)
    for q in range(YC):
        d = pl.multiple_of((me[0] * YC + q) * 8, 8)
        o = q * (AR + SR)
        out[o : o + SR, :] = acc_s[pl.ds(d, SR), :]
        out[o + SR : o + SR + AR, :] = acc_a[pl.ds(d, AR), :]


def last_kernel(rec, own, limit, cap, adv_out, slot_out):
    n = AR + SR
    total = rec[0:n, :]
    for q in range(1, YC):
        total = total + rec[q * n : (q + 1) * n, :]
    slot_out[...] = jnp.maximum(own[0:SR, :] + (total[0:SR] - cap[...]) * (1.0 / 512), 0.0)
    adv_out[...] = jnp.maximum(own[SR:n, :] + (total[SR:n] - limit[...]) * (1.0 / 1024), 0.0)


def f32(*shape):
    return jax.ShapeDtypeStruct(shape, jnp.float32)


def sweep_scratch():
    return [
        pltpu.VMEM((512, L), jnp.float32),
        pltpu.VMEM((64, L), jnp.float32),
        pltpu.VMEM((RB, L), jnp.float32),
        pltpu.VMEM((64, L), jnp.float32),
        pltpu.VMEM((TS, L), jnp.float32),
    ]


def tile_spec(n):
    return pl.BlockSpec((1, RB, 1024), lambda t, rb: (t, rb, 0))


def exchange(x, groups):
    n = x.shape[0]
    return lax.all_to_all(x, "tiles", 0, 0, axis_index_groups=groups, tiled=True)


TABLE = [pltpu.VMEM(((DEV + 1) * 8, L), jnp.float32), pltpu.VMEM(((DEV + 1) * 8, L), jnp.float32)]


def body(primal_start, cost, mask, tile_adv, tile_slot, adv_dual, slot_dual, spend_limit, capacity):
    own_adv = adv_dual.reshape(AR, L)
    own_slot = slot_dual.reshape(SR, L)
    limit = spend_limit.reshape(AR, L)
    cap = capacity.reshape(SR, L)
    index = lax.axis_index("tiles")
    me = jnp.stack([index // YC, index % YC]).astype(jnp.int32)
    present = (tile_adv >= 0).astype(jnp.float32)
    weight = (mask.astype(jnp.float32) * present[:, None, None]).reshape(-1)

    ids_row = jnp.pad(jnp.concatenate([tile_adv, tile_slot]).astype(jnp.float32), (0, L - 4))
    message = jnp.concatenate([adv_dual.reshape(-1), slot_dual.reshape(-1), ids_row])
    table = exchange(jnp.broadcast_to(message[None, :], (DEV, REC * L)), None)
    ids = table[:, (REC - 1) * L : (REC - 1) * L + 4].astype(jnp.int32).reshape(-1)

    update, sums = pl.pallas_call(
        first_kernel,
        grid=(2, NRB),
        in_specs=[SMEM_WHOLE] * 3 + [VMEM_WHOLE] * 5 + [tile_spec(0), tile_spec(0)],
        out_specs=[tile_spec(0), VMEM_WHOLE],
        out_shape=[f32(2, 512, 1024), f32(XZ * MSG, L)],
        scratch_shapes=sweep_scratch(),
        name="first",
    )(tile_adv, tile_slot, weight, table.reshape(DEV * REC, L), own_adv, own_slot, limit, cap, primal_start, cost)

    part = exchange(sums.reshape(XZ, MSG * L), XZ_GROUPS)
    wanted = pl.pallas_call(
        users_kernel,
        in_specs=[SMEM_WHOLE] * 2 + [VMEM_WHOLE],
        out_specs=VMEM_WHOLE,
        out_shape=f32(YC * MSG, L),
        scratch_shapes=TABLE,
        name="users",
    )(ids, me, part.reshape(XZ * MSG, L))
    duals = exchange(wanted.reshape(YC, MSG * L), YC_GROUPS)

    primal, sums, own = pl.pallas_call(
        second_kernel,
        grid=(2, NRB),
        in_specs=[SMEM_WHOLE, VMEM_WHOLE, tile_spec(0), tile_spec(0)],
        out_specs=[tile_spec(0), VMEM_WHOLE, VMEM_WHOLE],
        out_shape=[f32(2, 512, 1024), f32(XZ * TS, L), f32(AR + SR, L)],
        scratch_shapes=sweep_scratch() + [pltpu.VMEM((MSG, L), jnp.float32)],
        name="second",
    )(weight, duals.reshape(YC * MSG, L), update, cost)

    part = exchange(sums.reshape(XZ, TS * L), XZ_GROUPS)
    wanted = pl.pallas_call(
        owners_kernel,
        in_specs=[SMEM_WHOLE] * 2 + [VMEM_WHOLE],
        out_specs=VMEM_WHOLE,
        out_shape=f32(YC * (AR + SR), L),
        scratch_shapes=TABLE,
        name="owners",
    )(ids, me, part.reshape(XZ * TS, L))
    last = exchange(wanted.reshape(YC, (AR + SR) * L), YC_GROUPS)

    adv_out, slot_out = pl.pallas_call(
        last_kernel,
        in_specs=[VMEM_WHOLE] * 4,
        out_specs=[VMEM_WHOLE] * 2,
        out_shape=[f32(AR, L), f32(SR, L)],
        name="last",
    )(last.reshape(YC * (AR + SR), L), own, limit, cap)
    return primal, adv_out.reshape(1, 512), slot_out.reshape(1, 1024)


def solution(mesh):
    return jax.shard_map(
        body,
        mesh=mesh,
        in_specs=(
            P("tiles", None, None),
            P("tiles", None, None),
            P("tiles", None, None),
            P("tiles"),
            P("tiles"),
            P("tiles", None),
            P("tiles", None),
            P("tiles", None),
            P("tiles", None),
        ),
        out_specs=(P("tiles", None, None), P("tiles", None), P("tiles", None)),
        check_vma=False,
    )
```

```python
import jax
import jax.numpy as jnp
from jax import lax
from jax.experimental import pallas as pl
from jax.experimental.pallas import tpu as pltpu
from jax.sharding import PartitionSpec as P

CHIPS = 64
BLOCKS = 128
L = 128
AR = 4
SR = 8
OWN = AR + SR + 1
REC = 2 * OWN
TS = 2 * (AR + SR)
MSG = TS + SR + AR
OUT = SR + AR
RB = 128
NRB = 4
BIG = 1e30

CORE_GROUPS = [[j * 2 + c for j in range(CHIPS)] for c in range(2)]
PARTNERS = [(i, i ^ 1) for i in range(2 * CHIPS)]

IN_VMEM = pl.BlockSpec(memory_space=pltpu.VMEM)
IN_SMEM = pl.BlockSpec(memory_space=pltpu.SMEM)


def own_kernel(adv_id, slot_id, adv, slot, limit, cap, mask_hbm, out, bias, bounds, ids, mask, sem):
    keep_mask = pltpu.make_async_copy(mask_hbm, mask, sem)
    keep_mask.start()
    lane = lax.broadcasted_iota(jnp.int32, (1, L), 1)
    row = jnp.zeros((1, L), jnp.int32)
    for k, v in enumerate((adv_id[0], adv_id[1], slot_id[0], slot_id[1])):
        row = jnp.where(lane == k, v, row)
        ids[k] = v
    out[0:AR, :] = adv[...]
    out[AR : AR + SR, :] = slot[...]
    out[AR + SR : OWN, :] = row.astype(jnp.float32)
    bias[0:SR, :] = slot[...] * 512.0 - cap[...]
    bias[SR:OUT, :] = adv[...] * 1024.0 - limit[...]
    bounds[0:SR, :] = cap[...]
    bounds[SR:OUT, :] = limit[...]
    keep_mask.wait()


def repeat_kernel(own, other, out):
    a = own[...]
    b = other[...]
    for j in range(CHIPS):
        out[j * REC : j * REC + OWN, :] = a
        out[j * REC + OWN : (j + 1) * REC, :] = b


def spread_half(row, buf):
    for b in range(NRB):
        block = jnp.broadcast_to(0.5 * row[b : b + 1, :], (L, L))
        buf[b * L : (b + 1) * L, :] = block.T


def tree(xs):
    while len(xs) > 1:
        xs = [xs[i] + xs[i + 1] for i in range(0, len(xs), 2)]
    return xs[0]


def write_sums(t, sums, r_buf, cols):
    for b in range(NRB):
        sums[t * AR + b : t * AR + b + 1, :] = jnp.sum(r_buf[b * L : (b + 1) * L, :].T, axis=0, keepdims=True)
    rows = [jnp.sum(c, axis=0, keepdims=True) for c in cols]
    sums[8 + t * SR : 8 + (t + 1) * SR, :] = jnp.concatenate(rows, axis=0)


def slot_rows(srow):
    return [jnp.broadcast_to(0.5 * srow[cb : cb + 1, :], (8, L)) for cb in range(SR)]


ZEROS = lambda: (jnp.zeros((8, L), jnp.float32),) * SR


def first_tile(t, alive, mask, arow, srow, p_ref, c_ref, out, usum, esum, a_buf, r_buf, e_buf, ready):
    spread_half(arow, a_buf)
    s = slot_rows(srow)

    def step(g, carry):
        ucols, ecols = list(carry[0]), list(carry[1])
        us = [[], []]
        es = [[], []]
        r0 = pl.multiple_of(g * 16, 16)
        for cb in range(SR):
            lanes = pl.ds(cb * L, L)
            c16 = 0.5 * c_ref[t, pl.ds(r0, 16), lanes].astype(jnp.float32)
            for h in range(2):
                rows = pl.ds(pl.multiple_of(r0 + 8 * h, 8), 8)
                here = (mask[t, cb, g * 2 + h] > 0) & alive
                p = jnp.minimum(p_ref[t, rows, lanes], jnp.where(here, 1.0, 0.0))
                hc = jnp.maximum(c16[8 * h : 8 * h + 8], jnp.where(here, -BIG, BIG))
                u = jnp.minimum(jnp.maximum(((p - hc) - a_buf[rows, :]) - s[cb], 0.0), 1.0)
                out[t, rows, lanes] = u - hc
                e = (u - p) + u
                us[h].append(u)
                es[h].append(e)
                ucols[cb] = ucols[cb] + u
                ecols[cb] = ecols[cb] + e
        for h in range(2):
            rows = pl.ds(pl.multiple_of(r0 + 8 * h, 8), 8)
            r_buf[rows, :] = tree(us[h])
            e_buf[rows, :] = tree(es[h])
        return tuple(ucols), tuple(ecols)

    ucols, ecols = ZEROS(), ZEROS()
    for b in range(NRB):
        ready(t, b)
        ucols, ecols = lax.fori_loop(b * 8, (b + 1) * 8, step, (ucols, ecols))
    write_sums(t, usum, r_buf, ucols)
    write_sums(t, esum, e_buf, ecols)


def first_kernel(own_ids, mask, rec, bias, p_hbm, c_hbm, out, usum, msg, ids, p_ref, c_ref, a_buf, r_buf, e_buf, esum, id_buf, p_sems, c_sems, sem):
    def fetch(t, b):
        rows = pl.ds(b * RB, RB)
        n = t * NRB + b
        return (
            pltpu.make_async_copy(p_hbm.at[t, rows, :], p_ref.at[t, rows, :], p_sems.at[n]),
            pltpu.make_async_copy(c_hbm.at[t, rows, :], c_ref.at[t, rows, :], c_sems.at[n]),
        )

    for t in range(2):
        for b in range(NRB):
            for copy in fetch(t, b):
                copy.start()

    def ready(t, b):
        for copy in fetch(t, b):
            copy.wait()

    core = lax.axis_index("tiles") & 1
    both = jnp.concatenate(
        [rec[pl.ds(OWN - 1, CHIPS, stride=REC), :], rec[pl.ds(REC - 1, CHIPS, stride=REC), :]], axis=0
    )
    id_buf[...] = both.T[0:8, :].astype(jnp.int32)
    keep_ids = pltpu.make_async_copy(id_buf, ids, sem)
    keep_ids.start()
    for t in range(2):
        alive = own_ids[t] >= 0
        a = jnp.maximum(own_ids[t], 0)
        a = (a >> 1) * REC + jnp.where((a & 1) == core, 0, OWN)
        s = jnp.maximum(own_ids[2 + t], 0)
        s = (s >> 1) * REC + jnp.where((s & 1) == core, AR, OWN + AR)
        arow, srow = rec[pl.ds(a, AR), :], rec[pl.ds(s, SR), :]
        first_tile(t, alive, mask, arow, srow, p_ref, c_ref, out, usum, esum, a_buf, r_buf, e_buf, ready)
    data = jnp.concatenate([esum[...], bias[...]], axis=0)
    for j in range(CHIPS):
        msg[j * MSG : (j + 1) * MSG, :] = data
    keep_ids.wait()


def users_kernel(ids, rec, mine, other, acc_a0, acc_a1, acc_s0, acc_s1):
    me = lax.axis_index("tiles")
    chip = me >> 1
    core = me & 1

    def at(i):
        return pl.multiple_of(jnp.where(i < 0, BLOCKS, i) * 8, 8)

    wanted = []
    for side, out, index in ((0, mine, me), (CHIPS, other, me ^ 1)):
        adv = [(ids[k, side + chip], AR * k) for k in range(2)] + [(index, TS + SR)]
        slot = [(ids[2 + k, side + chip], 8 + SR * k) for k in range(2)] + [(index, TS)]
        wanted.append((out, adv, slot))
    zero = jnp.zeros((8, L), jnp.float32)
    for _, adv, slot in wanted:
        for i, _ in adv:
            acc_a0[pl.ds(at(i), 8), :] = zero
            acc_a1[pl.ds(at(i), 8), :] = zero
        for i, _ in slot:
            acc_s0[pl.ds(at(i), 8), :] = zero
            acc_s1[pl.ds(at(i), 8), :] = zero
    for j in range(CHIPS):
        for k, acc in ((0, acc_a0), (1, acc_a1)):
            rows = pl.ds(at(ids[k, j]), AR)
            acc[rows, :] = acc[rows, :] + rec[j * MSG + AR * k : j * MSG + AR * (k + 1), :]
        for k, acc in ((0, acc_s0), (1, acc_s1)):
            rows = pl.ds(at(ids[2 + k, j]), SR)
            acc[rows, :] = acc[rows, :] + rec[j * MSG + 8 + SR * k : j * MSG + 8 + SR * (k + 1), :]
    for out, adv, slot in wanted:
        for i, o in adv:
            b = jnp.maximum(i, 0)
            bias = rec[pl.ds((b >> 1) * MSG + TS + SR, AR), :] * jnp.where((b & 1) == core, 1.0, 0.0)
            rows = pl.ds(at(i), AR)
            out[o : o + AR, :] = (acc_a0[rows, :] + acc_a1[rows, :]) + bias
        for i, o in slot:
            b = jnp.maximum(i, 0)
            bias = rec[pl.ds((b >> 1) * MSG + TS, SR), :] * jnp.where((b & 1) == core, 1.0, 0.0)
            rows = pl.ds(at(i), SR)
            out[o : o + SR, :] = (acc_s0[rows, :] + acc_s1[rows, :]) + bias


def second_tile(t, arow, srow, base, out, usum, a_buf, r_buf, done):
    spread_half(arow, a_buf)
    s = slot_rows(srow)

    def step(g, cols):
        rows = pl.ds(pl.multiple_of(g * 8, 8), 8)
        a = a_buf[rows, :]
        cols = list(cols)
        us = []
        for cb in range(SR):
            lanes = pl.ds(cb * L, L)
            u = jnp.minimum(jnp.maximum((base[t, rows, lanes] - a) - s[cb], 0.0), 1.0)
            out[t, rows, lanes] = u
            cols[cb] = cols[cb] + u
            us.append(u)
        r_buf[rows, :] = tree(us)
        return tuple(cols)

    cols = ZEROS()
    for b in range(NRB):
        cols = lax.fori_loop(b * 16, (b + 1) * 16, step, cols, unroll=4)
        done(t, b)
    write_sums(t, usum, r_buf, cols)


def second_kernel(mine, other, base, psum, primal, sums, own, out, usum, a_buf, r_buf, sems):
    def keep(t, b):
        rows = pl.ds(b * RB, RB)
        return pltpu.make_async_copy(out.at[t, rows, :], primal.at[t, rows, :], sems.at[t * NRB + b])

    total = mine[...] + other[...]
    adv = jnp.maximum(total[0:8] * (1.0 / 1024), 0.0)
    slot = jnp.maximum(total[8:32] * (1.0 / 512), 0.0)
    own[0:SR, :] = slot[16:24]
    own[SR:OUT, :] = jnp.maximum(total[32:36] * (1.0 / 1024), 0.0)
    for t in range(2):
        second_tile(
            t, adv[4 * t : 4 * t + 4], slot[8 * t : 8 * t + 8], base, out, usum, a_buf, r_buf, lambda t, b: keep(t, b).start()
        )
    sums[...] = 2.0 * usum[...] - psum[...]
    for t in range(2):
        for b in range(NRB):
            keep(t, b).wait()


def owners_kernel(ids, mine, other, out):
    me = lax.axis_index("tiles")
    chip = me >> 1
    core = me & 1
    out[...] = jnp.zeros_like(out)
    for side, rec in ((0, mine), (CHIPS, other)):
        for k in range(2):
            for i, o, n, src in (
                (ids[k, side + chip], SR, AR, AR * k),
                (ids[2 + k, side + chip], 0, SR, 8 + SR * k),
            ):

                @pl.when((i >= 0) & ((i & 1) == core))
                def _():
                    rows = pl.ds((i >> 1) * OUT + o, n)
                    out[rows, :] = out[rows, :] + rec[src : src + n, :]


def last_kernel(rec, own, bounds, adv_out, slot_out):
    n = 2 * OUT
    parts = [rec[g * n : (g + 1) * n, :] for g in range(CHIPS // 2)]
    total = tree(parts)
    total = total[0:OUT] + total[OUT:n]
    slot_out[...] = jnp.maximum(own[0:SR, :] + (total[0:SR] - bounds[0:SR, :]) * (1.0 / 512), 0.0)
    adv_out[...] = jnp.maximum(own[SR:OUT, :] + (total[SR:OUT] - bounds[SR:OUT, :]) * (1.0 / 1024), 0.0)


def f32(*shape):
    return jax.ShapeDtypeStruct(shape, jnp.float32)


def vmem(*shape):
    return pltpu.VMEM(shape, jnp.float32)


def in_vmem(x):
    return pltpu.with_memory_space_constraint(x, pltpu.VMEM)


def in_smem(x):
    return pltpu.with_memory_space_constraint(x, pltpu.SMEM)


def call(kernel, name, ins, outs, scratch=(), mib=4):
    return pl.pallas_call(
        kernel,
        in_specs=[s for _, s in ins],
        out_specs=[s for _, s in outs],
        out_shape=[o for o, _ in outs],
        scratch_shapes=list(scratch),
        compiler_params=pltpu.CompilerParams(vmem_limit_bytes=mib << 20),
        name=name,
    )(*[x for x, _ in ins])


def in_hbm(x):
    return pltpu.with_memory_space_constraint(x, pltpu.HBM)


def hbm_arg(x):
    return (in_hbm(x), pl.BlockSpec(memory_space=pl.ANY))


def smem_out(*shape):
    return (pltpu.SMEM(shape, jnp.int32), IN_SMEM)


def smem_arg(x):
    return (in_smem(x), IN_SMEM)


def vmem_arg(x):
    return (in_vmem(x), IN_VMEM)


def vmem_out(*shape):
    return (vmem(*shape), IN_VMEM)


def exchange(x, rows):
    x = x.reshape(CHIPS, rows * L)
    x = lax.all_to_all(x, "tiles", 0, 0, axis_index_groups=CORE_GROUPS, tiled=True)
    return vmem_arg(x.reshape(CHIPS * rows, L))


def swap(x):
    return lax.ppermute(x, "tiles", PARTNERS)


def body(primal_start, cost, mask, tile_adv, tile_slot, adv_dual, slot_dual, spend_limit, capacity):
    tile = (2, 512, 1024)
    own, bias, bounds, own_ids, here = call(
        own_kernel,
        "own",
        [(in_hbm(tile_adv), IN_SMEM), (in_hbm(tile_slot), IN_SMEM)]
        + [(in_hbm(x.reshape(-1, L)), IN_VMEM) for x in (adv_dual, slot_dual, spend_limit, capacity)]
        + [hbm_arg(mask.transpose(0, 2, 1))],
        [vmem_out(OWN, L), vmem_out(OUT, L), vmem_out(OUT, L), smem_out(4), smem_out(2, 8, 64)],
        [pltpu.SemaphoreType.DMA(())],
    )
    (message,) = call(repeat_kernel, "repeat", [vmem_arg(own), vmem_arg(swap(own))], [vmem_out(CHIPS * REC, L)])
    table = exchange(message, REC)

    base, usum, message, ids = call(
        first_kernel,
        "first",
        [smem_arg(own_ids), smem_arg(here), table, vmem_arg(bias), hbm_arg(primal_start), hbm_arg(cost)],
        [vmem_out(*tile), vmem_out(TS, L), vmem_out(CHIPS * MSG, L), smem_out(8, L)],
        [vmem(*tile), pltpu.VMEM(tile, jnp.bfloat16)]
        + [vmem(512, L)] * 3
        + [vmem(TS, L), pltpu.VMEM((8, L), jnp.int32)]
        + [pltpu.SemaphoreType.DMA((2 * NRB,))] * 2
        + [pltpu.SemaphoreType.DMA(())],
        8,
    )
    part = exchange(message, MSG)
    mine, other = call(
        users_kernel,
        "users",
        [smem_arg(ids), part],
        [vmem_out(MSG, L), vmem_out(MSG, L)],
        [vmem((BLOCKS + 1) * 8, L)] * 4,
    )

    primal, sums, own = call(
        second_kernel,
        "second",
        [vmem_arg(mine), vmem_arg(swap(other)), vmem_arg(base), vmem_arg(usum)],
        [(f32(*tile), pl.BlockSpec(memory_space=pl.ANY)), vmem_out(TS, L), vmem_out(OUT, L)],
        [vmem(*tile), vmem(TS, L), vmem(512, L), vmem(512, L), pltpu.SemaphoreType.DMA((2 * NRB,))],
        8,
    )
    (message,) = call(
        owners_kernel, "owners", [smem_arg(ids), vmem_arg(sums), vmem_arg(swap(sums))], [vmem_out(CHIPS * OUT, L)]
    )
    adv_out, slot_out = call(
        last_kernel,
        "last",
        [exchange(message, OUT), vmem_arg(own), vmem_arg(bounds)],
        [(f32(AR, L), IN_VMEM), (f32(SR, L), IN_VMEM)],
    )
    return primal, adv_out.reshape(1, 512), slot_out.reshape(1, 1024)


def solution(mesh):
    return jax.shard_map(
        body,
        mesh=mesh,
        in_specs=(
            P("tiles", None, None),
            P("tiles", None, None),
            P("tiles", None, None),
            P("tiles"),
            P("tiles"),
            P("tiles", None),
            P("tiles", None),
            P("tiles", None),
            P("tiles", None),
        ),
        out_specs=(P("tiles", None, None), P("tiles", None), P("tiles", None)),
        check_vma=False,
    )
```

```python
import jax
import jax.numpy as jnp
from jax import lax
from jax.experimental import pallas as pl
from jax.experimental.pallas import tpu as pltpu
from jax.sharding import PartitionSpec as P

CHIPS = 64
BLOCKS = 128
L = 128
AR = 4
SR = 8
OWN = AR + SR + 1
SEL = 2 * (AR + SR) + 8
TS = 2 * (AR + SR)
MSG = TS + SR + AR
OUT = SR + AR
RB = 128
NRB = 4
BIG = 1e30
AHEAD = 3

CORE_GROUPS = [[j * 2 + c for j in range(CHIPS)] for c in range(2)]
PARTNERS = [(i, i ^ 1) for i in range(2 * CHIPS)]

IN_VMEM = pl.BlockSpec(memory_space=pltpu.VMEM)
IN_SMEM = pl.BlockSpec(memory_space=pltpu.SMEM)


def own_kernel(adv_id, slot_id, adv, slot, limit, cap, mask_hbm, out, bias, bounds, row_ids, ids, mask, sem):
    keep_mask = pltpu.make_async_copy(mask_hbm, mask, sem)
    keep_mask.start()
    lane = lax.broadcasted_iota(jnp.int32, (8, L), 1)
    row = jnp.zeros((8, L), jnp.int32)
    for k, v in enumerate((adv_id[0], adv_id[1], slot_id[0], slot_id[1])):
        row = jnp.where(lane == k, v, row)
        ids[k] = v
    row_ids[...] = row
    data = jnp.concatenate([slot[...], adv[...], row[0:1].astype(jnp.float32)], axis=0)
    for j in range(CHIPS):
        out[j * OWN : (j + 1) * OWN, :] = data
    bias[0:SR, :] = slot[...] * 512.0 - cap[...]
    bias[SR:OUT, :] = adv[...] * 1024.0 - limit[...]
    bounds[0:SR, :] = cap[...]
    bounds[SR:OUT, :] = limit[...]
    keep_mask.wait()


def rows_of(rec, i, slot):
    at = (jnp.maximum(i, 0) >> 1) * OWN
    return rec[pl.ds(at, SR), :] if slot else rec[pl.ds(at + SR, AR), :]


def pick_kernel(partner_ids, rec, out):
    lane = lax.broadcasted_iota(jnp.int32, (1, L), 1)
    row = partner_ids[0:1, :]
    wanted = [jnp.max(jnp.where(lane == k, row, -1)) for k in range(4)]
    for k in range(2):
        out[AR * k : AR * (k + 1), :] = rows_of(rec, wanted[k], False)
        out[8 + SR * k : 8 + SR * (k + 1), :] = rows_of(rec, wanted[2 + k], True)
    ids = rec[pl.ds(OWN - 1, CHIPS, stride=OWN), :]
    out[TS:SEL, :] = jnp.concatenate([ids, ids], axis=0).T[0:8, :]


def spread_half(row, buf):
    for b in range(NRB):
        block = jnp.broadcast_to(0.5 * row[b : b + 1, :], (L, L))
        buf[b * L : (b + 1) * L, :] = block.T


def tree(xs):
    while len(xs) > 1:
        xs = [xs[i] + xs[i + 1] for i in range(0, len(xs), 2)]
    return xs[0]


def write_sums(t, sums, r_buf, cols):
    for b in range(NRB):
        sums[t * AR + b : t * AR + b + 1, :] = jnp.sum(r_buf[b * L : (b + 1) * L, :].T, axis=0, keepdims=True)
    rows = [jnp.sum(c, axis=0, keepdims=True) for c in cols]
    sums[8 + t * SR : 8 + (t + 1) * SR, :] = jnp.concatenate(rows, axis=0)


def slot_rows(srow):
    return [jnp.broadcast_to(0.5 * srow[cb : cb + 1, :], (8, L)) for cb in range(SR)]


ZEROS = lambda: (jnp.zeros((8, L), jnp.float32),) * SR


def first_tile(t, alive, mask, arow, srow, p_ref, c_ref, out, usum, psum, a_buf, r_buf, q_buf, ready):
    spread_half(arow, a_buf)
    s = slot_rows(srow)

    def step(g, carry):
        ucols, pcols = list(carry[0]), list(carry[1])
        us = [[], []]
        ps = [[], []]
        r0 = pl.multiple_of(g * 16, 16)
        for cb in range(SR):
            lanes = pl.ds(cb * L, L)
            c16 = 0.5 * c_ref[t, pl.ds(r0, 16), lanes].astype(jnp.float32)
            for h in range(2):
                rows = pl.ds(pl.multiple_of(r0 + 8 * h, 8), 8)
                here = (mask[t, cb, g * 2 + h] > 0) & alive
                p = jnp.minimum(p_ref[t, rows, lanes], jnp.where(here, 1.0, 0.0))
                hc = jnp.maximum(c16[8 * h : 8 * h + 8], jnp.where(here, -BIG, BIG))
                u = jnp.minimum(jnp.maximum(((p - hc) - a_buf[rows, :]) - s[cb], 0.0), 1.0)
                out[t, rows, lanes] = u - hc
                us[h].append(u)
                ps[h].append(p)
                ucols[cb] = ucols[cb] + u
                pcols[cb] = pcols[cb] + p
        for h in range(2):
            rows = pl.ds(pl.multiple_of(r0 + 8 * h, 8), 8)
            r_buf[rows, :] = tree(us[h])
            q_buf[rows, :] = tree(ps[h])
        return tuple(ucols), tuple(pcols)

    ucols, pcols = ZEROS(), ZEROS()
    for b in range(NRB):
        ready(t * NRB + b)
        ucols, pcols = lax.fori_loop(b * 8, (b + 1) * 8, step, (ucols, pcols))
    write_sums(t, usum, r_buf, ucols)
    write_sums(t, psum, q_buf, pcols)


def first_kernel(own_ids, mask, rec, mine, other, bias, p_hbm, c_hbm, out, usum, msg, ids, p_ref, c_ref, a_buf, r_buf, q_buf, psum, id_buf, p_sems, c_sems, sem):
    def fetch(n):
        t, b = divmod(n, NRB)
        rows = pl.ds(b * RB, RB)
        return (
            pltpu.make_async_copy(p_hbm.at[t, rows, :], p_ref.at[t, rows, :], p_sems.at[n]),
            pltpu.make_async_copy(c_hbm.at[t, rows, :], c_ref.at[t, rows, :], c_sems.at[n]),
        )

    def start(n):
        for copy in fetch(n):
            copy.start()

    def ready(n):
        if n + AHEAD < 2 * NRB:
            start(n + AHEAD)
        for copy in fetch(n):
            copy.wait()

    for n in range(AHEAD):
        start(n)
    core = lax.axis_index("tiles") & 1
    id_buf[0:4, :] = mine[TS : TS + 4, :].astype(jnp.int32)
    id_buf[4:8, :] = other[TS : TS + 4, :].astype(jnp.int32)
    keep_ids = pltpu.make_async_copy(id_buf, ids, sem)
    keep_ids.start()
    for t in range(2):
        a, s = own_ids[t], own_ids[2 + t]
        arow = jnp.where((a & 1) == core, rows_of(rec, a, False), other[AR * t : AR * (t + 1), :])
        srow = jnp.where((s & 1) == core, rows_of(rec, s, True), other[8 + SR * t : 8 + SR * (t + 1), :])
        first_tile(t, a >= 0, mask, arow, srow, p_ref, c_ref, out, usum, psum, a_buf, r_buf, q_buf, ready)
    data = jnp.concatenate([2.0 * usum[...] - psum[...], bias[...]], axis=0)
    for j in range(CHIPS):
        msg[j * MSG : (j + 1) * MSG, :] = data
    keep_ids.wait()


def users_kernel(ids, rec, mine, other, acc_a0, acc_a1, acc_s0, acc_s1):
    me = lax.axis_index("tiles")
    chip = me >> 1
    core = me & 1

    def at(i):
        return pl.multiple_of(jnp.where(i < 0, BLOCKS, i) * 8, 8)

    wanted = []
    for side, out, index in ((0, mine, me), (4, other, me ^ 1)):
        adv = [(ids[side + k, chip], AR * k) for k in range(2)] + [(index, TS + SR)]
        slot = [(ids[side + 2 + k, chip], 8 + SR * k) for k in range(2)] + [(index, TS)]
        wanted.append((out, adv, slot))
    zero = jnp.zeros((8, L), jnp.float32)
    for _, adv, slot in wanted:
        for i, _ in adv:
            acc_a0[pl.ds(at(i), 8), :] = zero
            acc_a1[pl.ds(at(i), 8), :] = zero
        for i, _ in slot:
            acc_s0[pl.ds(at(i), 8), :] = zero
            acc_s1[pl.ds(at(i), 8), :] = zero
    for j in range(CHIPS):
        for k, acc in ((0, acc_a0), (1, acc_a1)):
            rows = pl.ds(at(ids[k, j]), AR)
            acc[rows, :] = acc[rows, :] + rec[j * MSG + AR * k : j * MSG + AR * (k + 1), :]
        for k, acc in ((0, acc_s0), (1, acc_s1)):
            rows = pl.ds(at(ids[2 + k, j]), SR)
            acc[rows, :] = acc[rows, :] + rec[j * MSG + 8 + SR * k : j * MSG + 8 + SR * (k + 1), :]
    for out, adv, slot in wanted:
        for i, o in adv:
            b = jnp.maximum(i, 0)
            bias = rec[pl.ds((b >> 1) * MSG + TS + SR, AR), :] * jnp.where((b & 1) == core, 1.0, 0.0)
            rows = pl.ds(at(i), AR)
            out[o : o + AR, :] = (acc_a0[rows, :] + acc_a1[rows, :]) + bias
        for i, o in slot:
            b = jnp.maximum(i, 0)
            bias = rec[pl.ds((b >> 1) * MSG + TS, SR), :] * jnp.where((b & 1) == core, 1.0, 0.0)
            rows = pl.ds(at(i), SR)
            out[o : o + SR, :] = (acc_s0[rows, :] + acc_s1[rows, :]) + bias


def second_tile(t, arow, srow, base, out, usum, a_buf, r_buf, done):
    spread_half(arow, a_buf)
    s = slot_rows(srow)

    def step(g, cols):
        rows = pl.ds(pl.multiple_of(g * 8, 8), 8)
        a = a_buf[rows, :]
        cols = list(cols)
        us = []
        for cb in range(SR):
            lanes = pl.ds(cb * L, L)
            u = jnp.minimum(jnp.maximum((base[t, rows, lanes] - a) - s[cb], 0.0), 1.0)
            out[t, rows, lanes] = u
            cols[cb] = cols[cb] + u
            us.append(u)
        r_buf[rows, :] = tree(us)
        return tuple(cols)

    cols = ZEROS()
    for b in range(NRB):
        cols = lax.fori_loop(b * 16, (b + 1) * 16, step, cols, unroll=4)
        done(t, b)
    write_sums(t, usum, r_buf, cols)


def second_kernel(mine, other, base, psum, primal, sums, own, out, usum, a_buf, r_buf, sems):
    def keep(t, b):
        rows = pl.ds(b * RB, RB)
        return pltpu.make_async_copy(out.at[t, rows, :], primal.at[t, rows, :], sems.at[t * NRB + b])

    total = mine[...] + other[...]
    adv = jnp.maximum(total[0:8] * (1.0 / 1024), 0.0)
    slot = jnp.maximum(total[8:32] * (1.0 / 512), 0.0)
    own[0:SR, :] = slot[16:24]
    own[SR:OUT, :] = jnp.maximum(total[32:36] * (1.0 / 1024), 0.0)
    for t in range(2):
        second_tile(
            t, adv[4 * t : 4 * t + 4], slot[8 * t : 8 * t + 8], base, out, usum, a_buf, r_buf, lambda t, b: keep(t, b).start()
        )
    sums[...] = 2.0 * usum[...] - psum[...]
    for t in range(2):
        for b in range(NRB):
            keep(t, b).wait()


def owners_kernel(ids, mine, other, out):
    me = lax.axis_index("tiles")
    chip = me >> 1
    core = me & 1
    out[...] = jnp.zeros_like(out)
    for side, rec in ((0, mine), (4, other)):
        for k in range(2):
            for i, o, n, src in (
                (ids[side + k, chip], SR, AR, AR * k),
                (ids[side + 2 + k, chip], 0, SR, 8 + SR * k),
            ):

                @pl.when((i >= 0) & ((i & 1) == core))
                def _():
                    rows = pl.ds((i >> 1) * OUT + o, n)
                    out[rows, :] = out[rows, :] + rec[src : src + n, :]


def last_kernel(rec, own, bounds, adv_out, slot_out):
    n = 2 * OUT
    parts = [rec[g * n : (g + 1) * n, :] for g in range(CHIPS // 2)]
    total = tree(parts)
    total = total[0:OUT] + total[OUT:n]
    slot_out[...] = jnp.maximum(own[0:SR, :] + (total[0:SR] - bounds[0:SR, :]) * (1.0 / 512), 0.0)
    adv_out[...] = jnp.maximum(own[SR:OUT, :] + (total[SR:OUT] - bounds[SR:OUT, :]) * (1.0 / 1024), 0.0)


def f32(*shape):
    return jax.ShapeDtypeStruct(shape, jnp.float32)


def vmem(*shape):
    return pltpu.VMEM(shape, jnp.float32)


def in_vmem(x):
    return pltpu.with_memory_space_constraint(x, pltpu.VMEM)


def in_smem(x):
    return pltpu.with_memory_space_constraint(x, pltpu.SMEM)


def call(kernel, name, ins, outs, scratch=(), mib=4):
    return pl.pallas_call(
        kernel,
        in_specs=[s for _, s in ins],
        out_specs=[s for _, s in outs],
        out_shape=[o for o, _ in outs],
        scratch_shapes=list(scratch),
        compiler_params=pltpu.CompilerParams(vmem_limit_bytes=mib << 20),
        name=name,
    )(*[x for x, _ in ins])


def in_hbm(x):
    return pltpu.with_memory_space_constraint(x, pltpu.HBM)


def hbm_arg(x):
    return (in_hbm(x), pl.BlockSpec(memory_space=pl.ANY))


def smem_out(*shape):
    return (pltpu.SMEM(shape, jnp.int32), IN_SMEM)


def smem_arg(x):
    return (in_smem(x), IN_SMEM)


def vmem_arg(x):
    return (in_vmem(x), IN_VMEM)


def vmem_out(*shape):
    return (vmem(*shape), IN_VMEM)


def exchange(x, rows):
    x = x.reshape(CHIPS, rows * L)
    x = lax.all_to_all(x, "tiles", 0, 0, axis_index_groups=CORE_GROUPS, tiled=True)
    return vmem_arg(x.reshape(CHIPS * rows, L))


def swap(x):
    return lax.ppermute(x, "tiles", PARTNERS)


def body(primal_start, cost, mask, tile_adv, tile_slot, adv_dual, slot_dual, spend_limit, capacity):
    tile = (2, 512, 1024)
    message, bias, bounds, row_ids, own_ids, here = call(
        own_kernel,
        "own",
        [(in_hbm(tile_adv), IN_SMEM), (in_hbm(tile_slot), IN_SMEM)]
        + [(in_hbm(x.reshape(-1, L)), IN_VMEM) for x in (adv_dual, slot_dual, spend_limit, capacity)]
        + [hbm_arg(mask.transpose(0, 2, 1))],
        [vmem_out(CHIPS * OWN, L), vmem_out(OUT, L), vmem_out(OUT, L)]
        + [(pltpu.VMEM((8, L), jnp.int32), IN_VMEM), smem_out(4), smem_out(2, 8, 64)],
        [pltpu.SemaphoreType.DMA(())],
    )
    table = exchange(message, OWN)
    (picked,) = call(pick_kernel, "pick", [vmem_arg(swap(row_ids)), table], [vmem_out(SEL, L)])

    base, usum, message, ids = call(
        first_kernel,
        "first",
        [smem_arg(own_ids), smem_arg(here), table, vmem_arg(picked), vmem_arg(swap(picked)), vmem_arg(bias)] + [hbm_arg(primal_start), hbm_arg(cost)],
        [vmem_out(*tile), vmem_out(TS, L), vmem_out(CHIPS * MSG, L), smem_out(8, L)],
        [vmem(*tile), pltpu.VMEM(tile, jnp.bfloat16)]
        + [vmem(512, L)] * 3
        + [vmem(TS, L), pltpu.VMEM((8, L), jnp.int32)]
        + [pltpu.SemaphoreType.DMA((2 * NRB,))] * 2
        + [pltpu.SemaphoreType.DMA(())],
        8,
    )
    part = exchange(message, MSG)
    mine, other = call(
        users_kernel,
        "users",
        [smem_arg(ids), part],
        [vmem_out(MSG, L), vmem_out(MSG, L)],
        [vmem((BLOCKS + 1) * 8, L)] * 4,
    )

    primal, sums, own = call(
        second_kernel,
        "second",
        [vmem_arg(mine), vmem_arg(swap(other)), vmem_arg(base), vmem_arg(usum)],
        [(f32(*tile), pl.BlockSpec(memory_space=pl.ANY)), vmem_out(TS, L), vmem_out(OUT, L)],
        [vmem(*tile), vmem(TS, L), vmem(512, L), vmem(512, L), pltpu.SemaphoreType.DMA((2 * NRB,))],
        8,
    )
    (message,) = call(
        owners_kernel, "owners", [smem_arg(ids), vmem_arg(sums), vmem_arg(swap(sums))], [vmem_out(CHIPS * OUT, L)]
    )
    adv_out, slot_out = call(
        last_kernel,
        "last",
        [exchange(message, OUT), vmem_arg(own), vmem_arg(bounds)],
        [(f32(AR, L), IN_VMEM), (f32(SR, L), IN_VMEM)],
    )
    return primal, adv_out.reshape(1, 512), slot_out.reshape(1, 1024)


def solution(mesh):
    return jax.shard_map(
        body,
        mesh=mesh,
        in_specs=(
            P("tiles", None, None),
            P("tiles", None, None),
            P("tiles", None, None),
            P("tiles"),
            P("tiles"),
            P("tiles", None),
            P("tiles", None),
            P("tiles", None),
            P("tiles", None),
        ),
        out_specs=(P("tiles", None, None), P("tiles", None), P("tiles", None)),
        check_vma=False,
    )
```

```python
import jax
import jax.numpy as jnp
from jax import lax
from jax.experimental import pallas as pl
from jax.experimental.pallas import tpu as pltpu
from jax.sharding import PartitionSpec as P

CHIPS = 64
BLOCKS = 128
L = 128
AR = 4
SR = 8
OWN = AR + SR + 1
SEL = 2 * (AR + SR) + 8
TS = 2 * (AR + SR)
MSG = TS + SR + AR
OUT = SR + AR
RB = 128
NRB = 4
BIG = 1e30
AHEAD = 3

PLANE = 16
CORE_GROUPS = [[j * 2 + c for j in range(CHIPS)] for c in range(2)]
PLANE_GROUPS = [[(x * PLANE + j) * 2 + c for j in range(PLANE)] for x in range(4) for c in range(2)]
PARTNERS = [(i, i ^ 1) for i in range(2 * CHIPS)]


def along_x(d):
    return [(i, (i + d * 2 * PLANE) % (2 * CHIPS)) for i in range(2 * CHIPS)]


IN_VMEM = pl.BlockSpec(memory_space=pltpu.VMEM)
IN_SMEM = pl.BlockSpec(memory_space=pltpu.SMEM)


def own_kernel(adv_id, slot_id, adv, slot, limit, cap, mask_hbm, out, bias, bounds, row_ids, ids, mask, sem):
    keep_mask = pltpu.make_async_copy(mask_hbm, mask, sem)
    keep_mask.start()
    lane = lax.broadcasted_iota(jnp.int32, (8, L), 1)
    row = jnp.zeros((8, L), jnp.int32)
    for k, v in enumerate((adv_id[0], adv_id[1], slot_id[0], slot_id[1])):
        row = jnp.where(lane == k, v, row)
        ids[k] = v
    row_ids[...] = row
    data = jnp.concatenate([slot[...], adv[...], row[0:1].astype(jnp.float32)], axis=0)
    for j in range(CHIPS):
        out[j * OWN : (j + 1) * OWN, :] = data
    bias[0:SR, :] = slot[...] * 512.0 - cap[...]
    bias[SR:OUT, :] = adv[...] * 1024.0 - limit[...]
    bounds[0:SR, :] = cap[...]
    bounds[SR:OUT, :] = limit[...]
    keep_mask.wait()


def rows_of(rec, i, slot):
    at = (jnp.maximum(i, 0) >> 1) * OWN
    return rec[pl.ds(at, SR), :] if slot else rec[pl.ds(at + SR, AR), :]


def pick_kernel(partner_ids, rec, _, out):

    lane = lax.broadcasted_iota(jnp.int32, (1, L), 1)
    row = partner_ids[0:1, :]
    wanted = [jnp.max(jnp.where(lane == k, row, -1)) for k in range(4)]
    for k in range(2):
        out[AR * k : AR * (k + 1), :] = rows_of(rec, wanted[k], False)
        out[8 + SR * k : 8 + SR * (k + 1), :] = rows_of(rec, wanted[2 + k], True)
    ids = rec[pl.ds(OWN - 1, CHIPS, stride=OWN), :]
    out[TS:SEL, :] = jnp.concatenate([ids, ids], axis=0).T[0:8, :]


def spread_half(row, buf):
    for b in range(NRB):
        block = jnp.broadcast_to(0.5 * row[b : b + 1, :], (L, L))
        buf[b * L : (b + 1) * L, :] = block.T


def tree(xs):
    while len(xs) > 1:
        xs = [xs[i] + xs[i + 1] for i in range(0, len(xs), 2)]
    return xs[0]


def write_sums(t, sums, r_buf, cols):
    for b in range(NRB):
        sums[t * AR + b : t * AR + b + 1, :] = jnp.sum(r_buf[b * L : (b + 1) * L, :].T, axis=0, keepdims=True)
    rows = [jnp.sum(c, axis=0, keepdims=True) for c in cols]
    sums[8 + t * SR : 8 + (t + 1) * SR, :] = jnp.concatenate(rows, axis=0)


def slot_rows(srow):
    return [jnp.broadcast_to(0.5 * srow[cb : cb + 1, :], (8, L)) for cb in range(SR)]


ZEROS = lambda: (jnp.zeros((8, L), jnp.float32),) * SR


def prepare_kernel(own_ids, mask, p_ref, c_ref, hc, psum, r_buf, col_buf):
    t = pl.program_id(0)
    rb = pl.program_id(1)

    @pl.when(rb == 0)
    def _():
        col_buf[...] = jnp.zeros_like(col_buf)

    alive = own_ids[t] >= 0

    def step(g, cols):
        r0 = pl.multiple_of(g * 16, 16)
        cols = list(cols)
        ps = [[], []]
        for cb in range(SR):
            lanes = pl.ds(cb * L, L)
            c16 = 0.5 * c_ref[0, pl.ds(r0, 16), lanes].astype(jnp.float32)
            halves = []
            for h in range(2):
                here = (mask[t, cb, rb * 16 + g * 2 + h] > 0) & alive
                rows = pl.ds(pl.multiple_of(r0 + 8 * h, 8), 8)
                p = jnp.minimum(p_ref[0, rows, lanes], jnp.where(here, 1.0, 0.0))
                halves.append(jnp.maximum(c16[8 * h : 8 * h + 8], jnp.where(here, -BIG, BIG)))
                ps[h].append(p)
                cols[cb] = cols[cb] + p
            hc[t, pl.ds(pl.multiple_of(rb * RB + r0, 16), 16), lanes] = jnp.concatenate(halves, axis=0).astype(jnp.bfloat16)
        for h in range(2):
            r_buf[pl.ds(pl.multiple_of(r0 + 8 * h, 8), 8), :] = tree(ps[h])
        return tuple(cols)

    cols = tuple(col_buf[pl.ds(cb * 8, 8), :] for cb in range(SR))
    cols = lax.fori_loop(0, RB // 16, step, cols)
    for cb in range(SR):
        col_buf[pl.ds(cb * 8, 8), :] = cols[cb]
    psum[pl.ds(t * AR + rb, 1), :] = jnp.sum(r_buf[...].T, axis=0, keepdims=True)

    @pl.when(rb == NRB - 1)
    def _():
        rows = [jnp.sum(cols[cb], axis=0, keepdims=True) for cb in range(SR)]
        psum[pl.ds(pl.multiple_of(8 + t * SR, 8), SR), :] = jnp.concatenate(rows, axis=0)


def first_tile(t, arow, srow, p_ref, hc_ref, out, usum, a_buf, r_buf, ready):
    spread_half(arow, a_buf)
    s = slot_rows(srow)

    def step(g, cols):
        cols = list(cols)
        us = [[], []]
        r0 = pl.multiple_of(g * 16, 16)
        a = [a_buf[pl.ds(pl.multiple_of(r0 + 8 * h, 8), 8), :] for h in range(2)]
        for cb in range(SR):
            lanes = pl.ds(cb * L, L)
            c16 = hc_ref[t, pl.ds(r0, 16), lanes].astype(jnp.float32)
            for h in range(2):
                rows = pl.ds(pl.multiple_of(r0 + 8 * h, 8), 8)
                hc = c16[8 * h : 8 * h + 8]
                u = jnp.minimum(jnp.maximum(((p_ref[t, rows, lanes] - hc) - a[h]) - s[cb], 0.0), 1.0)
                out[t, rows, lanes] = u - hc
                us[h].append(u)
                cols[cb] = cols[cb] + u
        for h in range(2):
            r_buf[pl.ds(pl.multiple_of(r0 + 8 * h, 8), 8), :] = tree(us[h])
        return tuple(cols)

    cols = ZEROS()
    for b in range(NRB):
        ready(t * NRB + b)
        cols = lax.fori_loop(b * 8, (b + 1) * 8, step, cols, unroll=2)
    write_sums(t, usum, r_buf, cols)


def first_kernel(own_ids, rec, mine, other, bias, psum, hc_ref, p_hbm, out, usum, msg, ids, p_ref, a_buf, r_buf, id_buf, p_sems, sem):
    def fetch(n):
        t, b = divmod(n, NRB)
        rows = pl.ds(b * RB, RB)
        return pltpu.make_async_copy(p_hbm.at[t, rows, :], p_ref.at[t, rows, :], p_sems.at[n])

    def ready(n):
        if n + AHEAD < 2 * NRB:
            fetch(n + AHEAD).start()
        fetch(n).wait()

    for n in range(AHEAD):
        fetch(n).start()
    core = lax.axis_index("tiles") & 1
    id_buf[0:4, :] = mine[TS : TS + 4, :].astype(jnp.int32)
    id_buf[4:8, :] = other[TS : TS + 4, :].astype(jnp.int32)
    keep_ids = pltpu.make_async_copy(id_buf, ids, sem)
    keep_ids.start()
    for t in range(2):
        a, s = own_ids[t], own_ids[2 + t]
        arow = jnp.where((a & 1) == core, rows_of(rec, a, False), other[AR * t : AR * (t + 1), :])
        srow = jnp.where((s & 1) == core, rows_of(rec, s, True), other[8 + SR * t : 8 + SR * (t + 1), :])
        first_tile(t, arow, srow, p_ref, hc_ref, out, usum, a_buf, r_buf, ready)
    data = jnp.concatenate([2.0 * usum[...] - psum[...], bias[...]], axis=0)
    for j in range(PLANE):
        msg[j * MSG : (j + 1) * MSG, :] = data
    keep_ids.wait()


def users_kernel(ids, rec, out0, out1, out2, out3, acc_a0, acc_a1, acc_s0, acc_s1):
    me = lax.axis_index("tiles")
    chip = me >> 1
    core = me & 1
    x = chip >> 4

    def at(i):
        return pl.multiple_of(jnp.where(i < 0, BLOCKS, i) * 8, 8)

    wanted = []
    for d, out in enumerate((out0, out1, out2, out3)):
        there = (((x + d) & 3) << 4) | (chip & 15)
        for side in range(2):
            o = side * MSG
            index = there * 2 + (core ^ side)
            adv = [(ids[4 * side + k, there], o + AR * k) for k in range(2)] + [(index, o + TS + SR)]
            slot = [(ids[4 * side + 2 + k, there], o + 8 + SR * k) for k in range(2)] + [(index, o + TS)]
            wanted.append((out, adv, slot))
    zero = jnp.zeros((8, L), jnp.float32)
    for _, adv, slot in wanted:
        for i, _ in adv:
            acc_a0[pl.ds(at(i), 8), :] = zero
            acc_a1[pl.ds(at(i), 8), :] = zero
        for i, _ in slot:
            acc_s0[pl.ds(at(i), 8), :] = zero
            acc_s1[pl.ds(at(i), 8), :] = zero
    for j in range(PLANE):
        source = (x << 4) | j
        for k, acc in ((0, acc_a0), (1, acc_a1)):
            rows = pl.ds(at(ids[k, source]), AR)
            acc[rows, :] = acc[rows, :] + rec[j * MSG + AR * k : j * MSG + AR * (k + 1), :]
        for k, acc in ((0, acc_s0), (1, acc_s1)):
            rows = pl.ds(at(ids[2 + k, source]), SR)
            acc[rows, :] = acc[rows, :] + rec[j * MSG + 8 + SR * k : j * MSG + 8 + SR * (k + 1), :]

    def bias(i, o, n):
        b = jnp.maximum(i, 0)
        here = ((b & 1) == core) & ((b >> 5) == x)
        return rec[pl.ds(((b >> 1) & 15) * MSG + o, n), :] * jnp.where(here, 1.0, 0.0)

    for out, adv, slot in wanted:
        for i, o in adv:
            rows = pl.ds(at(i), AR)
            out[o : o + AR, :] = (acc_a0[rows, :] + acc_a1[rows, :]) + bias(i, TS + SR, AR)
        for i, o in slot:
            rows = pl.ds(at(i), SR)
            out[o : o + SR, :] = (acc_s0[rows, :] + acc_s1[rows, :]) + bias(i, TS, SR)


def join_kernel(a, b, c, d, mine, other):
    total = (a[...] + b[...]) + (c[...] + d[...])
    mine[...] = total[0:MSG]
    other[...] = total[MSG:]


def second_tile(t, arow, srow, base, out, usum, a_buf, r_buf, done):
    spread_half(arow, a_buf)
    s = slot_rows(srow)

    def step(g, cols):
        rows = pl.ds(pl.multiple_of(g * 8, 8), 8)
        a = a_buf[rows, :]
        cols = list(cols)
        us = []
        for cb in range(SR):
            lanes = pl.ds(cb * L, L)
            u = jnp.minimum(jnp.maximum((base[t, rows, lanes] - a) - s[cb], 0.0), 1.0)
            out[t, rows, lanes] = u
            cols[cb] = cols[cb] + u
            us.append(u)
        r_buf[rows, :] = tree(us)
        return tuple(cols)

    cols = ZEROS()
    for b in range(NRB):
        cols = lax.fori_loop(b * 16, (b + 1) * 16, step, cols, unroll=4)
        done(t, b)
    write_sums(t, usum, r_buf, cols)


def second_kernel(mine, other, base, psum, primal, sums, own, out, usum, a_buf, r_buf, sems):
    def keep(t, b):
        rows = pl.ds(b * RB, RB)
        return pltpu.make_async_copy(out.at[t, rows, :], primal.at[t, rows, :], sems.at[t * NRB + b])

    total = mine[...] + other[...]
    adv = jnp.maximum(total[0:8] * (1.0 / 1024), 0.0)
    slot = jnp.maximum(total[8:32] * (1.0 / 512), 0.0)
    own[0:SR, :] = slot[16:24]
    own[SR:OUT, :] = jnp.maximum(total[32:36] * (1.0 / 1024), 0.0)
    for t in range(2):
        second_tile(
            t, adv[4 * t : 4 * t + 4], slot[8 * t : 8 * t + 8], base, out, usum, a_buf, r_buf, lambda t, b: keep(t, b).start()
        )
    sums[...] = 2.0 * usum[...] - psum[...]
    for t in range(2):
        for b in range(NRB):
            keep(t, b).wait()


def owners_kernel(ids, mine, other, out):
    me = lax.axis_index("tiles")
    chip = me >> 1
    core = me & 1
    out[...] = jnp.zeros_like(out)
    for side, rec in ((0, mine), (4, other)):
        for k in range(2):
            for i, o, n, src in (
                (ids[side + k, chip], SR, AR, AR * k),
                (ids[side + 2 + k, chip], 0, SR, 8 + SR * k),
            ):

                @pl.when((i >= 0) & ((i & 1) == core))
                def _():
                    rows = pl.ds((i >> 1) * OUT + o, n)
                    out[rows, :] = out[rows, :] + rec[src : src + n, :]


def last_kernel(rec, own, bounds, adv_out, slot_out):
    n = 2 * OUT
    parts = [rec[g * n : (g + 1) * n, :] for g in range(CHIPS // 2)]
    total = tree(parts)
    total = total[0:OUT] + total[OUT:n]
    slot_out[...] = jnp.maximum(own[0:SR, :] + (total[0:SR] - bounds[0:SR, :]) * (1.0 / 512), 0.0)
    adv_out[...] = jnp.maximum(own[SR:OUT, :] + (total[SR:OUT] - bounds[SR:OUT, :]) * (1.0 / 1024), 0.0)


def f32(*shape):
    return jax.ShapeDtypeStruct(shape, jnp.float32)


def vmem(*shape):
    return pltpu.VMEM(shape, jnp.float32)


def in_vmem(x):
    return pltpu.with_memory_space_constraint(x, pltpu.VMEM)


def in_smem(x):
    return pltpu.with_memory_space_constraint(x, pltpu.SMEM)


def call(kernel, name, ins, outs, scratch=(), mib=4):
    return pl.pallas_call(
        kernel,
        in_specs=[s for _, s in ins],
        out_specs=[s for _, s in outs],
        out_shape=[o for o, _ in outs],
        scratch_shapes=list(scratch),
        compiler_params=pltpu.CompilerParams(vmem_limit_bytes=mib << 20),
        name=name,
    )(*[x for x, _ in ins])


def in_hbm(x):
    return pltpu.with_memory_space_constraint(x, pltpu.HBM)


def hbm_arg(x):
    return (in_hbm(x), pl.BlockSpec(memory_space=pl.ANY))


def smem_out(*shape):
    return (pltpu.SMEM(shape, jnp.int32), IN_SMEM)


def smem_arg(x):
    return (in_smem(x), IN_SMEM)


def vmem_arg(x):
    return (in_vmem(x), IN_VMEM)


def vmem_out(*shape):
    return (vmem(*shape), IN_VMEM)


def exchange(x, groups, rows):
    n = len(groups[0])
    x = lax.all_to_all(x.reshape(n, rows * L), "tiles", 0, 0, axis_index_groups=groups, tiled=True)
    return vmem_arg(x.reshape(n * rows, L))


def swap(x):
    return lax.ppermute(x, "tiles", PARTNERS)


def body(primal_start, cost, mask, tile_adv, tile_slot, adv_dual, slot_dual, spend_limit, capacity):
    tile = (2, 512, 1024)
    message, bias, bounds, row_ids, own_ids, here = call(
        own_kernel,
        "own",
        [(in_hbm(tile_adv), IN_SMEM), (in_hbm(tile_slot), IN_SMEM)]
        + [(in_hbm(x.reshape(-1, L)), IN_VMEM) for x in (adv_dual, slot_dual, spend_limit, capacity)]
        + [hbm_arg(mask.transpose(0, 2, 1))],
        [vmem_out(CHIPS * OWN, L), vmem_out(OUT, L), vmem_out(OUT, L)]
        + [(pltpu.VMEM((8, L), jnp.int32), IN_VMEM), smem_out(4), smem_out(2, 8, 64)],
        [pltpu.SemaphoreType.DMA(())],
    )
    table = exchange(message, CORE_GROUPS, OWN)
    block = pl.BlockSpec((1, RB, 1024), lambda t, rb: (t, rb, 0))
    hc, psum = pl.pallas_call(
        prepare_kernel,
        grid=(2, NRB),
        in_specs=[IN_SMEM, IN_SMEM, block, block],
        out_specs=[IN_VMEM, IN_VMEM],
        out_shape=[pltpu.VMEM(tile, jnp.bfloat16), vmem(TS, L)],
        scratch_shapes=[vmem(RB, L), vmem(64, L)],
        compiler_params=pltpu.CompilerParams(vmem_limit_bytes=4 << 20),
        name="prepare",
    )(in_smem(own_ids), in_smem(here), in_hbm(primal_start), in_hbm(cost))
    (picked,) = call(pick_kernel, "pick", [vmem_arg(swap(row_ids)), table, vmem_arg(psum)], [vmem_out(SEL, L)])
    base, usum, message, ids = call(
        first_kernel,
        "first",
        [smem_arg(own_ids), table, vmem_arg(picked), vmem_arg(swap(picked)), vmem_arg(bias), vmem_arg(psum), vmem_arg(hc)]
        + [hbm_arg(primal_start)],
        [vmem_out(*tile), vmem_out(TS, L), vmem_out(PLANE * MSG, L), smem_out(8, L)],
        [vmem(*tile), vmem(512, L), vmem(512, L), pltpu.VMEM((8, L), jnp.int32)]
        + [pltpu.SemaphoreType.DMA((2 * NRB,)), pltpu.SemaphoreType.DMA(())],
        8,
    )
    part = exchange(message, PLANE_GROUPS, MSG)
    parts = call(users_kernel, "users", [smem_arg(ids), part], [vmem_out(2 * MSG, L)] * 4, [vmem((BLOCKS + 1) * 8, L)] * 4)
    parts = [parts[0]] + [lax.ppermute(parts[d], "tiles", along_x(d)) for d in range(1, 4)]
    mine, other = call(join_kernel, "join", [vmem_arg(v) for v in parts], [vmem_out(MSG, L)] * 2)

    primal, sums, own = call(
        second_kernel,
        "second",
        [vmem_arg(mine), vmem_arg(swap(other)), vmem_arg(base), vmem_arg(usum)],
        [(f32(*tile), pl.BlockSpec(memory_space=pl.ANY)), vmem_out(TS, L), vmem_out(OUT, L)],
        [vmem(*tile), vmem(TS, L), vmem(512, L), vmem(512, L), pltpu.SemaphoreType.DMA((2 * NRB,))],
        8,
    )
    (message,) = call(
        owners_kernel, "owners", [smem_arg(ids), vmem_arg(sums), vmem_arg(swap(sums))], [vmem_out(CHIPS * OUT, L)]
    )
    adv_out, slot_out = call(
        last_kernel,
        "last",
        [exchange(message, CORE_GROUPS, OUT), vmem_arg(own), vmem_arg(bounds)],
        [(f32(AR, L), IN_VMEM), (f32(SR, L), IN_VMEM)],
    )
    return primal, adv_out.reshape(1, 512), slot_out.reshape(1, 1024)


def solution(mesh):
    return jax.shard_map(
        body,
        mesh=mesh,
        in_specs=(
            P("tiles", None, None),
            P("tiles", None, None),
            P("tiles", None, None),
            P("tiles"),
            P("tiles"),
            P("tiles", None),
            P("tiles", None),
            P("tiles", None),
            P("tiles", None),
        ),
        out_specs=(P("tiles", None, None), P("tiles", None), P("tiles", None)),
        check_vma=False,
    )
```

```python
import jax
import jax.numpy as jnp
from jax import lax
from jax.experimental import pallas as pl
from jax.experimental.pallas import tpu as pltpu
from jax.sharding import PartitionSpec as P

CHIPS = 64
BLOCKS = 128
L = 128
AR = 4
SR = 8
OWN = AR + SR + 1
SEL = 2 * (AR + SR) + 8
TS = 2 * (AR + SR)
MSG = TS + SR + AR
OUT = SR + AR
RB = 128
NRB = 4
BIG = 1e30

PLANE = 16
CORE_GROUPS = [[j * 2 + c for j in range(CHIPS)] for c in range(2)]
PLANE_GROUPS = [[(x * PLANE + j) * 2 + c for j in range(PLANE)] for x in range(4) for c in range(2)]
PARTNERS = [(i, i ^ 1) for i in range(2 * CHIPS)]


def along_x(d):
    return [(i, (i + d * 2 * PLANE) % (2 * CHIPS)) for i in range(2 * CHIPS)]


IN_VMEM = pl.BlockSpec(memory_space=pltpu.VMEM)
IN_SMEM = pl.BlockSpec(memory_space=pltpu.SMEM)


def own_kernel(adv_id, slot_id, adv, slot, limit, cap, mask_hbm, out, bias, bounds, row_ids, ids, mask, sem):
    keep_mask = pltpu.make_async_copy(mask_hbm, mask, sem)
    keep_mask.start()
    lane = lax.broadcasted_iota(jnp.int32, (8, L), 1)
    row = jnp.zeros((8, L), jnp.int32)
    for k, v in enumerate((adv_id[0], adv_id[1], slot_id[0], slot_id[1])):
        row = jnp.where(lane == k, v, row)
        ids[k] = v
    row_ids[...] = row
    data = jnp.concatenate([slot[...], adv[...], row[0:1].astype(jnp.float32)], axis=0)
    for j in range(CHIPS):
        out[j * OWN : (j + 1) * OWN, :] = data
    bias[0:SR, :] = slot[...] * 512.0 - cap[...]
    bias[SR:OUT, :] = adv[...] * 1024.0 - limit[...]
    bounds[0:SR, :] = cap[...]
    bounds[SR:OUT, :] = limit[...]
    keep_mask.wait()


def rows_of(rec, i, slot):
    at = (jnp.maximum(i, 0) >> 1) * OWN
    return rec[pl.ds(at, SR), :] if slot else rec[pl.ds(at + SR, AR), :]


def pick_kernel(partner_ids, rec, _, out):

    lane = lax.broadcasted_iota(jnp.int32, (1, L), 1)
    row = partner_ids[0:1, :]
    wanted = [jnp.max(jnp.where(lane == k, row, -1)) for k in range(4)]
    for k in range(2):
        out[AR * k : AR * (k + 1), :] = rows_of(rec, wanted[k], False)
        out[8 + SR * k : 8 + SR * (k + 1), :] = rows_of(rec, wanted[2 + k], True)
    ids = rec[pl.ds(OWN - 1, CHIPS, stride=OWN), :]
    out[TS:SEL, :] = jnp.concatenate([ids, ids], axis=0).T[0:8, :]


def spread_half(row, buf):
    for b in range(NRB):
        block = jnp.broadcast_to(0.5 * row[b : b + 1, :], (L, L))
        buf[b * L : (b + 1) * L, :] = block.T


def tree(xs):
    while len(xs) > 1:
        xs = [xs[i] + xs[i + 1] for i in range(0, len(xs), 2)]
    return xs[0]


def write_sums(t, sums, r_buf, cols):
    for b in range(NRB):
        sums[t * AR + b : t * AR + b + 1, :] = jnp.sum(r_buf[b * L : (b + 1) * L, :].T, axis=0, keepdims=True)
    rows = [jnp.sum(c, axis=0, keepdims=True) for c in cols]
    sums[8 + t * SR : 8 + (t + 1) * SR, :] = jnp.concatenate(rows, axis=0)


def slot_rows(srow):
    return [jnp.broadcast_to(0.5 * srow[cb : cb + 1, :], (8, L)) for cb in range(SR)]


ZEROS = lambda: (jnp.zeros((8, L), jnp.float32),) * SR


def prepare_kernel(own_ids, mask, p_ref, c_ref, hc, psum, r_buf, col_buf):
    t = pl.program_id(0)
    rb = pl.program_id(1)

    @pl.when(rb == 0)
    def _():
        col_buf[...] = jnp.zeros_like(col_buf)

    alive = jnp.where(own_ids[t] >= 0, 1, 0)

    def step(g, cols):
        r0 = pl.multiple_of(g * 16, 16)
        cols = list(cols)
        ps = [[], []]
        for cb in range(SR):
            lanes = pl.ds(cb * L, L)
            c16 = 0.5 * c_ref[0, pl.ds(r0, 16), lanes].astype(jnp.float32)
            halves = []
            for h in range(2):
                here = jnp.full((8, L), mask[t, cb, rb * 16 + g * 2 + h] * alive, jnp.int32) > 0
                rows = pl.ds(pl.multiple_of(r0 + 8 * h, 8), 8)
                p = jnp.where(here, p_ref[0, rows, lanes], 0.0)
                halves.append(jnp.where(here, c16[8 * h : 8 * h + 8], BIG))
                ps[h].append(p)
                cols[cb] = cols[cb] + p
            hc[t, pl.ds(pl.multiple_of(rb * RB + r0, 16), 16), lanes] = jnp.concatenate(halves, axis=0).astype(jnp.bfloat16)
        for h in range(2):
            r_buf[pl.ds(pl.multiple_of(r0 + 8 * h, 8), 8), :] = tree(ps[h])
        return tuple(cols)

    cols = tuple(col_buf[pl.ds(cb * 8, 8), :] for cb in range(SR))
    cols = lax.fori_loop(0, RB // 16, step, cols)
    for cb in range(SR):
        col_buf[pl.ds(cb * 8, 8), :] = cols[cb]
    psum[pl.ds(t * AR + rb, 1), :] = jnp.sum(r_buf[...].T, axis=0, keepdims=True)

    @pl.when(rb == NRB - 1)
    def _():
        rows = [jnp.sum(cols[cb], axis=0, keepdims=True) for cb in range(SR)]
        psum[pl.ds(pl.multiple_of(8 + t * SR, 8), SR), :] = jnp.concatenate(rows, axis=0)


def load_kernel(p_hbm, _, out, sem):
    copy = pltpu.make_async_copy(p_hbm.at[0], out, sem)
    copy.start()
    copy.wait()


def first_tile(t, arow, srow, p_ref, hc_ref, out, usum, a_buf, r_buf, ready):
    spread_half(arow, a_buf)
    s = slot_rows(srow)

    def step(g, cols):
        cols = list(cols)
        us = [[], []]
        r0 = pl.multiple_of(g * 16, 16)
        a = [a_buf[pl.ds(pl.multiple_of(r0 + 8 * h, 8), 8), :] for h in range(2)]
        for cb in range(SR):
            lanes = pl.ds(cb * L, L)
            c16 = hc_ref[t, pl.ds(r0, 16), lanes].astype(jnp.float32)
            for h in range(2):
                rows = pl.ds(pl.multiple_of(r0 + 8 * h, 8), 8)
                hc = c16[8 * h : 8 * h + 8]
                u = jnp.minimum(jnp.maximum(((p_ref[rows, lanes] - hc) - a[h]) - s[cb], 0.0), 1.0)
                out[t, rows, lanes] = u - hc
                us[h].append(u)
                cols[cb] = cols[cb] + u
        for h in range(2):
            r_buf[pl.ds(pl.multiple_of(r0 + 8 * h, 8), 8), :] = tree(us[h])
        return tuple(cols)

    cols = ZEROS()
    for b in range(NRB):
        ready(b)
        cols = lax.fori_loop(b * 8, (b + 1) * 8, step, cols, unroll=2)
    write_sums(t, usum, r_buf, cols)


def first_kernel(own_ids, rec, mine, other, bias, psum, hc_ref, p0_ref, p_hbm, out, usum, msg, ids, p1_ref, a_buf, r_buf, id_buf, p_sems, sem):
    def fetch(b):
        rows = pl.ds(b * RB, RB)
        return pltpu.make_async_copy(p_hbm.at[1, rows, :], p1_ref.at[rows, :], p_sems.at[b])

    for b in range(NRB):
        fetch(b).start()
    core = lax.axis_index("tiles") & 1
    id_buf[0:4, :] = mine[TS : TS + 4, :].astype(jnp.int32)
    id_buf[4:8, :] = other[TS : TS + 4, :].astype(jnp.int32)
    keep_ids = pltpu.make_async_copy(id_buf, ids, sem)
    keep_ids.start()
    for t in range(2):
        a, s = own_ids[t], own_ids[2 + t]
        arow = jnp.where((a & 1) == core, rows_of(rec, a, False), other[AR * t : AR * (t + 1), :])
        srow = jnp.where((s & 1) == core, rows_of(rec, s, True), other[8 + SR * t : 8 + SR * (t + 1), :])
        first_tile(
            t,
            arow,
            srow,
            (p0_ref, p1_ref)[t],
            hc_ref,
            out,
            usum,
            a_buf,
            r_buf,
            (lambda b: None, lambda b: fetch(b).wait())[t],
        )
    msg[0:TS, :] = 2.0 * usum[...] - psum[...]
    msg[TS:MSG, :] = bias[...]
    keep_ids.wait()


def pair_kernel(a, b, out):
    out[0:MSG, :] = a[...]
    out[MSG:, :] = b[...]


def users_kernel(ids, rec0, rec1, rec2, rec3, out, rec, acc_a0, acc_a1, acc_s0, acc_s1):
    me = lax.axis_index("tiles")
    chip = me >> 1
    core = me & 1
    x = chip >> 4
    line = chip & 15
    both = 2 * MSG

    def at(i):
        return pl.multiple_of(jnp.where(i < 0, BLOCKS, i) * 8, 8)

    wanted = []
    for j in range(PLANE):
        there = (x << 4) | j
        o = j * MSG
        index = there * 2 + core
        adv = [(ids[k, there], o + AR * k) for k in range(2)] + [(index, o + TS + SR)]
        slot = [(ids[2 + k, there], o + 8 + SR * k) for k in range(2)] + [(index, o + TS)]
        wanted.append((adv, slot))
    zero = jnp.zeros((8, L), jnp.float32)
    for adv, slot in wanted:
        for i, _ in adv:
            acc_a0[pl.ds(at(i), 8), :] = zero
            acc_a1[pl.ds(at(i), 8), :] = zero
        for i, _ in slot:
            acc_s0[pl.ds(at(i), 8), :] = zero
            acc_s1[pl.ds(at(i), 8), :] = zero
    for d, part in enumerate((rec0, rec1, rec2, rec3)):
        rec[d * both : (d + 1) * both, :] = part[...]
        source = (((x - d) & 3) << 4) | line
        for side in range(2):
            o = side * MSG
            for k, acc in ((0, acc_a0), (1, acc_a1)):
                rows = pl.ds(at(ids[4 * side + k, source]), AR)
                acc[rows, :] = acc[rows, :] + part[o + AR * k : o + AR * (k + 1), :]
            for k, acc in ((0, acc_s0), (1, acc_s1)):
                rows = pl.ds(at(ids[4 * side + 2 + k, source]), SR)
                acc[rows, :] = acc[rows, :] + part[o + 8 + SR * k : o + 8 + SR * (k + 1), :]

    def bias(i, o, n):
        b = jnp.maximum(i, 0)
        here = ((b >> 1) & 15) == line
        row = ((x - (b >> 5)) & 3) * both + ((b & 1) ^ core) * MSG + o
        return rec[pl.ds(row, n), :] * jnp.where(here, 1.0, 0.0)

    for adv, slot in wanted:
        for i, o in adv:
            rows = pl.ds(at(i), AR)
            out[o : o + AR, :] = (acc_a0[rows, :] + acc_a1[rows, :]) + bias(i, TS + SR, AR)
        for i, o in slot:
            rows = pl.ds(at(i), SR)
            out[o : o + SR, :] = (acc_s0[rows, :] + acc_s1[rows, :]) + bias(i, TS, SR)


def second_tile(t, arow, srow, base, out, usum, a_buf, r_buf, done):
    spread_half(arow, a_buf)
    s = slot_rows(srow)

    def step(g, cols):
        rows = pl.ds(pl.multiple_of(g * 8, 8), 8)
        a = a_buf[rows, :]
        cols = list(cols)
        us = []
        for cb in range(SR):
            lanes = pl.ds(cb * L, L)
            u = jnp.minimum(jnp.maximum((base[t, rows, lanes] - a) - s[cb], 0.0), 1.0)
            out[t, rows, lanes] = u
            cols[cb] = cols[cb] + u
            us.append(u)
        r_buf[rows, :] = tree(us)
        return tuple(cols)

    cols = ZEROS()
    for b in range(NRB):
        cols = lax.fori_loop(b * 16, (b + 1) * 16, step, cols, unroll=4)
        done(t, b)
    write_sums(t, usum, r_buf, cols)


def second_kernel(rec, base, psum, primal, sums, own, out, usum, a_buf, r_buf, sems):
    def keep(t, b):
        rows = pl.ds(b * RB, RB)
        return pltpu.make_async_copy(out.at[t, rows, :], primal.at[t, rows, :], sems.at[t * NRB + b])

    total = tree([rec[j * MSG : (j + 1) * MSG, :] for j in range(PLANE)])
    adv = jnp.maximum(total[0:8] * (1.0 / 1024), 0.0)
    slot = jnp.maximum(total[8:32] * (1.0 / 512), 0.0)
    own[0:SR, :] = slot[16:24]
    own[SR:OUT, :] = jnp.maximum(total[32:36] * (1.0 / 1024), 0.0)
    for t in range(2):
        second_tile(
            t, adv[4 * t : 4 * t + 4], slot[8 * t : 8 * t + 8], base, out, usum, a_buf, r_buf, lambda t, b: keep(t, b).start()
        )
    sums[...] = 2.0 * usum[...] - psum[...]
    for t in range(2):
        for b in range(NRB):
            keep(t, b).wait()


def owners_kernel(ids, mine, other, out):
    me = lax.axis_index("tiles")
    chip = me >> 1
    core = me & 1
    out[...] = jnp.zeros_like(out)
    for side, rec in ((0, mine), (4, other)):
        for k in range(2):
            for i, o, n, src in (
                (ids[side + k, chip], SR, AR, AR * k),
                (ids[side + 2 + k, chip], 0, SR, 8 + SR * k),
            ):

                @pl.when((i >= 0) & ((i & 1) == core))
                def _():
                    rows = pl.ds((i >> 1) * OUT + o, n)
                    out[rows, :] = out[rows, :] + rec[src : src + n, :]


def last_kernel(rec, own, bounds, adv_out, slot_out):
    n = 2 * OUT
    parts = [rec[g * n : (g + 1) * n, :] for g in range(CHIPS // 2)]
    total = tree(parts)
    total = total[0:OUT] + total[OUT:n]
    slot_out[...] = jnp.maximum(own[0:SR, :] + (total[0:SR] - bounds[0:SR, :]) * (1.0 / 512), 0.0)
    adv_out[...] = jnp.maximum(own[SR:OUT, :] + (total[SR:OUT] - bounds[SR:OUT, :]) * (1.0 / 1024), 0.0)


def f32(*shape):
    return jax.ShapeDtypeStruct(shape, jnp.float32)


def vmem(*shape):
    return pltpu.VMEM(shape, jnp.float32)


def in_vmem(x):
    return pltpu.with_memory_space_constraint(x, pltpu.VMEM)


def in_smem(x):
    return pltpu.with_memory_space_constraint(x, pltpu.SMEM)


def call(kernel, name, ins, outs, scratch=(), mib=4):
    return pl.pallas_call(
        kernel,
        in_specs=[s for _, s in ins],
        out_specs=[s for _, s in outs],
        out_shape=[o for o, _ in outs],
        scratch_shapes=list(scratch),
        compiler_params=pltpu.CompilerParams(vmem_limit_bytes=mib << 20),
        name=name,
    )(*[x for x, _ in ins])


def in_hbm(x):
    return pltpu.with_memory_space_constraint(x, pltpu.HBM)


def hbm_arg(x):
    return (in_hbm(x), pl.BlockSpec(memory_space=pl.ANY))


def smem_out(*shape):
    return (pltpu.SMEM(shape, jnp.int32), IN_SMEM)


def smem_arg(x):
    return (in_smem(x), IN_SMEM)


def vmem_arg(x):
    return (in_vmem(x), IN_VMEM)


def vmem_out(*shape):
    return (vmem(*shape), IN_VMEM)


def exchange(x, groups, rows):
    n = len(groups[0])
    x = lax.all_to_all(x.reshape(n, rows * L), "tiles", 0, 0, axis_index_groups=groups, tiled=True)
    return vmem_arg(x.reshape(n * rows, L))


def swap(x):
    return lax.ppermute(x, "tiles", PARTNERS)


def body(primal_start, cost, mask, tile_adv, tile_slot, adv_dual, slot_dual, spend_limit, capacity):
    tile = (2, 512, 1024)
    message, bias, bounds, row_ids, own_ids, here = call(
        own_kernel,
        "own",
        [(in_hbm(tile_adv), IN_SMEM), (in_hbm(tile_slot), IN_SMEM)]
        + [(in_hbm(x.reshape(-1, L)), IN_VMEM) for x in (adv_dual, slot_dual, spend_limit, capacity)]
        + [hbm_arg(mask.transpose(0, 2, 1))],
        [vmem_out(CHIPS * OWN, L), vmem_out(OUT, L), vmem_out(OUT, L)]
        + [(pltpu.VMEM((8, L), jnp.int32), IN_VMEM), smem_out(4), smem_out(2, 8, 64)],
        [pltpu.SemaphoreType.DMA(())],
    )
    table = exchange(message, CORE_GROUPS, OWN)
    block = pl.BlockSpec((1, RB, 1024), lambda t, rb: (t, rb, 0))
    hc, psum = pl.pallas_call(
        prepare_kernel,
        grid=(2, NRB),
        in_specs=[IN_SMEM, IN_SMEM, block, block],
        out_specs=[IN_VMEM, IN_VMEM],
        out_shape=[pltpu.VMEM(tile, jnp.bfloat16), vmem(TS, L)],
        scratch_shapes=[vmem(RB, L), vmem(64, L)],
        compiler_params=pltpu.CompilerParams(vmem_limit_bytes=4 << 20),
        name="prepare",
    )(in_smem(own_ids), in_smem(here), in_hbm(primal_start), in_hbm(cost))
    (picked,) = call(pick_kernel, "pick", [vmem_arg(swap(row_ids)), table, vmem_arg(psum)], [vmem_out(SEL, L)])
    (start,) = call(
        load_kernel,
        "load",
        [hbm_arg(primal_start), vmem_arg(picked)],
        [vmem_out(*tile[1:])],
        [pltpu.SemaphoreType.DMA(())],
    )
    base, usum, message, ids = call(
        first_kernel,
        "first",
        [smem_arg(own_ids), table, vmem_arg(picked), vmem_arg(swap(picked)), vmem_arg(bias), vmem_arg(psum), vmem_arg(hc)]
        + [vmem_arg(start), hbm_arg(primal_start)],
        [vmem_out(*tile), vmem_out(TS, L), vmem_out(MSG, L), smem_out(8, L)],
        [vmem(*tile[1:]), vmem(512, L), vmem(512, L), pltpu.VMEM((8, L), jnp.int32)]
        + [pltpu.SemaphoreType.DMA((NRB,)), pltpu.SemaphoreType.DMA(())],
        8,
    )
    (both,) = call(pair_kernel, "pair", [vmem_arg(message), vmem_arg(swap(message))], [vmem_out(2 * MSG, L)])
    parts = [vmem_arg(both)] + [vmem_arg(lax.ppermute(both, "tiles", along_x(d))) for d in range(1, 4)]
    (message,) = call(
        users_kernel,
        "users",
        [smem_arg(ids)] + parts,
        [vmem_out(PLANE * MSG, L)],
        [vmem(8 * MSG, L)] + [vmem((BLOCKS + 1) * 8, L)] * 4,
    )
    primal, sums, own = call(
        second_kernel,
        "second",
        [exchange(message, PLANE_GROUPS, MSG), vmem_arg(base), vmem_arg(usum)],
        [(f32(*tile), pl.BlockSpec(memory_space=pl.ANY)), vmem_out(TS, L), vmem_out(OUT, L)],
        [vmem(*tile), vmem(TS, L), vmem(512, L), vmem(512, L), pltpu.SemaphoreType.DMA((2 * NRB,))],
        8,
    )
    (message,) = call(
        owners_kernel, "owners", [smem_arg(ids), vmem_arg(sums), vmem_arg(swap(sums))], [vmem_out(CHIPS * OUT, L)]
    )
    adv_out, slot_out = call(
        last_kernel,
        "last",
        [exchange(message, CORE_GROUPS, OUT), vmem_arg(own), vmem_arg(bounds)],
        [(f32(AR, L), IN_VMEM), (f32(SR, L), IN_VMEM)],
    )
    return primal, adv_out.reshape(1, 512), slot_out.reshape(1, 1024)


def solution(mesh):
    return jax.shard_map(
        body,
        mesh=mesh,
        in_specs=(
            P("tiles", None, None),
            P("tiles", None, None),
            P("tiles", None, None),
            P("tiles"),
            P("tiles"),
            P("tiles", None),
            P("tiles", None),
            P("tiles", None),
            P("tiles", None),
        ),
        out_specs=(P("tiles", None, None), P("tiles", None), P("tiles", None)),
        check_vma=False,
    )
```

```python
import functools

import jax
import jax.numpy as jnp
from jax import lax
from jax.experimental import pallas as pl
from jax.experimental.pallas import tpu as pltpu
from jax.sharding import PartitionSpec as P

CHIPS = 64
BLOCKS = 128
L = 128
AR = 4
SR = 8
OWN = AR + SR + 1
SEL = 2 * (AR + SR) + 8
TS = 2 * (AR + SR)
MSG = TS + SR + AR
OUT = SR + AR
RB = 128
NRB = 4
BIG = 1e30
HEAD = 256
TAIL = 256

PLANE = 16
CORE_GROUPS = [[j * 2 + c for j in range(CHIPS)] for c in range(2)]
PLANE_GROUPS = [[(x * PLANE + j) * 2 + c for j in range(PLANE)] for x in range(4) for c in range(2)]
PARTNERS = [(i, i ^ 1) for i in range(2 * CHIPS)]


def along_x(d):
    return [(i, (i + d * 2 * PLANE) % (2 * CHIPS)) for i in range(2 * CHIPS)]


IN_VMEM = pl.BlockSpec(memory_space=pltpu.VMEM)
IN_SMEM = pl.BlockSpec(memory_space=pltpu.SMEM)


def own_kernel(adv_id, slot_id, adv, slot, limit, cap, out, bias, bounds, row_ids, ids):
    lane = lax.broadcasted_iota(jnp.int32, (8, L), 1)
    row = jnp.zeros((8, L), jnp.int32)
    for k, v in enumerate((adv_id[0], adv_id[1], slot_id[0], slot_id[1])):
        row = jnp.where(lane == k, v, row)
        ids[k] = v
    row_ids[...] = row
    data = jnp.concatenate([slot[...], adv[...], row[0:1].astype(jnp.float32)], axis=0)
    for j in range(CHIPS):
        out[j * OWN : (j + 1) * OWN, :] = data
    bias[0:SR, :] = slot[...] * 512.0 - cap[...]
    bias[SR:OUT, :] = adv[...] * 1024.0 - limit[...]
    bounds[0:SR, :] = cap[...]
    bounds[SR:OUT, :] = limit[...]


def rows_of(rec, i, slot):
    at = (jnp.maximum(i, 0) >> 1) * OWN
    return rec[pl.ds(at, SR), :] if slot else rec[pl.ds(at + SR, AR), :]


def pick_kernel(partner_ids, rec, _, out):

    lane = lax.broadcasted_iota(jnp.int32, (1, L), 1)
    row = partner_ids[0:1, :]
    wanted = [jnp.max(jnp.where(lane == k, row, -1)) for k in range(4)]
    for k in range(2):
        out[AR * k : AR * (k + 1), :] = rows_of(rec, wanted[k], False)
        out[8 + SR * k : 8 + SR * (k + 1), :] = rows_of(rec, wanted[2 + k], True)
    ids = rec[pl.ds(OWN - 1, CHIPS, stride=OWN), :]
    out[TS:SEL, :] = jnp.concatenate([ids, ids], axis=0).T[0:8, :]


def spread_half(row, buf):
    for b in range(NRB):
        block = jnp.broadcast_to(0.5 * row[b : b + 1, :], (L, L))
        buf[b * L : (b + 1) * L, :] = block.T


def tree(xs):
    while len(xs) > 1:
        xs = [xs[i] + xs[i + 1] for i in range(0, len(xs), 2)]
    return xs[0]


def write_sums(t, sums, r_buf, cols):
    for b in range(NRB):
        sums[t * AR + b : t * AR + b + 1, :] = jnp.sum(r_buf[b * L : (b + 1) * L, :].T, axis=0, keepdims=True)
    rows = [jnp.sum(c, axis=0, keepdims=True) for c in cols]
    sums[8 + t * SR : 8 + (t + 1) * SR, :] = jnp.concatenate(rows, axis=0)


def slot_rows(srow):
    return [jnp.broadcast_to(0.5 * srow[cb : cb + 1, :], (8, L)) for cb in range(SR)]


ZEROS = lambda: (jnp.zeros((8, L), jnp.float32),) * SR


def prepare_kernel(own_ids, mask, p_hbm, c_hbm, hc, psum, p_ref, c_ref, r_buf, p_sems, c_sems):
    def fetch(t, b):
        rows = pl.ds(b * RB, RB)
        n = t * NRB + b
        return (
            pltpu.make_async_copy(p_hbm.at[t, rows, :], p_ref.at[t, rows, :], p_sems.at[n]),
            pltpu.make_async_copy(c_hbm.at[t, rows, :], c_ref.at[t, rows, :], c_sems.at[n]),
        )

    for t in range(2):
        for b in range(NRB):
            for copy in fetch(t, b):
                copy.start()
    for t in range(2):
        alive = jnp.where(own_ids[t] >= 0, 1, 0)

        def step(g, cols):
            r0 = pl.multiple_of(g * 16, 16)
            cols = list(cols)
            ps = [[], []]
            for cb in range(SR):
                lanes = pl.ds(cb * L, L)
                c16 = 0.5 * c_ref[t, pl.ds(r0, 16), lanes].astype(jnp.float32)
                halves = []
                for h in range(2):
                    here = jnp.full((8, L), mask[t, cb, g * 2 + h] * alive, jnp.int32) > 0
                    rows = pl.ds(pl.multiple_of(r0 + 8 * h, 8), 8)
                    p = jnp.where(here, p_ref[t, rows, lanes], 0.0)
                    halves.append(jnp.where(here, c16[8 * h : 8 * h + 8], BIG))
                    ps[h].append(p)
                    cols[cb] = cols[cb] + p
                hc[t, pl.ds(r0, 16), lanes] = jnp.concatenate(halves, axis=0).astype(jnp.bfloat16)
            for h in range(2):
                r_buf[pl.ds(pl.multiple_of(r0 + 8 * h, 8), 8), :] = tree(ps[h])
            return tuple(cols)

        cols = ZEROS()
        for b in range(NRB):
            for copy in fetch(t, b):
                copy.wait()
            cols = lax.fori_loop(b * 8, (b + 1) * 8, step, cols)
        write_sums(t, psum, r_buf, cols)


def load_kernel(p_hbm, _, out, sem):
    copy = pltpu.make_async_copy(p_hbm.at[0, pl.ds(0, HEAD), :], out, sem)
    copy.start()
    copy.wait()


def first_tile(t, arow, srow, sources, hc_ref, out, usum, a_buf, r_buf, ready):
    spread_half(arow, a_buf)
    s = slot_rows(srow)

    def step(p_ref, skip, g, cols):
        cols = list(cols)
        us = [[], []]
        r0 = pl.multiple_of(g * 16, 16)
        a = [a_buf[pl.ds(pl.multiple_of(r0 + 8 * h, 8), 8), :] for h in range(2)]
        for cb in range(SR):
            lanes = pl.ds(cb * L, L)
            c16 = hc_ref[t, pl.ds(r0, 16), lanes].astype(jnp.float32)
            for h in range(2):
                rows = pl.ds(pl.multiple_of(r0 + 8 * h, 8), 8)
                hc = c16[8 * h : 8 * h + 8]
                u = jnp.minimum(jnp.maximum(((p_ref[pl.ds(pl.multiple_of(r0 + 8 * h - skip, 8), 8), lanes] - hc) - a[h]) - s[cb], 0.0), 1.0)
                out[t, rows, lanes] = u - hc
                us[h].append(u)
                cols[cb] = cols[cb] + u
        for h in range(2):
            r_buf[pl.ds(pl.multiple_of(r0 + 8 * h, 8), 8), :] = tree(us[h])
        return tuple(cols)

    cols = ZEROS()
    for b in range(NRB):
        ready(b)
        cols = lax.fori_loop(b * 8, (b + 1) * 8, functools.partial(step, *sources[b]), cols, unroll=2)
    write_sums(t, usum, r_buf, cols)


def first_kernel(own_ids, rec, mine, other, bias, psum, hc_ref, head, p_hbm, out, usum, msg, ids, p_ref, a_buf, r_buf, id_buf, p_sems, sem):
    def fetch(t, b):
        n = (t * NRB + b) * RB - HEAD
        return pltpu.make_async_copy(p_hbm.at[t, pl.ds(b * RB, RB), :], p_ref.at[pl.ds(n, RB), :], p_sems.at[n // RB])

    def ready(t, b):
        if (t * NRB + b) * RB >= HEAD:
            fetch(t, b).wait()

    for n in range(HEAD // RB, 2 * NRB):
        fetch(*divmod(n, NRB)).start()
    core = lax.axis_index("tiles") & 1
    id_buf[0:4, :] = mine[TS : TS + 4, :].astype(jnp.int32)
    id_buf[4:8, :] = other[TS : TS + 4, :].astype(jnp.int32)
    keep_ids = pltpu.make_async_copy(id_buf, ids, sem)
    keep_ids.start()
    for t in range(2):
        a, s = own_ids[t], own_ids[2 + t]
        arow = jnp.where((a & 1) == core, rows_of(rec, a, False), other[AR * t : AR * (t + 1), :])
        srow = jnp.where((s & 1) == core, rows_of(rec, s, True), other[8 + SR * t : 8 + SR * (t + 1), :])
        sources = [(head, 0) if t * 512 + b * RB < HEAD else (p_ref, HEAD - t * 512) for b in range(NRB)]
        first_tile(t, arow, srow, sources, hc_ref, out, usum, a_buf, r_buf, functools.partial(ready, t))
    msg[0:TS, :] = 2.0 * usum[...] - psum[...]
    msg[TS:MSG, :] = bias[...]
    keep_ids.wait()


def pair_kernel(a, b, out):
    out[0:MSG, :] = a[...]
    out[MSG:, :] = b[...]


def users_kernel(ids, rec0, rec1, rec2, rec3, out, rec, acc_a0, acc_a1, acc_s0, acc_s1):
    me = lax.axis_index("tiles")
    chip = me >> 1
    core = me & 1
    x = chip >> 4
    line = chip & 15
    both = 2 * MSG

    def at(i):
        return pl.multiple_of(jnp.where(i < 0, BLOCKS, i) * 8, 8)

    wanted = []
    for j in range(PLANE):
        there = (x << 4) | j
        o = j * MSG
        index = there * 2 + core
        adv = [(ids[k, there], o + AR * k) for k in range(2)] + [(index, o + TS + SR)]
        slot = [(ids[2 + k, there], o + 8 + SR * k) for k in range(2)] + [(index, o + TS)]
        wanted.append((adv, slot))
    zero = jnp.zeros((8, L), jnp.float32)
    for adv, slot in wanted:
        for i, _ in adv:
            acc_a0[pl.ds(at(i), 8), :] = zero
            acc_a1[pl.ds(at(i), 8), :] = zero
        for i, _ in slot:
            acc_s0[pl.ds(at(i), 8), :] = zero
            acc_s1[pl.ds(at(i), 8), :] = zero
    for d, part in enumerate((rec0, rec1, rec2, rec3)):
        rec[d * both : (d + 1) * both, :] = part[...]
        source = (((x - d) & 3) << 4) | line
        for side in range(2):
            o = side * MSG
            for k, acc in ((0, acc_a0), (1, acc_a1)):
                rows = pl.ds(at(ids[4 * side + k, source]), AR)
                acc[rows, :] = acc[rows, :] + part[o + AR * k : o + AR * (k + 1), :]
            for k, acc in ((0, acc_s0), (1, acc_s1)):
                rows = pl.ds(at(ids[4 * side + 2 + k, source]), SR)
                acc[rows, :] = acc[rows, :] + part[o + 8 + SR * k : o + 8 + SR * (k + 1), :]

    def bias(i, o, n):
        b = jnp.maximum(i, 0)
        here = ((b >> 1) & 15) == line
        row = ((x - (b >> 5)) & 3) * both + ((b & 1) ^ core) * MSG + o
        return rec[pl.ds(row, n), :] * jnp.where(here, 1.0, 0.0)

    for adv, slot in wanted:
        for i, o in adv:
            rows = pl.ds(at(i), AR)
            out[o : o + AR, :] = (acc_a0[rows, :] + acc_a1[rows, :]) + bias(i, TS + SR, AR)
        for i, o in slot:
            rows = pl.ds(at(i), SR)
            out[o : o + SR, :] = (acc_s0[rows, :] + acc_s1[rows, :]) + bias(i, TS, SR)


def second_tile(t, arow, srow, base, outs, usum, a_buf, r_buf, done):
    spread_half(arow, a_buf)
    s = slot_rows(srow)

    def step(out, skip, g, cols):
        rows = pl.ds(pl.multiple_of(g * 8, 8), 8)
        a = a_buf[rows, :]
        cols = list(cols)
        us = []
        for cb in range(SR):
            lanes = pl.ds(cb * L, L)
            u = jnp.minimum(jnp.maximum((base[t, rows, lanes] - a) - s[cb], 0.0), 1.0)
            out[pl.ds(pl.multiple_of(g * 8 - skip, 8), 8), lanes] = u
            cols[cb] = cols[cb] + u
            us.append(u)
        r_buf[rows, :] = tree(us)
        return tuple(cols)

    cols = ZEROS()
    for b in range(NRB):
        cols = lax.fori_loop(b * 16, (b + 1) * 16, functools.partial(step, *outs[b]), cols, unroll=4)
        done(t, b)
    write_sums(t, usum, r_buf, cols)


def second_kernel(rec, base, psum, primal, sums, own, tail, out, usum, a_buf, r_buf, sems):
    early = 1024 - TAIL

    def keep(t, b):
        n = t * NRB + b
        return pltpu.make_async_copy(out.at[pl.ds(n * RB, RB), :], primal.at[t, pl.ds(b * RB, RB), :], sems.at[n])

    def done(t, b):
        if (t * NRB + b) * RB < early:
            keep(t, b).start()

    total = tree([rec[j * MSG : (j + 1) * MSG, :] for j in range(PLANE)])
    adv = jnp.maximum(total[0:8] * (1.0 / 1024), 0.0)
    slot = jnp.maximum(total[8:32] * (1.0 / 512), 0.0)
    own[0:SR, :] = slot[16:24]
    own[SR:OUT, :] = jnp.maximum(total[32:36] * (1.0 / 1024), 0.0)
    for t in range(2):
        outs = [(out, -t * 512) if t * 512 + b * RB < early else (tail, early - t * 512) for b in range(NRB)]
        second_tile(t, adv[4 * t : 4 * t + 4], slot[8 * t : 8 * t + 8], base, outs, usum, a_buf, r_buf, done)
    sums[...] = 2.0 * usum[...] - psum[...]
    for n in range(early // RB):
        keep(*divmod(n, NRB)).wait()


def store_kernel(tail, _, primal, sem):
    copy = pltpu.make_async_copy(tail, primal.at[1, pl.ds(512 - TAIL, TAIL), :], sem)
    copy.start()
    copy.wait()


def owners_kernel(ids, mine, other, _, out):

    me = lax.axis_index("tiles")
    chip = me >> 1
    core = me & 1
    out[...] = jnp.zeros_like(out)
    for side, rec in ((0, mine), (4, other)):
        for k in range(2):
            for i, o, n, src in (
                (ids[side + k, chip], SR, AR, AR * k),
                (ids[side + 2 + k, chip], 0, SR, 8 + SR * k),
            ):

                @pl.when((i >= 0) & ((i & 1) == core))
                def _():
                    rows = pl.ds((i >> 1) * OUT + o, n)
                    out[rows, :] = out[rows, :] + rec[src : src + n, :]


def last_kernel(rec, own, bounds, adv_out, slot_out):
    n = 2 * OUT
    parts = [rec[g * n : (g + 1) * n, :] for g in range(CHIPS // 2)]
    total = tree(parts)
    total = total[0:OUT] + total[OUT:n]
    slot_out[...] = jnp.maximum(own[0:SR, :] + (total[0:SR] - bounds[0:SR, :]) * (1.0 / 512), 0.0)
    adv_out[...] = jnp.maximum(own[SR:OUT, :] + (total[SR:OUT] - bounds[SR:OUT, :]) * (1.0 / 1024), 0.0)


def f32(*shape):
    return jax.ShapeDtypeStruct(shape, jnp.float32)


def vmem(*shape):
    return pltpu.VMEM(shape, jnp.float32)


def in_vmem(x):
    return pltpu.with_memory_space_constraint(x, pltpu.VMEM)


def in_smem(x):
    return pltpu.with_memory_space_constraint(x, pltpu.SMEM)


def call(kernel, name, ins, outs, scratch=(), mib=4, aliases={}):
    return pl.pallas_call(
        kernel,
        in_specs=[s for _, s in ins],
        out_specs=[s for _, s in outs],
        out_shape=[o for o, _ in outs],
        scratch_shapes=list(scratch),
        compiler_params=pltpu.CompilerParams(vmem_limit_bytes=mib << 20),
        input_output_aliases=aliases,
        name=name,
    )(*[x for x, _ in ins])


def in_hbm(x):
    return pltpu.with_memory_space_constraint(x, pltpu.HBM)


def hbm_arg(x):
    return (in_hbm(x), pl.BlockSpec(memory_space=pl.ANY))


def smem_out(*shape):
    return (pltpu.SMEM(shape, jnp.int32), IN_SMEM)


def smem_arg(x):
    return (in_smem(x), IN_SMEM)


def vmem_arg(x):
    return (in_vmem(x), IN_VMEM)


def vmem_out(*shape):
    return (vmem(*shape), IN_VMEM)


def exchange(x, groups, rows):
    n = len(groups[0])
    x = lax.all_to_all(x.reshape(n, rows * L), "tiles", 0, 0, axis_index_groups=groups, tiled=True)
    return vmem_arg(x.reshape(n * rows, L))


def swap(x):
    return lax.ppermute(x, "tiles", PARTNERS)


def body(primal_start, cost, mask, tile_adv, tile_slot, adv_dual, slot_dual, spend_limit, capacity):
    tile = (2, 512, 1024)
    message, bias, bounds, row_ids, own_ids = call(
        own_kernel,
        "own",
        [(in_hbm(tile_adv), IN_SMEM), (in_hbm(tile_slot), IN_SMEM)]
        + [(in_hbm(x.reshape(-1, L)), IN_VMEM) for x in (adv_dual, slot_dual, spend_limit, capacity)],
        [vmem_out(CHIPS * OWN, L), vmem_out(OUT, L), vmem_out(OUT, L)]
        + [(pltpu.VMEM((8, L), jnp.int32), IN_VMEM), smem_out(4)],
    )
    table = exchange(message, CORE_GROUPS, OWN)
    hc, psum = call(
        prepare_kernel,
        "prepare",
        [smem_arg(own_ids), (in_hbm(mask.transpose(0, 2, 1)), IN_SMEM), hbm_arg(primal_start), hbm_arg(cost)],
        [(pltpu.VMEM(tile, jnp.bfloat16), IN_VMEM), vmem_out(TS, L)],
        [vmem(*tile), pltpu.VMEM(tile, jnp.bfloat16), vmem(512, L)] + [pltpu.SemaphoreType.DMA((2 * NRB,))] * 2,
        8,
    )
    (picked,) = call(pick_kernel, "pick", [vmem_arg(swap(row_ids)), table, vmem_arg(psum)], [vmem_out(SEL, L)])
    (start,) = call(
        load_kernel,
        "load",
        [hbm_arg(primal_start), vmem_arg(picked)],
        [vmem_out(HEAD, 1024)],
        [pltpu.SemaphoreType.DMA(())],
    )
    base, usum, message, ids = call(
        first_kernel,
        "first",
        [smem_arg(own_ids), table, vmem_arg(picked), vmem_arg(swap(picked)), vmem_arg(bias), vmem_arg(psum), vmem_arg(hc)]
        + [vmem_arg(start), hbm_arg(primal_start)],
        [vmem_out(*tile), vmem_out(TS, L), vmem_out(MSG, L), smem_out(8, L)],
        [vmem(1024 - HEAD, 1024), vmem(512, L), vmem(512, L), pltpu.VMEM((8, L), jnp.int32)]
        + [pltpu.SemaphoreType.DMA((2 * NRB - HEAD // RB,)), pltpu.SemaphoreType.DMA(())],
        8,
    )
    (both,) = call(pair_kernel, "pair", [vmem_arg(message), vmem_arg(swap(message))], [vmem_out(2 * MSG, L)])
    parts = [vmem_arg(both)] + [vmem_arg(lax.ppermute(both, "tiles", along_x(d))) for d in range(1, 4)]
    (message,) = call(
        users_kernel,
        "users",
        [smem_arg(ids)] + parts,
        [vmem_out(PLANE * MSG, L)],
        [vmem(8 * MSG, L)] + [vmem((BLOCKS + 1) * 8, L)] * 4,
    )
    primal, sums, own, tail = call(
        second_kernel,
        "second",
        [exchange(message, PLANE_GROUPS, MSG), vmem_arg(base), vmem_arg(usum)],
        [(f32(*tile), pl.BlockSpec(memory_space=pl.ANY))] + [vmem_out(TS, L), vmem_out(OUT, L), vmem_out(TAIL, 1024)],
        [vmem(1024 - TAIL, 1024), vmem(TS, L), vmem(512, L), vmem(512, L)]
        + [pltpu.SemaphoreType.DMA((2 * NRB - TAIL // RB,))],
        8,
    )
    (primal,) = call(
        store_kernel,
        "store",
        [vmem_arg(tail), hbm_arg(primal)],
        [(f32(*tile), pl.BlockSpec(memory_space=pl.ANY))],
        [pltpu.SemaphoreType.DMA(())],
        aliases={1: 0},
    )
    (message,) = call(
        owners_kernel,
        "owners",
        [smem_arg(ids), vmem_arg(sums), vmem_arg(swap(sums)), hbm_arg(primal)],
        [vmem_out(CHIPS * OUT, L)],
    )
    adv_out, slot_out = call(
        last_kernel,
        "last",
        [exchange(message, CORE_GROUPS, OUT), vmem_arg(own), vmem_arg(bounds)],
        [(f32(AR, L), IN_VMEM), (f32(SR, L), IN_VMEM)],
    )
    return primal, adv_out.reshape(1, 512), slot_out.reshape(1, 1024)


def solution(mesh):
    return jax.shard_map(
        body,
        mesh=mesh,
        in_specs=(
            P("tiles", None, None),
            P("tiles", None, None),
            P("tiles", None, None),
            P("tiles"),
            P("tiles"),
            P("tiles", None),
            P("tiles", None),
            P("tiles", None),
            P("tiles", None),
        ),
        out_specs=(P("tiles", None, None), P("tiles", None), P("tiles", None)),
        check_vma=False,
    )
```

```python
import functools

import jax
import jax.numpy as jnp
from jax import lax
from jax.experimental import pallas as pl
from jax.experimental.pallas import tpu as pltpu
from jax.sharding import PartitionSpec as P

CHIPS = 64
BLOCKS = 128
L = 128
AR = 4
SR = 8
OWN = AR + SR + 1
SEL = 2 * (AR + SR) + 8
TS = 2 * (AR + SR)
MSG = TS + SR + AR
OUT = SR + AR
RB = 128
NRB = 4
BIG = 1e30
HEAD = 128
AHEAD = 2
TAIL = 256

PLANE = 16
CORE_GROUPS = [[j * 2 + c for j in range(CHIPS)] for c in range(2)]
PLANE_GROUPS = [[(x * PLANE + j) * 2 + c for j in range(PLANE)] for x in range(4) for c in range(2)]
PARTNERS = [(i, i ^ 1) for i in range(2 * CHIPS)]


def along_x(d):
    return [(i, (i + d * 2 * PLANE) % (2 * CHIPS)) for i in range(2 * CHIPS)]


IN_VMEM = pl.BlockSpec(memory_space=pltpu.VMEM)
IN_SMEM = pl.BlockSpec(memory_space=pltpu.SMEM)


def own_kernel(adv_id, slot_id, adv, slot, limit, cap, out, bias, bounds, row_ids, ids):
    lane = lax.broadcasted_iota(jnp.int32, (8, L), 1)
    row = jnp.zeros((8, L), jnp.int32)
    for k, v in enumerate((adv_id[0], adv_id[1], slot_id[0], slot_id[1])):
        row = jnp.where(lane == k, v, row)
        ids[k] = v
    row_ids[...] = row
    data = jnp.concatenate([slot[...], adv[...], row[0:1].astype(jnp.float32)], axis=0)
    for j in range(CHIPS):
        out[j * OWN : (j + 1) * OWN, :] = data
    bias[0:SR, :] = slot[...] * 512.0 - cap[...]
    bias[SR:OUT, :] = adv[...] * 1024.0 - limit[...]
    bounds[0:SR, :] = cap[...]
    bounds[SR:OUT, :] = limit[...]


def rows_of(rec, i, slot):
    at = (jnp.maximum(i, 0) >> 1) * OWN
    return rec[pl.ds(at, SR), :] if slot else rec[pl.ds(at + SR, AR), :]


def pick_kernel(partner_ids, rec, _, out):

    lane = lax.broadcasted_iota(jnp.int32, (1, L), 1)
    row = partner_ids[0:1, :]
    wanted = [jnp.max(jnp.where(lane == k, row, -1)) for k in range(4)]
    for k in range(2):
        out[AR * k : AR * (k + 1), :] = rows_of(rec, wanted[k], False)
        out[8 + SR * k : 8 + SR * (k + 1), :] = rows_of(rec, wanted[2 + k], True)
    ids = rec[pl.ds(OWN - 1, CHIPS, stride=OWN), :]
    out[TS:SEL, :] = jnp.concatenate([ids, ids], axis=0).T[0:8, :]


def spread_half(row, buf):
    for b in range(NRB):
        block = jnp.broadcast_to(0.5 * row[b : b + 1, :], (L, L))
        buf[b * L : (b + 1) * L, :] = block.T


def tree(xs):
    while len(xs) > 1:
        xs = [xs[i] + xs[i + 1] for i in range(0, len(xs), 2)]
    return xs[0]


def write_sums(t, sums, r_buf, cols):
    for b in range(NRB):
        sums[t * AR + b : t * AR + b + 1, :] = jnp.sum(r_buf[b * L : (b + 1) * L, :].T, axis=0, keepdims=True)
    rows = [jnp.sum(c, axis=0, keepdims=True) for c in cols]
    sums[8 + t * SR : 8 + (t + 1) * SR, :] = jnp.concatenate(rows, axis=0)


def slot_rows(srow):
    return [jnp.broadcast_to(0.5 * srow[cb : cb + 1, :], (8, L)) for cb in range(SR)]


ZEROS = lambda: (jnp.zeros((8, L), jnp.float32),) * SR


def prepare_kernel(own_ids, mask, p_hbm, c_hbm, hc, psum, head, p_rest, c_ref, r_buf, p_sems, c_sems):
    def place(t, b):
        n = (t * NRB + b) * RB
        return (head, -t * 512) if n < HEAD else (p_rest, HEAD - t * 512)

    def fetch(t, b):
        rows = pl.ds(b * RB, RB)
        n = t * NRB + b
        p_ref, skip = place(t, b)
        return (
            pltpu.make_async_copy(p_hbm.at[t, rows, :], p_ref.at[pl.ds(b * RB - skip, RB), :], p_sems.at[n]),
            pltpu.make_async_copy(c_hbm.at[t, rows, :], c_ref.at[t, rows, :], c_sems.at[n]),
        )

    for t in range(2):
        for b in range(NRB):
            for copy in fetch(t, b):
                copy.start()
    for t in range(2):
        alive = jnp.where(own_ids[t] >= 0, 1, 0)

        def step(p_ref, skip, g, cols):
            r0 = pl.multiple_of(g * 16, 16)
            cols = list(cols)
            ps = [[], []]
            for cb in range(SR):
                lanes = pl.ds(cb * L, L)
                c16 = 0.5 * c_ref[t, pl.ds(r0, 16), lanes].astype(jnp.float32)
                halves = []
                for h in range(2):
                    here = jnp.full((8, L), mask[t, cb, g * 2 + h] * alive, jnp.int32) > 0
                    rows = pl.ds(pl.multiple_of(r0 + 8 * h - skip, 8), 8)
                    p = jnp.where(here, p_ref[rows, lanes], 0.0)
                    halves.append(jnp.where(here, c16[8 * h : 8 * h + 8], BIG))
                    ps[h].append(p)
                    cols[cb] = cols[cb] + p
                hc[t, pl.ds(r0, 16), lanes] = jnp.concatenate(halves, axis=0).astype(jnp.bfloat16)
            for h in range(2):
                r_buf[pl.ds(pl.multiple_of(r0 + 8 * h, 8), 8), :] = tree(ps[h])
            return tuple(cols)

        cols = ZEROS()
        for b in range(NRB):
            for copy in fetch(t, b):
                copy.wait()
            cols = lax.fori_loop(b * 8, (b + 1) * 8, functools.partial(step, *place(t, b)), cols)
        write_sums(t, psum, r_buf, cols)


def first_tile(t, arow, srow, sources, hc_ref, out, usum, a_buf, r_buf, ready):
    spread_half(arow, a_buf)
    s = slot_rows(srow)

    def step(p_ref, skip, g, cols):
        cols = list(cols)
        us = [[], []]
        r0 = pl.multiple_of(g * 16, 16)
        a = [a_buf[pl.ds(pl.multiple_of(r0 + 8 * h, 8), 8), :] for h in range(2)]
        for cb in range(SR):
            lanes = pl.ds(cb * L, L)
            c16 = hc_ref[t, pl.ds(r0, 16), lanes].astype(jnp.float32)
            for h in range(2):
                rows = pl.ds(pl.multiple_of(r0 + 8 * h, 8), 8)
                hc = c16[8 * h : 8 * h + 8]
                u = jnp.minimum(jnp.maximum(((p_ref[pl.ds(pl.multiple_of(r0 + 8 * h - skip, 8), 8), lanes] - hc) - a[h]) - s[cb], 0.0), 1.0)
                out[t, rows, lanes] = u - hc
                us[h].append(u)
                cols[cb] = cols[cb] + u
        for h in range(2):
            r_buf[pl.ds(pl.multiple_of(r0 + 8 * h, 8), 8), :] = tree(us[h])
        return tuple(cols)

    cols = ZEROS()
    for b in range(NRB):
        ready(b)
        cols = lax.fori_loop(b * 8, (b + 1) * 8, functools.partial(step, *sources[b]), cols, unroll=2)
    write_sums(t, usum, r_buf, cols)


def first_kernel(own_ids, rec, mine, other, bias, psum, hc_ref, head, p_hbm, out, usum, msg, ids, p_ref, a_buf, r_buf, id_buf, p_sems, sem):
    def fetch(t, b):
        n = (t * NRB + b) * RB - HEAD
        return pltpu.make_async_copy(p_hbm.at[t, pl.ds(b * RB, RB), :], p_ref.at[pl.ds(n, RB), :], p_sems.at[n // RB])

    first = HEAD // RB

    def ready(t, b):
        n = t * NRB + b
        if first + AHEAD <= n + AHEAD < 2 * NRB:
            fetch(*divmod(n + AHEAD, NRB)).start()
        if n >= first:
            fetch(t, b).wait()

    for n in range(first, first + AHEAD):
        fetch(*divmod(n, NRB)).start()
    core = lax.axis_index("tiles") & 1
    id_buf[0:4, :] = mine[TS : TS + 4, :].astype(jnp.int32)
    id_buf[4:8, :] = other[TS : TS + 4, :].astype(jnp.int32)
    keep_ids = pltpu.make_async_copy(id_buf, ids, sem)
    keep_ids.start()
    for t in range(2):
        a, s = own_ids[t], own_ids[2 + t]
        arow = jnp.where((a & 1) == core, rows_of(rec, a, False), other[AR * t : AR * (t + 1), :])
        srow = jnp.where((s & 1) == core, rows_of(rec, s, True), other[8 + SR * t : 8 + SR * (t + 1), :])
        sources = [(head, 0) if t * 512 + b * RB < HEAD else (p_ref, HEAD - t * 512) for b in range(NRB)]
        first_tile(t, arow, srow, sources, hc_ref, out, usum, a_buf, r_buf, functools.partial(ready, t))
    msg[0:TS, :] = 2.0 * usum[...] - psum[...]
    msg[TS:MSG, :] = bias[...]
    keep_ids.wait()


def pair_kernel(a, b, out):
    out[0:MSG, :] = a[...]
    out[MSG:, :] = b[...]


def flags_kernel(own_ids, mine, other, _, flags):
    me = lax.axis_index("tiles")
    core = me & 1
    lane = lax.broadcasted_iota(jnp.int32, (4, L), 1)
    row = lax.broadcasted_iota(jnp.int32, (4, L), 0)
    place = lane * 4 + jnp.where(row < 2, core, 1 - core) * 2 + (row & 1)

    def found(where):
        return jnp.max(jnp.where(where & (lane < CHIPS), 1, 0))

    for kind in range(2):
        rows = pl.ds(TS + 2 * kind, 2)
        ids = jnp.concatenate([mine[rows, :], other[rows, :]], axis=0).astype(jnp.int32)
        for k in range(2):
            i = own_ids[2 * kind + k]
            earlier = found((ids == i) & (place < me * 2 + k))
            flags[2 * kind + k] = jnp.where((i >= 0) & (earlier == 0), 1, 0)
        flags[4 + kind] = 1 - found(ids == me)


def users_kernel(ids, rec0, rec1, rec2, rec3, _, out, rec, acc_a0, acc_a1, acc_s0, acc_s1):
    me = lax.axis_index("tiles")
    chip = me >> 1
    core = me & 1
    x = chip >> 4
    line = chip & 15
    both = 2 * MSG

    def at(i):
        return pl.multiple_of(jnp.where(i < 0, BLOCKS, i) * 8, 8)

    wanted = []
    for j in range(PLANE):
        there = (x << 4) | j
        o = j * TS
        adv = [(ids[k, there], o + AR * k) for k in range(2)]
        slot = [(ids[2 + k, there], o + 8 + SR * k) for k in range(2)]
        wanted.append((adv, slot))
    zero = jnp.zeros((8, L), jnp.float32)
    for adv, slot in wanted:
        for i, _ in adv:
            acc_a0[pl.ds(at(i), 8), :] = zero
            acc_a1[pl.ds(at(i), 8), :] = zero
        for i, _ in slot:
            acc_s0[pl.ds(at(i), 8), :] = zero
            acc_s1[pl.ds(at(i), 8), :] = zero
    for d, part in enumerate((rec0, rec1, rec2, rec3)):
        rec[d * both : (d + 1) * both, :] = part[...]
        source = (((x - d) & 3) << 4) | line
        for side in range(2):
            o = side * MSG
            for k, acc in ((0, acc_a0), (1, acc_a1)):
                rows = pl.ds(at(ids[4 * side + k, source]), AR)
                acc[rows, :] = acc[rows, :] + part[o + AR * k : o + AR * (k + 1), :]
            for k, acc in ((0, acc_s0), (1, acc_s1)):
                rows = pl.ds(at(ids[4 * side + 2 + k, source]), SR)
                acc[rows, :] = acc[rows, :] + part[o + 8 + SR * k : o + 8 + SR * (k + 1), :]

    def bias(i, o, n):
        b = jnp.maximum(i, 0)
        here = ((b >> 1) & 15) == line
        row = ((x - (b >> 5)) & 3) * both + ((b & 1) ^ core) * MSG + o
        return rec[pl.ds(row, n), :] * jnp.where(here, 1.0, 0.0)

    for adv, slot in wanted:
        for i, o in adv:
            rows = pl.ds(at(i), AR)
            out[o : o + AR, :] = (acc_a0[rows, :] + acc_a1[rows, :]) + bias(i, TS + SR, AR)
        for i, o in slot:
            rows = pl.ds(at(i), SR)
            out[o : o + SR, :] = (acc_s0[rows, :] + acc_s1[rows, :]) + bias(i, TS, SR)


def second_tile(t, arow, srow, base, outs, usum, a_buf, r_buf, done):
    spread_half(arow, a_buf)
    s = slot_rows(srow)

    def step(out, skip, g, cols):
        rows = pl.ds(pl.multiple_of(g * 8, 8), 8)
        a = a_buf[rows, :]
        cols = list(cols)
        us = []
        for cb in range(SR):
            lanes = pl.ds(cb * L, L)
            u = jnp.minimum(jnp.maximum((base[t, rows, lanes] - a) - s[cb], 0.0), 1.0)
            out[pl.ds(pl.multiple_of(g * 8 - skip, 8), 8), lanes] = u
            cols[cb] = cols[cb] + u
            us.append(u)
        r_buf[rows, :] = tree(us)
        return tuple(cols)

    cols = ZEROS()
    for b in range(NRB):
        cols = lax.fori_loop(b * 16, (b + 1) * 16, functools.partial(step, *outs[b]), cols, unroll=4)
        done(t, b)
    write_sums(t, usum, r_buf, cols)


def second_kernel(flags, rec, base, psum, primal, sums, tail, out, usum, a_buf, r_buf, sems):
    early = 1024 - TAIL

    def keep(t, b):
        n = t * NRB + b
        return pltpu.make_async_copy(out.at[pl.ds(n * RB, RB), :], primal.at[t, pl.ds(b * RB, RB), :], sems.at[n])

    def done(t, b):
        if (t * NRB + b) * RB < early:
            keep(t, b).start()

    total = jnp.maximum(tree([rec[j * TS : (j + 1) * TS, :] for j in range(PLANE)]), 0.0)
    adv = total[0:8] * (1.0 / 1024)
    slot = total[8:24] * (1.0 / 512)
    for t in range(2):
        outs = [(out, -t * 512) if t * 512 + b * RB < early else (tail, early - t * 512) for b in range(NRB)]
        second_tile(t, adv[4 * t : 4 * t + 4], slot[8 * t : 8 * t + 8], base, outs, usum, a_buf, r_buf, done)
    for k, (o, n) in enumerate(((0, AR), (AR, AR), (8, SR), (8 + SR, SR))):
        rows = pl.ds(o, n)
        named = total[o : o + n] * jnp.where(flags[k] > 0, 1.0, 0.0)
        sums[rows, :] = named + (2.0 * usum[rows, :] - psum[rows, :])
    for n in range(early // RB):
        keep(*divmod(n, NRB)).wait()


def store_kernel(tail, _, primal, sem):
    copy = pltpu.make_async_copy(tail, primal.at[1, pl.ds(512 - TAIL, TAIL), :], sem)
    copy.start()
    copy.wait()


def owners_kernel(ids, mine, other, _, out):

    me = lax.axis_index("tiles")
    chip = me >> 1
    core = me & 1
    out[...] = jnp.zeros_like(out)
    for side, rec in ((0, mine), (4, other)):
        for k in range(2):
            for i, o, n, src in (
                (ids[side + k, chip], SR, AR, AR * k),
                (ids[side + 2 + k, chip], 0, SR, 8 + SR * k),
            ):

                @pl.when((i >= 0) & ((i & 1) == core))
                def _():
                    rows = pl.ds((i >> 1) * OUT + o, n)
                    out[rows, :] = out[rows, :] + rec[src : src + n, :]


def last_kernel(flags, rec, bias, bounds, adv_out, slot_out):
    n = 2 * OUT
    total = tree([rec[g * n : (g + 1) * n, :] for g in range(CHIPS // 2)])
    total = total[0:OUT] + total[OUT:n]
    unnamed = jnp.maximum(bias[...], 0.0)
    slot = total[0:SR] + unnamed[0:SR] * jnp.where(flags[5] > 0, 1.0, 0.0)
    adv = total[SR:OUT] + unnamed[SR:OUT] * jnp.where(flags[4] > 0, 1.0, 0.0)
    slot_out[...] = jnp.maximum((slot - bounds[0:SR, :]) * (1.0 / 512), 0.0)
    adv_out[...] = jnp.maximum((adv - bounds[SR:OUT, :]) * (1.0 / 1024), 0.0)


def f32(*shape):
    return jax.ShapeDtypeStruct(shape, jnp.float32)


def vmem(*shape):
    return pltpu.VMEM(shape, jnp.float32)


def in_vmem(x):
    return pltpu.with_memory_space_constraint(x, pltpu.VMEM)


def in_smem(x):
    return pltpu.with_memory_space_constraint(x, pltpu.SMEM)


def call(kernel, name, ins, outs, scratch=(), mib=4, aliases={}):
    return pl.pallas_call(
        kernel,
        in_specs=[s for _, s in ins],
        out_specs=[s for _, s in outs],
        out_shape=[o for o, _ in outs],
        scratch_shapes=list(scratch),
        compiler_params=pltpu.CompilerParams(vmem_limit_bytes=mib << 20),
        input_output_aliases=aliases,
        name=name,
    )(*[x for x, _ in ins])


def in_hbm(x):
    return pltpu.with_memory_space_constraint(x, pltpu.HBM)


def hbm_arg(x):
    return (in_hbm(x), pl.BlockSpec(memory_space=pl.ANY))


def smem_out(*shape):
    return (pltpu.SMEM(shape, jnp.int32), IN_SMEM)


def smem_arg(x):
    return (in_smem(x), IN_SMEM)


def vmem_arg(x):
    return (in_vmem(x), IN_VMEM)


def vmem_out(*shape):
    return (vmem(*shape), IN_VMEM)


def exchange(x, groups, rows):
    n = len(groups[0])
    x = lax.all_to_all(x.reshape(n, rows * L), "tiles", 0, 0, axis_index_groups=groups, tiled=True)
    return vmem_arg(x.reshape(n * rows, L))


def swap(x):
    return lax.ppermute(x, "tiles", PARTNERS)


def body(primal_start, cost, mask, tile_adv, tile_slot, adv_dual, slot_dual, spend_limit, capacity):
    tile = (2, 512, 1024)
    message, bias, bounds, row_ids, own_ids = call(
        own_kernel,
        "own",
        [(in_hbm(tile_adv), IN_SMEM), (in_hbm(tile_slot), IN_SMEM)]
        + [(in_hbm(x.reshape(-1, L)), IN_VMEM) for x in (adv_dual, slot_dual, spend_limit, capacity)],
        [vmem_out(CHIPS * OWN, L), vmem_out(OUT, L), vmem_out(OUT, L)]
        + [(pltpu.VMEM((8, L), jnp.int32), IN_VMEM), smem_out(4)],
    )
    table = exchange(message, CORE_GROUPS, OWN)
    hc, psum, head = call(
        prepare_kernel,
        "prepare",
        [smem_arg(own_ids), (in_hbm(mask.transpose(0, 2, 1)), IN_SMEM), hbm_arg(primal_start), hbm_arg(cost)],
        [(pltpu.VMEM(tile, jnp.bfloat16), IN_VMEM), vmem_out(TS, L), vmem_out(HEAD, 1024)],
        [vmem(1024 - HEAD, 1024), pltpu.VMEM(tile, jnp.bfloat16), vmem(512, L)] + [pltpu.SemaphoreType.DMA((2 * NRB,))] * 2,
        8,
    )
    (picked,) = call(pick_kernel, "pick", [vmem_arg(swap(row_ids)), table, vmem_arg(psum)], [vmem_out(SEL, L)])
    other = swap(picked)
    base, usum, message, ids = call(
        first_kernel,
        "first",
        [smem_arg(own_ids), table, vmem_arg(picked), vmem_arg(other), vmem_arg(bias), vmem_arg(psum), vmem_arg(hc)]
        + [vmem_arg(head), hbm_arg(primal_start)],
        [vmem_out(*tile), vmem_out(TS, L), vmem_out(MSG, L), smem_out(8, L)],
        [vmem(1024 - HEAD, 1024), vmem(512, L), vmem(512, L), pltpu.VMEM((8, L), jnp.int32)]
        + [pltpu.SemaphoreType.DMA((2 * NRB - HEAD // RB,)), pltpu.SemaphoreType.DMA(())],
        8,
    )
    (both,) = call(pair_kernel, "pair", [vmem_arg(message), vmem_arg(swap(message))], [vmem_out(2 * MSG, L)])
    parts = [vmem_arg(both)] + [vmem_arg(lax.ppermute(both, "tiles", along_x(d))) for d in range(1, 4)]
    (flags,) = call(
        flags_kernel,
        "flags",
        [smem_arg(own_ids), vmem_arg(picked), vmem_arg(other), vmem_arg(both)],
        [smem_out(6)],
    )
    (message,) = call(
        users_kernel,
        "users",
        [smem_arg(ids)] + parts + [smem_arg(flags)],
        [vmem_out(PLANE * TS, L)],
        [vmem(8 * MSG, L)] + [vmem((BLOCKS + 1) * 8, L)] * 4,
    )
    primal, sums, tail = call(
        second_kernel,
        "second",
        [smem_arg(flags), exchange(message, PLANE_GROUPS, TS), vmem_arg(base), vmem_arg(usum)],
        [(f32(*tile), pl.BlockSpec(memory_space=pl.ANY))] + [vmem_out(TS, L), vmem_out(TAIL, 1024)],
        [vmem(1024 - TAIL, 1024), vmem(TS, L), vmem(512, L), vmem(512, L)]
        + [pltpu.SemaphoreType.DMA((2 * NRB - TAIL // RB,))],
        8,
    )
    (primal,) = call(
        store_kernel,
        "store",
        [vmem_arg(tail), hbm_arg(primal)],
        [(f32(*tile), pl.BlockSpec(memory_space=pl.ANY))],
        [pltpu.SemaphoreType.DMA(())],
        aliases={1: 0},
    )
    (message,) = call(
        owners_kernel,
        "owners",
        [smem_arg(ids), vmem_arg(sums), vmem_arg(swap(sums)), hbm_arg(primal)],
        [vmem_out(CHIPS * OUT, L)],
    )
    adv_out, slot_out = call(
        last_kernel,
        "last",
        [smem_arg(flags), exchange(message, CORE_GROUPS, OUT), vmem_arg(bias), vmem_arg(bounds)],
        [(f32(AR, L), IN_VMEM), (f32(SR, L), IN_VMEM)],
    )
    return primal, adv_out.reshape(1, 512), slot_out.reshape(1, 1024)


def solution(mesh):
    return jax.shard_map(
        body,
        mesh=mesh,
        in_specs=(
            P("tiles", None, None),
            P("tiles", None, None),
            P("tiles", None, None),
            P("tiles"),
            P("tiles"),
            P("tiles", None),
            P("tiles", None),
            P("tiles", None),
            P("tiles", None),
        ),
        out_specs=(P("tiles", None, None), P("tiles", None), P("tiles", None)),
        check_vma=False,
    )
```

```python
import functools

import jax
import jax.numpy as jnp
from jax import lax
from jax.experimental import pallas as pl
from jax.experimental.pallas import tpu as pltpu
from jax.sharding import PartitionSpec as P

CHIPS = 64
BLOCKS = 128
L = 128
AR = 4
SR = 8
OWN = AR + SR + 1
SEL = 2 * (AR + SR) + 8
TS = 2 * (AR + SR)
MSG = TS + SR + AR
OUT = SR + AR
RB = 128
NRB = 4
BIG = 1e30
HEAD = 128
TAIL = 256

PLANE = 16
CORE_GROUPS = [[j * 2 + c for j in range(CHIPS)] for c in range(2)]
PLANE_GROUPS = [[(x * PLANE + j) * 2 + c for j in range(PLANE)] for x in range(4) for c in range(2)]
PARTNERS = [(i, i ^ 1) for i in range(2 * CHIPS)]


def along_x(d):
    return [(i, (i + d * 2 * PLANE) % (2 * CHIPS)) for i in range(2 * CHIPS)]


IN_VMEM = pl.BlockSpec(memory_space=pltpu.VMEM)
IN_SMEM = pl.BlockSpec(memory_space=pltpu.SMEM)


def own_kernel(adv_id, slot_id, adv, slot, limit, cap, out, bias, bounds, row_ids, ids):
    lane = lax.broadcasted_iota(jnp.int32, (8, L), 1)
    row = jnp.zeros((8, L), jnp.int32)
    for k, v in enumerate((adv_id[0], adv_id[1], slot_id[0], slot_id[1])):
        row = jnp.where(lane == k, v, row)
        ids[k] = v
    row_ids[...] = row
    data = jnp.concatenate([slot[...], adv[...], row[0:1].astype(jnp.float32)], axis=0)
    for j in range(CHIPS):
        out[j * OWN : (j + 1) * OWN, :] = data
    bias[0:SR, :] = slot[...] * 512.0 - cap[...]
    bias[SR:OUT, :] = adv[...] * 1024.0 - limit[...]
    bounds[0:SR, :] = cap[...]
    bounds[SR:OUT, :] = limit[...]


def rows_of(rec, i, slot):
    at = (jnp.maximum(i, 0) >> 1) * OWN
    return rec[pl.ds(at, SR), :] if slot else rec[pl.ds(at + SR, AR), :]


def pick_kernel(partner_ids, rec, _, out):

    lane = lax.broadcasted_iota(jnp.int32, (1, L), 1)
    row = partner_ids[0:1, :]
    wanted = [jnp.max(jnp.where(lane == k, row, -1)) for k in range(4)]
    for k in range(2):
        out[AR * k : AR * (k + 1), :] = rows_of(rec, wanted[k], False)
        out[8 + SR * k : 8 + SR * (k + 1), :] = rows_of(rec, wanted[2 + k], True)
    ids = rec[pl.ds(OWN - 1, CHIPS, stride=OWN), :]
    out[TS:SEL, :] = jnp.concatenate([ids, ids], axis=0).T[0:8, :]


def spread_half(row, buf):
    for b in range(NRB):
        block = jnp.broadcast_to(0.5 * row[b : b + 1, :], (L, L))
        buf[b * L : (b + 1) * L, :] = block.T


def tree(xs):
    while len(xs) > 1:
        xs = [xs[i] + xs[i + 1] for i in range(0, len(xs), 2)]
    return xs[0]


def write_sums(t, sums, r_buf, cols):
    for b in range(NRB):
        sums[t * AR + b : t * AR + b + 1, :] = jnp.sum(r_buf[b * L : (b + 1) * L, :].T, axis=0, keepdims=True)
    rows = [jnp.sum(c, axis=0, keepdims=True) for c in cols]
    sums[8 + t * SR : 8 + (t + 1) * SR, :] = jnp.concatenate(rows, axis=0)


def slot_rows(srow):
    return [jnp.broadcast_to(0.5 * srow[cb : cb + 1, :], (8, L)) for cb in range(SR)]


ZEROS = lambda: (jnp.zeros((8, L), jnp.float32),) * SR


def prepare_kernel(own_ids, mask, p_hbm, c_hbm, hc, psum, head, p_rest, c_ref, r_buf, p_sems, c_sems):
    def place(t, b):
        n = (t * NRB + b) * RB
        return (head, -t * 512) if n < HEAD else (p_rest, HEAD - t * 512)

    def fetch(t, b):
        rows = pl.ds(b * RB, RB)
        n = t * NRB + b
        p_ref, skip = place(t, b)
        return (
            pltpu.make_async_copy(p_hbm.at[t, rows, :], p_ref.at[pl.ds(b * RB - skip, RB), :], p_sems.at[n]),
            pltpu.make_async_copy(c_hbm.at[t, rows, :], c_ref.at[t, rows, :], c_sems.at[n]),
        )

    for t in range(2):
        for b in range(NRB):
            for copy in fetch(t, b):
                copy.start()
    for t in range(2):
        alive = jnp.where(own_ids[t] >= 0, 1, 0)

        def step(p_ref, skip, g, cols):
            r0 = pl.multiple_of(g * 16, 16)
            cols = list(cols)
            ps = [[], []]
            for cb in range(SR):
                lanes = pl.ds(cb * L, L)
                c16 = 0.5 * c_ref[t, pl.ds(r0, 16), lanes].astype(jnp.float32)
                halves = []
                for h in range(2):
                    here = jnp.full((8, L), mask[t, cb, g * 2 + h] * alive, jnp.int32) > 0
                    rows = pl.ds(pl.multiple_of(r0 + 8 * h - skip, 8), 8)
                    p = jnp.where(here, p_ref[rows, lanes], 0.0)
                    halves.append(jnp.where(here, c16[8 * h : 8 * h + 8], BIG))
                    ps[h].append(p)
                    cols[cb] = cols[cb] + p
                hc[t, pl.ds(r0, 16), lanes] = jnp.concatenate(halves, axis=0).astype(jnp.bfloat16)
            for h in range(2):
                r_buf[pl.ds(pl.multiple_of(r0 + 8 * h, 8), 8), :] = tree(ps[h])
            return tuple(cols)

        cols = ZEROS()
        for b in range(NRB):
            for copy in fetch(t, b):
                copy.wait()
            cols = lax.fori_loop(b * 8, (b + 1) * 8, functools.partial(step, *place(t, b)), cols)
        write_sums(t, psum, r_buf, cols)


def load_kernel(p_hbm, _, out, sem):
    copy = pltpu.make_async_copy(p_hbm.at[0, pl.ds(HEAD, 512 - HEAD), :], out, sem)
    copy.start()
    copy.wait()


def first_tile(t, arow, srow, sources, hc_ref, out, usum, a_buf, r_buf, ready):
    spread_half(arow, a_buf)
    s = slot_rows(srow)

    def step(p_ref, skip, g, cols):
        cols = list(cols)
        us = [[], []]
        r0 = pl.multiple_of(g * 16, 16)
        a = [a_buf[pl.ds(pl.multiple_of(r0 + 8 * h, 8), 8), :] for h in range(2)]
        for cb in range(SR):
            lanes = pl.ds(cb * L, L)
            c16 = hc_ref[t, pl.ds(r0, 16), lanes].astype(jnp.float32)
            for h in range(2):
                rows = pl.ds(pl.multiple_of(r0 + 8 * h, 8), 8)
                hc = c16[8 * h : 8 * h + 8]
                u = jnp.minimum(jnp.maximum(((p_ref[pl.ds(pl.multiple_of(r0 + 8 * h - skip, 8), 8), lanes] - hc) - a[h]) - s[cb], 0.0), 1.0)
                out[t, rows, lanes] = u - hc
                us[h].append(u)
                cols[cb] = cols[cb] + u
        for h in range(2):
            r_buf[pl.ds(pl.multiple_of(r0 + 8 * h, 8), 8), :] = tree(us[h])
        return tuple(cols)

    cols = ZEROS()
    for b in range(NRB):
        ready(b)
        cols = lax.fori_loop(b * 8, (b + 1) * 8, functools.partial(step, *sources[b]), cols, unroll=2)
    write_sums(t, usum, r_buf, cols)


def first_kernel(own_ids, rec, mine, other, bias, psum, hc_ref, head, rest, p_hbm, out, usum, msg, ids, p_ref, a_buf, r_buf, id_buf, p_sems, sem):
    def fetch(b):
        rows = pl.ds(b * RB, RB)
        return pltpu.make_async_copy(p_hbm.at[1, rows, :], p_ref.at[rows, :], p_sems.at[b])

    def ready(t, b):
        if t == 1:
            fetch(b).wait()

    for b in range(NRB):
        fetch(b).start()
    core = lax.axis_index("tiles") & 1
    id_buf[0:4, :] = mine[TS : TS + 4, :].astype(jnp.int32)
    id_buf[4:8, :] = other[TS : TS + 4, :].astype(jnp.int32)
    keep_ids = pltpu.make_async_copy(id_buf, ids, sem)
    keep_ids.start()
    for t in range(2):
        a, s = own_ids[t], own_ids[2 + t]
        arow = jnp.where((a & 1) == core, rows_of(rec, a, False), other[AR * t : AR * (t + 1), :])
        srow = jnp.where((s & 1) == core, rows_of(rec, s, True), other[8 + SR * t : 8 + SR * (t + 1), :])
        sources = [(p_ref, 0) if t else (head, 0) if b * RB < HEAD else (rest, HEAD) for b in range(NRB)]
        first_tile(t, arow, srow, sources, hc_ref, out, usum, a_buf, r_buf, functools.partial(ready, t))
    msg[0:TS, :] = 2.0 * usum[...] - psum[...]
    msg[TS:MSG, :] = bias[...]
    keep_ids.wait()


def pair_kernel(a, b, out):
    out[0:MSG, :] = a[...]
    out[MSG:, :] = b[...]


def flags_kernel(own_ids, mine, other, _, flags):
    me = lax.axis_index("tiles")
    core = me & 1
    lane = lax.broadcasted_iota(jnp.int32, (4, L), 1)
    row = lax.broadcasted_iota(jnp.int32, (4, L), 0)
    place = lane * 4 + jnp.where(row < 2, core, 1 - core) * 2 + (row & 1)

    def found(where):
        return jnp.max(jnp.where(where & (lane < CHIPS), 1, 0))

    for kind in range(2):
        rows = pl.ds(TS + 2 * kind, 2)
        ids = jnp.concatenate([mine[rows, :], other[rows, :]], axis=0).astype(jnp.int32)
        for k in range(2):
            i = own_ids[2 * kind + k]
            earlier = found((ids == i) & (place < me * 2 + k))
            flags[2 * kind + k] = jnp.where((i >= 0) & (earlier == 0), 1, 0)
        flags[4 + kind] = 1 - found(ids == me)


def users_kernel(ids, rec0, rec1, rec2, rec3, _, out, rec, acc_a0, acc_a1, acc_s0, acc_s1):
    me = lax.axis_index("tiles")
    chip = me >> 1
    core = me & 1
    x = chip >> 4
    line = chip & 15
    both = 2 * MSG

    def at(i):
        return pl.multiple_of(jnp.where(i < 0, BLOCKS, i) * 8, 8)

    wanted = []
    for j in range(PLANE):
        there = (x << 4) | j
        o = j * TS
        adv = [(ids[k, there], o + AR * k) for k in range(2)]
        slot = [(ids[2 + k, there], o + 8 + SR * k) for k in range(2)]
        wanted.append((adv, slot))
    zero = jnp.zeros((8, L), jnp.float32)
    for adv, slot in wanted:
        for i, _ in adv:
            acc_a0[pl.ds(at(i), 8), :] = zero
            acc_a1[pl.ds(at(i), 8), :] = zero
        for i, _ in slot:
            acc_s0[pl.ds(at(i), 8), :] = zero
            acc_s1[pl.ds(at(i), 8), :] = zero
    for d, part in enumerate((rec0, rec1, rec2, rec3)):
        rec[d * both : (d + 1) * both, :] = part[...]
        source = (((x - d) & 3) << 4) | line
        for side in range(2):
            o = side * MSG
            for k, acc in ((0, acc_a0), (1, acc_a1)):
                rows = pl.ds(at(ids[4 * side + k, source]), AR)
                acc[rows, :] = acc[rows, :] + part[o + AR * k : o + AR * (k + 1), :]
            for k, acc in ((0, acc_s0), (1, acc_s1)):
                rows = pl.ds(at(ids[4 * side + 2 + k, source]), SR)
                acc[rows, :] = acc[rows, :] + part[o + 8 + SR * k : o + 8 + SR * (k + 1), :]

    def bias(i, o, n):
        b = jnp.maximum(i, 0)
        here = ((b >> 1) & 15) == line
        row = ((x - (b >> 5)) & 3) * both + ((b & 1) ^ core) * MSG + o
        return rec[pl.ds(row, n), :] * jnp.where(here, 1.0, 0.0)

    for adv, slot in wanted:
        for i, o in adv:
            rows = pl.ds(at(i), AR)
            out[o : o + AR, :] = (acc_a0[rows, :] + acc_a1[rows, :]) + bias(i, TS + SR, AR)
        for i, o in slot:
            rows = pl.ds(at(i), SR)
            out[o : o + SR, :] = (acc_s0[rows, :] + acc_s1[rows, :]) + bias(i, TS, SR)


def second_tile(t, arow, srow, base, outs, usum, a_buf, r_buf, done):
    spread_half(arow, a_buf)
    s = slot_rows(srow)

    def step(out, skip, g, cols):
        rows = pl.ds(pl.multiple_of(g * 8, 8), 8)
        a = a_buf[rows, :]
        cols = list(cols)
        us = []
        for cb in range(SR):
            lanes = pl.ds(cb * L, L)
            u = jnp.minimum(jnp.maximum((base[t, rows, lanes] - a) - s[cb], 0.0), 1.0)
            out[pl.ds(pl.multiple_of(g * 8 - skip, 8), 8), lanes] = u
            cols[cb] = cols[cb] + u
            us.append(u)
        r_buf[rows, :] = tree(us)
        return tuple(cols)

    cols = ZEROS()
    for b in range(NRB):
        cols = lax.fori_loop(b * 16, (b + 1) * 16, functools.partial(step, *outs[b]), cols, unroll=4)
        done(t, b)
    write_sums(t, usum, r_buf, cols)


def second_kernel(flags, rec, base, psum, primal, sums, tail, out, usum, a_buf, r_buf, sems):
    early = 1024 - TAIL

    def keep(t, b):
        n = t * NRB + b
        return pltpu.make_async_copy(out.at[pl.ds(n * RB, RB), :], primal.at[t, pl.ds(b * RB, RB), :], sems.at[n])

    def done(t, b):
        if (t * NRB + b) * RB < early:
            keep(t, b).start()

    total = jnp.maximum(tree([rec[j * TS : (j + 1) * TS, :] for j in range(PLANE)]), 0.0)
    adv = total[0:8] * (1.0 / 1024)
    slot = total[8:24] * (1.0 / 512)
    for t in range(2):
        outs = [(out, -t * 512) if t * 512 + b * RB < early else (tail, early - t * 512) for b in range(NRB)]
        second_tile(t, adv[4 * t : 4 * t + 4], slot[8 * t : 8 * t + 8], base, outs, usum, a_buf, r_buf, done)
    for k, (o, n) in enumerate(((0, AR), (AR, AR), (8, SR), (8 + SR, SR))):
        rows = pl.ds(o, n)
        named = total[o : o + n] * jnp.where(flags[k] > 0, 1.0, 0.0)
        sums[rows, :] = named + (2.0 * usum[rows, :] - psum[rows, :])
    for n in range(early // RB):
        keep(*divmod(n, NRB)).wait()


def store_kernel(tail, _, primal, sem):
    copy = pltpu.make_async_copy(tail, primal.at[1, pl.ds(512 - TAIL, TAIL), :], sem)
    copy.start()
    copy.wait()


def owners_kernel(ids, mine, other, _, out):

    me = lax.axis_index("tiles")
    chip = me >> 1
    core = me & 1
    out[...] = jnp.zeros_like(out)
    for side, rec in ((0, mine), (4, other)):
        for k in range(2):
            for i, o, n, src in (
                (ids[side + k, chip], SR, AR, AR * k),
                (ids[side + 2 + k, chip], 0, SR, 8 + SR * k),
            ):

                @pl.when((i >= 0) & ((i & 1) == core))
                def _():
                    rows = pl.ds((i >> 1) * OUT + o, n)
                    out[rows, :] = out[rows, :] + rec[src : src + n, :]


def last_kernel(flags, rec, bias, bounds, adv_out, slot_out):
    n = 2 * OUT
    total = tree([rec[g * n : (g + 1) * n, :] for g in range(CHIPS // 2)])
    total = total[0:OUT] + total[OUT:n]
    unnamed = jnp.maximum(bias[...], 0.0)
    slot = total[0:SR] + unnamed[0:SR] * jnp.where(flags[5] > 0, 1.0, 0.0)
    adv = total[SR:OUT] + unnamed[SR:OUT] * jnp.where(flags[4] > 0, 1.0, 0.0)
    slot_out[...] = jnp.maximum((slot - bounds[0:SR, :]) * (1.0 / 512), 0.0)
    adv_out[...] = jnp.maximum((adv - bounds[SR:OUT, :]) * (1.0 / 1024), 0.0)


def f32(*shape):
    return jax.ShapeDtypeStruct(shape, jnp.float32)


def vmem(*shape):
    return pltpu.VMEM(shape, jnp.float32)


def in_vmem(x):
    return pltpu.with_memory_space_constraint(x, pltpu.VMEM)


def in_smem(x):
    return pltpu.with_memory_space_constraint(x, pltpu.SMEM)


def call(kernel, name, ins, outs, scratch=(), mib=4, aliases={}):
    return pl.pallas_call(
        kernel,
        in_specs=[s for _, s in ins],
        out_specs=[s for _, s in outs],
        out_shape=[o for o, _ in outs],
        scratch_shapes=list(scratch),
        compiler_params=pltpu.CompilerParams(vmem_limit_bytes=mib << 20),
        input_output_aliases=aliases,
        name=name,
    )(*[x for x, _ in ins])


def in_hbm(x):
    return pltpu.with_memory_space_constraint(x, pltpu.HBM)


def hbm_arg(x):
    return (in_hbm(x), pl.BlockSpec(memory_space=pl.ANY))


def smem_out(*shape):
    return (pltpu.SMEM(shape, jnp.int32), IN_SMEM)


def smem_arg(x):
    return (in_smem(x), IN_SMEM)


def vmem_arg(x):
    return (in_vmem(x), IN_VMEM)


def vmem_out(*shape):
    return (vmem(*shape), IN_VMEM)


def exchange(x, groups, rows):
    n = len(groups[0])
    x = lax.all_to_all(x.reshape(n, rows * L), "tiles", 0, 0, axis_index_groups=groups, tiled=True)
    return vmem_arg(x.reshape(n * rows, L))


def swap(x):
    return lax.ppermute(x, "tiles", PARTNERS)


def body(primal_start, cost, mask, tile_adv, tile_slot, adv_dual, slot_dual, spend_limit, capacity):
    tile = (2, 512, 1024)
    message, bias, bounds, row_ids, own_ids = call(
        own_kernel,
        "own",
        [(in_hbm(tile_adv), IN_SMEM), (in_hbm(tile_slot), IN_SMEM)]
        + [(in_hbm(x.reshape(-1, L)), IN_VMEM) for x in (adv_dual, slot_dual, spend_limit, capacity)],
        [vmem_out(CHIPS * OWN, L), vmem_out(OUT, L), vmem_out(OUT, L)]
        + [(pltpu.VMEM((8, L), jnp.int32), IN_VMEM), smem_out(4)],
    )
    table = exchange(message, CORE_GROUPS, OWN)
    hc, psum, head = call(
        prepare_kernel,
        "prepare",
        [smem_arg(own_ids), (in_hbm(mask.transpose(0, 2, 1)), IN_SMEM), hbm_arg(primal_start), hbm_arg(cost)],
        [(pltpu.VMEM(tile, jnp.bfloat16), IN_VMEM), vmem_out(TS, L), vmem_out(HEAD, 1024)],
        [vmem(1024 - HEAD, 1024), pltpu.VMEM(tile, jnp.bfloat16), vmem(512, L)] + [pltpu.SemaphoreType.DMA((2 * NRB,))] * 2,
        8,
    )
    (picked,) = call(pick_kernel, "pick", [vmem_arg(swap(row_ids)), table, vmem_arg(psum)], [vmem_out(SEL, L)])
    other = swap(picked)
    (rest,) = call(
        load_kernel,
        "load",
        [hbm_arg(primal_start), vmem_arg(picked)],
        [vmem_out(512 - HEAD, 1024)],
        [pltpu.SemaphoreType.DMA(())],
    )
    base, usum, message, ids = call(
        first_kernel,
        "first",
        [smem_arg(own_ids), table, vmem_arg(picked), vmem_arg(other), vmem_arg(bias), vmem_arg(psum), vmem_arg(hc)]
        + [vmem_arg(head), vmem_arg(rest), hbm_arg(primal_start)],
        [vmem_out(*tile), vmem_out(TS, L), vmem_out(MSG, L), smem_out(8, L)],
        [vmem(512, 1024), vmem(512, L), vmem(512, L), pltpu.VMEM((8, L), jnp.int32)]
        + [pltpu.SemaphoreType.DMA((NRB,)), pltpu.SemaphoreType.DMA(())],
        8,
    )
    (both,) = call(pair_kernel, "pair", [vmem_arg(message), vmem_arg(swap(message))], [vmem_out(2 * MSG, L)])
    parts = [vmem_arg(both)] + [vmem_arg(lax.ppermute(both, "tiles", along_x(d))) for d in range(1, 4)]
    (flags,) = call(
        flags_kernel,
        "flags",
        [smem_arg(own_ids), vmem_arg(picked), vmem_arg(other), vmem_arg(both)],
        [smem_out(6)],
    )
    (message,) = call(
        users_kernel,
        "users",
        [smem_arg(ids)] + parts + [smem_arg(flags)],
        [vmem_out(PLANE * TS, L)],
        [vmem(8 * MSG, L)] + [vmem((BLOCKS + 1) * 8, L)] * 4,
    )
    primal, sums, tail = call(
        second_kernel,
        "second",
        [smem_arg(flags), exchange(message, PLANE_GROUPS, TS), vmem_arg(base), vmem_arg(usum)],
        [(f32(*tile), pl.BlockSpec(memory_space=pl.ANY))] + [vmem_out(TS, L), vmem_out(TAIL, 1024)],
        [vmem(1024 - TAIL, 1024), vmem(TS, L), vmem(512, L), vmem(512, L)]
        + [pltpu.SemaphoreType.DMA((2 * NRB - TAIL // RB,))],
        8,
    )
    (primal,) = call(
        store_kernel,
        "store",
        [vmem_arg(tail), hbm_arg(primal)],
        [(f32(*tile), pl.BlockSpec(memory_space=pl.ANY))],
        [pltpu.SemaphoreType.DMA(())],
        aliases={1: 0},
    )
    (message,) = call(
        owners_kernel,
        "owners",
        [smem_arg(ids), vmem_arg(sums), vmem_arg(swap(sums)), hbm_arg(primal)],
        [vmem_out(CHIPS * OUT, L)],
    )
    adv_out, slot_out = call(
        last_kernel,
        "last",
        [smem_arg(flags), exchange(message, CORE_GROUPS, OUT), vmem_arg(bias), vmem_arg(bounds)],
        [(f32(AR, L), IN_VMEM), (f32(SR, L), IN_VMEM)],
    )
    return primal, adv_out.reshape(1, 512), slot_out.reshape(1, 1024)


def solution(mesh):
    return jax.shard_map(
        body,
        mesh=mesh,
        in_specs=(
            P("tiles", None, None),
            P("tiles", None, None),
            P("tiles", None, None),
            P("tiles"),
            P("tiles"),
            P("tiles", None),
            P("tiles", None),
            P("tiles", None),
            P("tiles", None),
        ),
        out_specs=(P("tiles", None, None), P("tiles", None), P("tiles", None)),
        check_vma=False,
    )
```

```python
import functools

import jax
import jax.numpy as jnp
from jax import lax
from jax.experimental import pallas as pl
from jax.experimental.pallas import tpu as pltpu
from jax.sharding import PartitionSpec as P

CHIPS = 64
BLOCKS = 128
L = 128
AR = 4
SR = 8
OWN = AR + SR + 1
SEL = 2 * (AR + SR) + 8
TS = 2 * (AR + SR)
MSG = TS + SR + AR
OUT = SR + AR
RB = 128
NRB = 4
BIG = 1e30
HEAD = 128
TAIL = 256

PLANE = 16
CORE_GROUPS = [[j * 2 + c for j in range(CHIPS)] for c in range(2)]
PLANE_GROUPS = [[(x * PLANE + j) * 2 + c for j in range(PLANE)] for x in range(4) for c in range(2)]
PARTNERS = [(i, i ^ 1) for i in range(2 * CHIPS)]


def along_x(d):
    return [(i, (i + d * 2 * PLANE) % (2 * CHIPS)) for i in range(2 * CHIPS)]


IN_VMEM = pl.BlockSpec(memory_space=pltpu.VMEM)
IN_SMEM = pl.BlockSpec(memory_space=pltpu.SMEM)


def own_kernel(adv_id, slot_id, adv, slot, limit, cap, out, bias, bounds, row_ids, ids):
    lane = lax.broadcasted_iota(jnp.int32, (8, L), 1)
    row = jnp.zeros((8, L), jnp.int32)
    for k, v in enumerate((adv_id[0], adv_id[1], slot_id[0], slot_id[1])):
        row = jnp.where(lane == k, v, row)
        ids[k] = v
    row_ids[...] = row
    data = jnp.concatenate([slot[...], adv[...], row[0:1].astype(jnp.float32)], axis=0)
    for j in range(CHIPS):
        out[j * OWN : (j + 1) * OWN, :] = data
    bias[0:SR, :] = slot[...] * 512.0 - cap[...]
    bias[SR:OUT, :] = adv[...] * 1024.0 - limit[...]
    bounds[0:SR, :] = cap[...]
    bounds[SR:OUT, :] = limit[...]


def rows_of(rec, i, slot):
    at = (jnp.maximum(i, 0) >> 1) * OWN
    return rec[pl.ds(at, SR), :] if slot else rec[pl.ds(at + SR, AR), :]


def pick_kernel(partner_ids, rec, _, out):

    lane = lax.broadcasted_iota(jnp.int32, (1, L), 1)
    row = partner_ids[0:1, :]
    wanted = [jnp.max(jnp.where(lane == k, row, -1)) for k in range(4)]
    for k in range(2):
        out[AR * k : AR * (k + 1), :] = rows_of(rec, wanted[k], False)
        out[8 + SR * k : 8 + SR * (k + 1), :] = rows_of(rec, wanted[2 + k], True)
    ids = rec[pl.ds(OWN - 1, CHIPS, stride=OWN), :]
    out[TS:SEL, :] = jnp.concatenate([ids, ids], axis=0).T[0:8, :]


def spread_half(rows, buf):
    for b in range(rows.shape[0]):
        block = jnp.broadcast_to(0.5 * rows[b : b + 1, :], (L, L))
        buf[b * L : (b + 1) * L, :] = block.T


def tree(xs):
    while len(xs) > 1:
        xs = [xs[i] + xs[i + 1] for i in range(0, len(xs), 2)]
    return xs[0]


def write_rows(sums, r_buf, tiles=(0, 1)):
    for n in range(len(tiles) * NRB):
        o = tiles[0] * AR + n
        sums[o : o + 1, :] = jnp.sum(r_buf[n * L : (n + 1) * L, :].T, axis=0, keepdims=True)


def write_cols(t, sums, cols):
    rows = [jnp.sum(c, axis=0, keepdims=True) for c in cols]
    sums[8 + t * SR : 8 + (t + 1) * SR, :] = jnp.concatenate(rows, axis=0)


def slot_rows(srow):
    return [jnp.broadcast_to(0.5 * srow[cb : cb + 1, :], (8, L)) for cb in range(SR)]


ZEROS = lambda: (jnp.zeros((8, L), jnp.float32),) * SR


def prepare_kernel(own_ids, mask, p_hbm, c_hbm, hc, psum, head, p_rest, c_ref, r_buf, p_sems, c_sems):
    def place(t, b):
        n = (t * NRB + b) * RB
        return (head, -t * 512) if n < HEAD else (p_rest, HEAD - t * 512)

    def fetch(t, b):
        rows = pl.ds(b * RB, RB)
        n = t * NRB + b
        p_ref, skip = place(t, b)
        return (
            pltpu.make_async_copy(p_hbm.at[t, rows, :], p_ref.at[pl.ds(b * RB - skip, RB), :], p_sems.at[n]),
            pltpu.make_async_copy(c_hbm.at[t, rows, :], c_ref.at[t, rows, :], c_sems.at[n]),
        )

    for t in range(2):
        for b in range(NRB):
            for copy in fetch(t, b):
                copy.start()
    for t in range(2):
        alive = jnp.where(own_ids[t] >= 0, 1, 0)

        def step(p_ref, skip, g, cols):
            r0 = pl.multiple_of(g * 16, 16)
            cols = list(cols)
            ps = [[], []]
            for cb in range(SR):
                lanes = pl.ds(cb * L, L)
                c16 = 0.5 * c_ref[t, pl.ds(r0, 16), lanes].astype(jnp.float32)
                halves = []
                for h in range(2):
                    here = jnp.full((8, L), mask[t, cb, g * 2 + h] * alive, jnp.int32) > 0
                    rows = pl.ds(pl.multiple_of(r0 + 8 * h - skip, 8), 8)
                    p = jnp.where(here, p_ref[rows, lanes], 0.0)
                    halves.append(jnp.where(here, c16[8 * h : 8 * h + 8], BIG))
                    ps[h].append(p)
                    cols[cb] = cols[cb] + p
                hc[t, pl.ds(r0, 16), lanes] = jnp.concatenate(halves, axis=0).astype(jnp.bfloat16)
            for h in range(2):
                r_buf[pl.ds(pl.multiple_of(r0 + 8 * h, 8), 8), :] = tree(ps[h])
            return tuple(cols)

        cols = ZEROS()
        for b in range(NRB):
            for copy in fetch(t, b):
                copy.wait()
            cols = lax.fori_loop(b * 8, (b + 1) * 8, functools.partial(step, *place(t, b)), cols)
        write_rows(psum, r_buf, (t,))
        write_cols(t, psum, cols)


def load_kernel(p_hbm, _, out, sem):
    copy = pltpu.make_async_copy(p_hbm.at[0, pl.ds(HEAD, 512 - HEAD), :], out, sem)
    copy.start()
    copy.wait()


def first_tile(t, srow, sources, hc_ref, out, usum, a_buf, r_buf, ready):
    s = slot_rows(srow)

    def step(p_ref, skip, g, cols):
        cols = list(cols)
        us = [[], []]
        r0 = pl.multiple_of(g * 16, 16)
        a = [a_buf[pl.ds(pl.multiple_of(t * 512 + r0 + 8 * h, 8), 8), :] for h in range(2)]
        for cb in range(SR):
            lanes = pl.ds(cb * L, L)
            c16 = hc_ref[t, pl.ds(r0, 16), lanes].astype(jnp.float32)
            for h in range(2):
                p = p_ref[pl.ds(pl.multiple_of(r0 + 8 * h - skip, 8), 8), lanes]
                u = jnp.minimum(jnp.maximum(((p - c16[8 * h : 8 * h + 8]) - a[h]) - s[cb], 0.0), 1.0)
                out[t, pl.ds(pl.multiple_of(r0 + 8 * h, 8), 8), lanes] = u
                us[h].append(u)
                cols[cb] = cols[cb] + u
        for h in range(2):
            r_buf[pl.ds(pl.multiple_of(t * 512 + r0 + 8 * h, 8), 8), :] = tree(us[h])
        return tuple(cols)

    cols = ZEROS()
    for b in range(NRB):
        ready(t, b)
        cols = lax.fori_loop(b * 8, (b + 1) * 8, functools.partial(step, *sources[b]), cols, unroll=2)
    write_cols(t, usum, cols)


def first_kernel(own_ids, rec, mine, other, bias, psum, hc_ref, head, rest, p_hbm, out, usum, msg, ids, p_ref, a_buf, r_buf, id_buf, p_sems, sem):
    def fetch(b):
        rows = pl.ds(b * RB, RB)
        return pltpu.make_async_copy(p_hbm.at[1, rows, :], p_ref.at[rows, :], p_sems.at[b])

    def ready(t, b):
        if t == 1:
            fetch(b).wait()

    for b in range(NRB):
        fetch(b).start()
    core = lax.axis_index("tiles") & 1
    id_buf[0:4, :] = mine[TS : TS + 4, :].astype(jnp.int32)
    id_buf[4:8, :] = other[TS : TS + 4, :].astype(jnp.int32)
    keep_ids = pltpu.make_async_copy(id_buf, ids, sem)
    keep_ids.start()
    slots = []
    for t in range(2):
        a, s = own_ids[t], own_ids[2 + t]
        arow = jnp.where((a & 1) == core, rows_of(rec, a, False), other[AR * t : AR * (t + 1), :])
        spread_half(arow, a_buf.at[pl.ds(t * 512, 512), :])
        slots.append(jnp.where((s & 1) == core, rows_of(rec, s, True), other[8 + SR * t : 8 + SR * (t + 1), :]))
    for t in range(2):
        sources = [(p_ref, 0) if t else (head, 0) if b * RB < HEAD else (rest, HEAD) for b in range(NRB)]
        first_tile(t, slots[t], sources, hc_ref, out, usum, a_buf, r_buf, ready)
    write_rows(usum, r_buf)
    msg[0:TS, :] = 2.0 * usum[...] - psum[...]
    msg[TS:MSG, :] = bias[...]
    keep_ids.wait()


def pair_kernel(a, b, out):
    out[0:MSG, :] = a[...]
    out[MSG:, :] = b[...]


def between_kernel(own_ids, mine, other, u, hc, _, flags, base):
    me = lax.axis_index("tiles")
    core = me & 1
    lane = lax.broadcasted_iota(jnp.int32, (4, L), 1)
    row = lax.broadcasted_iota(jnp.int32, (4, L), 0)
    place = lane * 4 + jnp.where(row < 2, core, 1 - core) * 2 + (row & 1)

    def found(where):
        return jnp.max(jnp.where(where & (lane < CHIPS), 1, 0))

    for kind in range(2):
        rows = pl.ds(TS + 2 * kind, 2)
        ids = jnp.concatenate([mine[rows, :], other[rows, :]], axis=0).astype(jnp.int32)
        for k in range(2):
            i = own_ids[2 * kind + k]
            earlier = found((ids == i) & (place < me * 2 + k))
            flags[2 * kind + k] = jnp.where((i >= 0) & (earlier == 0), 1, 0)
        flags[4 + kind] = 1 - found(ids == me)

    def step(g, carry):
        rows = pl.ds(pl.multiple_of(g * 16, 16), 16)
        for t in range(2):
            base[t, rows, :] = u[t, rows, :] - hc[t, rows, :].astype(jnp.float32)
        return carry

    lax.fori_loop(0, 32, step, 0, unroll=2)


def users_kernel(ids, rec0, rec1, rec2, rec3, _, out, rec, acc_a0, acc_a1, acc_s0, acc_s1):
    me = lax.axis_index("tiles")
    chip = me >> 1
    core = me & 1
    x = chip >> 4
    line = chip & 15
    both = 2 * MSG

    def at(i):
        return pl.multiple_of(jnp.where(i < 0, BLOCKS, i) * 8, 8)

    wanted = []
    for j in range(PLANE):
        there = (x << 4) | j
        o = j * TS
        adv = [(ids[k, there], o + AR * k) for k in range(2)]
        slot = [(ids[2 + k, there], o + 8 + SR * k) for k in range(2)]
        wanted.append((adv, slot))
    zero = jnp.zeros((8, L), jnp.float32)
    for adv, slot in wanted:
        for i, _ in adv:
            acc_a0[pl.ds(at(i), 8), :] = zero
            acc_a1[pl.ds(at(i), 8), :] = zero
        for i, _ in slot:
            acc_s0[pl.ds(at(i), 8), :] = zero
            acc_s1[pl.ds(at(i), 8), :] = zero
    for d, part in ((0, rec0), (1, rec1), (3, rec2), (2, rec3)):
        rec[d * both : (d + 1) * both, :] = part[...]
        source = (((x - d) & 3) << 4) | line
        for side in range(2):
            o = side * MSG
            for k, acc in ((0, acc_a0), (1, acc_a1)):
                rows = pl.ds(at(ids[4 * side + k, source]), AR)
                acc[rows, :] = acc[rows, :] + part[o + AR * k : o + AR * (k + 1), :]
            for k, acc in ((0, acc_s0), (1, acc_s1)):
                rows = pl.ds(at(ids[4 * side + 2 + k, source]), SR)
                acc[rows, :] = acc[rows, :] + part[o + 8 + SR * k : o + 8 + SR * (k + 1), :]

    def bias(i, o, n):
        b = jnp.maximum(i, 0)
        here = ((b >> 1) & 15) == line
        row = ((x - (b >> 5)) & 3) * both + ((b & 1) ^ core) * MSG + o
        return rec[pl.ds(row, n), :] * jnp.where(here, 1.0, 0.0)

    for adv, slot in wanted:
        for i, o in adv:
            rows = pl.ds(at(i), AR)
            out[o : o + AR, :] = (acc_a0[rows, :] + acc_a1[rows, :]) + bias(i, TS + SR, AR)
        for i, o in slot:
            rows = pl.ds(at(i), SR)
            out[o : o + SR, :] = (acc_s0[rows, :] + acc_s1[rows, :]) + bias(i, TS, SR)


def second_tile(t, srow, base, outs, usum, a_buf, r_buf, done):
    s = slot_rows(srow)

    def step(out, skip, g, cols):
        rows = pl.ds(pl.multiple_of(g * 8, 8), 8)
        wide = pl.ds(pl.multiple_of(t * 512 + g * 8, 8), 8)
        a = a_buf[wide, :]
        cols = list(cols)
        us = []
        for cb in range(SR):
            lanes = pl.ds(cb * L, L)
            u = jnp.minimum(jnp.maximum((base[t, rows, lanes] - a) - s[cb], 0.0), 1.0)
            out[pl.ds(pl.multiple_of(g * 8 - skip, 8), 8), lanes] = u
            cols[cb] = cols[cb] + u
            us.append(u)
        r_buf[wide, :] = tree(us)
        return tuple(cols)

    cols = ZEROS()
    for b in range(NRB):
        cols = lax.fori_loop(b * 16, (b + 1) * 16, functools.partial(step, *outs[b]), cols, unroll=4)
        done(t, b)
    write_cols(t, usum, cols)


def second_kernel(flags, rec, base, psum, primal, sums, tail, out, usum, a_buf, r_buf, sems):
    early = 1024 - TAIL

    def keep(t, b):
        n = t * NRB + b
        return pltpu.make_async_copy(out.at[pl.ds(n * RB, RB), :], primal.at[t, pl.ds(b * RB, RB), :], sems.at[n])

    def done(t, b):
        if (t * NRB + b) * RB < early:
            keep(t, b).start()

    total = jnp.maximum(tree([rec[j * TS : (j + 1) * TS, :] for j in range(PLANE)]), 0.0)
    adv = total[0:8] * (1.0 / 1024)
    slot = total[8:24] * (1.0 / 512)
    spread_half(adv, a_buf)
    for t in range(2):
        outs = [(out, -t * 512) if t * 512 + b * RB < early else (tail, early - t * 512) for b in range(NRB)]
        second_tile(t, slot[8 * t : 8 * t + 8], base, outs, usum, a_buf, r_buf, done)
    write_rows(usum, r_buf)
    for k, (o, n) in enumerate(((0, AR), (AR, AR), (8, SR), (8 + SR, SR))):
        rows = pl.ds(o, n)
        named = total[o : o + n] * jnp.where(flags[k] > 0, 1.0, 0.0)
        sums[rows, :] = named + (2.0 * usum[rows, :] - psum[rows, :])
    for n in range(early // RB):
        keep(*divmod(n, NRB)).wait()


def store_kernel(tail, _, primal, sem):
    copy = pltpu.make_async_copy(tail, primal.at[1, pl.ds(512 - TAIL, TAIL), :], sem)
    copy.start()
    copy.wait()


def owners_kernel(ids, mine, other, _, out):

    me = lax.axis_index("tiles")
    chip = me >> 1
    core = me & 1
    out[...] = jnp.zeros_like(out)
    for side, rec in ((0, mine), (4, other)):
        for k in range(2):
            for i, o, n, src in (
                (ids[side + k, chip], SR, AR, AR * k),
                (ids[side + 2 + k, chip], 0, SR, 8 + SR * k),
            ):

                @pl.when((i >= 0) & ((i & 1) == core))
                def _():
                    rows = pl.ds((i >> 1) * OUT + o, n)
                    out[rows, :] = out[rows, :] + rec[src : src + n, :]


def last_kernel(flags, rec, bias, bounds, adv_out, slot_out):
    n = 2 * OUT
    total = tree([rec[g * n : (g + 1) * n, :] for g in range(CHIPS // 2)])
    total = total[0:OUT] + total[OUT:n]
    unnamed = jnp.maximum(bias[...], 0.0)
    slot = total[0:SR] + unnamed[0:SR] * jnp.where(flags[5] > 0, 1.0, 0.0)
    adv = total[SR:OUT] + unnamed[SR:OUT] * jnp.where(flags[4] > 0, 1.0, 0.0)
    slot_out[...] = jnp.maximum((slot - bounds[0:SR, :]) * (1.0 / 512), 0.0)
    adv_out[...] = jnp.maximum((adv - bounds[SR:OUT, :]) * (1.0 / 1024), 0.0)


def f32(*shape):
    return jax.ShapeDtypeStruct(shape, jnp.float32)


def vmem(*shape):
    return pltpu.VMEM(shape, jnp.float32)


def in_vmem(x):
    return pltpu.with_memory_space_constraint(x, pltpu.VMEM)


def in_smem(x):
    return pltpu.with_memory_space_constraint(x, pltpu.SMEM)


def call(kernel, name, ins, outs, scratch=(), mib=4, aliases={}):
    return pl.pallas_call(
        kernel,
        in_specs=[s for _, s in ins],
        out_specs=[s for _, s in outs],
        out_shape=[o for o, _ in outs],
        scratch_shapes=list(scratch),
        compiler_params=pltpu.CompilerParams(vmem_limit_bytes=mib << 20),
        input_output_aliases=aliases,
        name=name,
    )(*[x for x, _ in ins])


def in_hbm(x):
    return pltpu.with_memory_space_constraint(x, pltpu.HBM)


def hbm_arg(x):
    return (in_hbm(x), pl.BlockSpec(memory_space=pl.ANY))


def smem_out(*shape):
    return (pltpu.SMEM(shape, jnp.int32), IN_SMEM)


def smem_arg(x):
    return (in_smem(x), IN_SMEM)


def vmem_arg(x):
    return (in_vmem(x), IN_VMEM)


def vmem_out(*shape):
    return (vmem(*shape), IN_VMEM)


def exchange(x, groups, rows):
    n = len(groups[0])
    x = lax.all_to_all(x.reshape(n, rows * L), "tiles", 0, 0, axis_index_groups=groups, tiled=True)
    return vmem_arg(x.reshape(n * rows, L))


def swap(x):
    return lax.ppermute(x, "tiles", PARTNERS)


def body(primal_start, cost, mask, tile_adv, tile_slot, adv_dual, slot_dual, spend_limit, capacity):
    tile = (2, 512, 1024)
    message, bias, bounds, row_ids, own_ids = call(
        own_kernel,
        "own",
        [(in_hbm(tile_adv), IN_SMEM), (in_hbm(tile_slot), IN_SMEM)]
        + [(in_hbm(x.reshape(-1, L)), IN_VMEM) for x in (adv_dual, slot_dual, spend_limit, capacity)],
        [vmem_out(CHIPS * OWN, L), vmem_out(OUT, L), vmem_out(OUT, L)]
        + [(pltpu.VMEM((8, L), jnp.int32), IN_VMEM), smem_out(4)],
    )
    table = exchange(message, CORE_GROUPS, OWN)
    hc, psum, head = call(
        prepare_kernel,
        "prepare",
        [smem_arg(own_ids), (in_hbm(mask.transpose(0, 2, 1)), IN_SMEM), hbm_arg(primal_start), hbm_arg(cost)],
        [(pltpu.VMEM(tile, jnp.bfloat16), IN_VMEM), vmem_out(TS, L), vmem_out(HEAD, 1024)],
        [vmem(1024 - HEAD, 1024), pltpu.VMEM(tile, jnp.bfloat16), vmem(512, L)] + [pltpu.SemaphoreType.DMA((2 * NRB,))] * 2,
        8,
    )
    (picked,) = call(pick_kernel, "pick", [vmem_arg(swap(row_ids)), table, vmem_arg(psum)], [vmem_out(SEL, L)])
    other = swap(picked)
    (rest,) = call(
        load_kernel,
        "load",
        [hbm_arg(primal_start), vmem_arg(picked)],
        [vmem_out(512 - HEAD, 1024)],
        [pltpu.SemaphoreType.DMA(())],
    )
    update, usum, message, ids = call(
        first_kernel,
        "first",
        [smem_arg(own_ids), table, vmem_arg(picked), vmem_arg(other), vmem_arg(bias), vmem_arg(psum), vmem_arg(hc)]
        + [vmem_arg(head), vmem_arg(rest), hbm_arg(primal_start)],
        [vmem_out(*tile), vmem_out(TS, L), vmem_out(MSG, L), smem_out(8, L)],
        [vmem(512, 1024), vmem(1024, L), vmem(1024, L), pltpu.VMEM((8, L), jnp.int32)]
        + [pltpu.SemaphoreType.DMA((NRB,)), pltpu.SemaphoreType.DMA(())],
        8,
    )
    (both,) = call(pair_kernel, "pair", [vmem_arg(message), vmem_arg(swap(message))], [vmem_out(2 * MSG, L)])
    parts = [vmem_arg(both)] + [vmem_arg(lax.ppermute(both, "tiles", along_x(d))) for d in (1, 3, 2)]
    flags, base = call(
        between_kernel,
        "between",
        [smem_arg(own_ids), vmem_arg(picked), vmem_arg(other), vmem_arg(update), vmem_arg(hc), vmem_arg(both)],
        [smem_out(6), vmem_out(*tile)],
    )
    (message,) = call(
        users_kernel,
        "users",
        [smem_arg(ids)] + parts + [smem_arg(flags)],
        [vmem_out(PLANE * TS, L)],
        [vmem(8 * MSG, L)] + [vmem((BLOCKS + 1) * 8, L)] * 4,
    )
    primal, sums, tail = call(
        second_kernel,
        "second",
        [smem_arg(flags), exchange(message, PLANE_GROUPS, TS), vmem_arg(base), vmem_arg(usum)],
        [(f32(*tile), pl.BlockSpec(memory_space=pl.ANY))] + [vmem_out(TS, L), vmem_out(TAIL, 1024)],
        [vmem(1024 - TAIL, 1024), vmem(TS, L), vmem(1024, L), vmem(1024, L)]
        + [pltpu.SemaphoreType.DMA((2 * NRB - TAIL // RB,))],
        8,
    )
    (primal,) = call(
        store_kernel,
        "store",
        [vmem_arg(tail), hbm_arg(primal)],
        [(f32(*tile), pl.BlockSpec(memory_space=pl.ANY))],
        [pltpu.SemaphoreType.DMA(())],
        aliases={1: 0},
    )
    (message,) = call(
        owners_kernel,
        "owners",
        [smem_arg(ids), vmem_arg(sums), vmem_arg(swap(sums)), hbm_arg(primal)],
        [vmem_out(CHIPS * OUT, L)],
    )
    adv_out, slot_out = call(
        last_kernel,
        "last",
        [smem_arg(flags), exchange(message, CORE_GROUPS, OUT), vmem_arg(bias), vmem_arg(bounds)],
        [(f32(AR, L), IN_VMEM), (f32(SR, L), IN_VMEM)],
    )
    return primal, adv_out.reshape(1, 512), slot_out.reshape(1, 1024)


def solution(mesh):
    return jax.shard_map(
        body,
        mesh=mesh,
        in_specs=(
            P("tiles", None, None),
            P("tiles", None, None),
            P("tiles", None, None),
            P("tiles"),
            P("tiles"),
            P("tiles", None),
            P("tiles", None),
            P("tiles", None),
            P("tiles", None),
        ),
        out_specs=(P("tiles", None, None), P("tiles", None), P("tiles", None)),
        check_vma=False,
    )
```

```python
import functools

import jax
import jax.numpy as jnp
from jax import lax
from jax.experimental import pallas as pl
from jax.experimental.pallas import tpu as pltpu
from jax.sharding import PartitionSpec as P

CHIPS = 64
BLOCKS = 128
L = 128
AR = 4
SR = 8
OWN = AR + SR + 1
SEL = 2 * (AR + SR) + 8
TS = 2 * (AR + SR)
MSG = TS + SR + AR
OUT = SR + AR
RB = 128
NRB = 4
BIG = 1e30
HEAD = 128
TAIL = 256

PLANE = 16
CORE_GROUPS = [[j * 2 + c for j in range(CHIPS)] for c in range(2)]
PLANE_GROUPS = [[(x * PLANE + j) * 2 + c for j in range(PLANE)] for x in range(4) for c in range(2)]
LINE = 8
LINE_GROUPS = [[(x * PLANE + j) * 2 + c for x in range(4) for c in range(2)] for j in range(PLANE)]
PARTNERS = [(i, i ^ 1) for i in range(2 * CHIPS)]


IN_VMEM = pl.BlockSpec(memory_space=pltpu.VMEM)
IN_SMEM = pl.BlockSpec(memory_space=pltpu.SMEM)


def own_kernel(adv_id, slot_id, adv, slot, limit, cap, out, bias, bounds, row_ids, ids):
    lane = lax.broadcasted_iota(jnp.int32, (8, L), 1)
    row = jnp.zeros((8, L), jnp.int32)
    for k, v in enumerate((adv_id[0], adv_id[1], slot_id[0], slot_id[1])):
        row = jnp.where(lane == k, v, row)
        ids[k] = v
    row_ids[...] = row
    data = jnp.concatenate([slot[...], adv[...], row[0:1].astype(jnp.float32)], axis=0)
    for j in range(CHIPS):
        out[j * OWN : (j + 1) * OWN, :] = data
    bias[0:SR, :] = slot[...] * 512.0 - cap[...]
    bias[SR:OUT, :] = adv[...] * 1024.0 - limit[...]
    bounds[0:SR, :] = cap[...]
    bounds[SR:OUT, :] = limit[...]


def rows_of(rec, i, slot):
    at = (jnp.maximum(i, 0) >> 1) * OWN
    return rec[pl.ds(at, SR), :] if slot else rec[pl.ds(at + SR, AR), :]


def pick_kernel(partner_ids, rec, _, out):

    lane = lax.broadcasted_iota(jnp.int32, (1, L), 1)
    row = partner_ids[0:1, :]
    wanted = [jnp.max(jnp.where(lane == k, row, -1)) for k in range(4)]
    for k in range(2):
        out[AR * k : AR * (k + 1), :] = rows_of(rec, wanted[k], False)
        out[8 + SR * k : 8 + SR * (k + 1), :] = rows_of(rec, wanted[2 + k], True)
    ids = rec[pl.ds(OWN - 1, CHIPS, stride=OWN), :]
    out[TS:SEL, :] = jnp.concatenate([ids, ids], axis=0).T[0:8, :]


def spread_half(rows, buf):
    for b in range(rows.shape[0]):
        block = jnp.broadcast_to(0.5 * rows[b : b + 1, :], (L, L))
        buf[b * L : (b + 1) * L, :] = block.T


def tree(xs):
    while len(xs) > 1:
        xs = [xs[i] + xs[i + 1] for i in range(0, len(xs), 2)]
    return xs[0]


def write_rows(sums, r_buf, tiles=(0, 1)):
    for n in range(len(tiles) * NRB):
        o = tiles[0] * AR + n
        sums[o : o + 1, :] = jnp.sum(r_buf[n * L : (n + 1) * L, :].T, axis=0, keepdims=True)


def write_cols(t, sums, cols):
    rows = [jnp.sum(c, axis=0, keepdims=True) for c in cols]
    sums[8 + t * SR : 8 + (t + 1) * SR, :] = jnp.concatenate(rows, axis=0)


def slot_rows(srow):
    return [jnp.broadcast_to(0.5 * srow[cb : cb + 1, :], (8, L)) for cb in range(SR)]


ZEROS = lambda: (jnp.zeros((8, L), jnp.float32),) * SR


def prepare_kernel(own_ids, mask, p_hbm, c_hbm, hc, psum, head, p_rest, c_ref, r_buf, p_sems, c_sems):
    def place(t, b):
        n = (t * NRB + b) * RB
        return (head, -t * 512) if n < HEAD else (p_rest, HEAD - t * 512)

    def fetch(t, b):
        rows = pl.ds(b * RB, RB)
        n = t * NRB + b
        p_ref, skip = place(t, b)
        return (
            pltpu.make_async_copy(p_hbm.at[t, rows, :], p_ref.at[pl.ds(b * RB - skip, RB), :], p_sems.at[n]),
            pltpu.make_async_copy(c_hbm.at[t, rows, :], c_ref.at[t, rows, :], c_sems.at[n]),
        )

    for t in range(2):
        for b in range(NRB):
            for copy in fetch(t, b):
                copy.start()
    for t in range(2):
        alive = jnp.where(own_ids[t] >= 0, 1, 0)

        def step(p_ref, skip, g, cols):
            r0 = pl.multiple_of(g * 16, 16)
            cols = list(cols)
            ps = [[], []]
            for cb in range(SR):
                lanes = pl.ds(cb * L, L)
                c16 = 0.5 * c_ref[t, pl.ds(r0, 16), lanes].astype(jnp.float32)
                halves = []
                for h in range(2):
                    here = jnp.full((8, L), mask[t, cb, g * 2 + h] * alive, jnp.int32) > 0
                    rows = pl.ds(pl.multiple_of(r0 + 8 * h - skip, 8), 8)
                    p = jnp.where(here, p_ref[rows, lanes], 0.0)
                    halves.append(jnp.where(here, c16[8 * h : 8 * h + 8], BIG))
                    ps[h].append(p)
                    cols[cb] = cols[cb] + p
                hc[t, pl.ds(r0, 16), lanes] = jnp.concatenate(halves, axis=0).astype(jnp.bfloat16)
            for h in range(2):
                r_buf[pl.ds(pl.multiple_of(r0 + 8 * h, 8), 8), :] = tree(ps[h])
            return tuple(cols)

        cols = ZEROS()
        for b in range(NRB):
            for copy in fetch(t, b):
                copy.wait()
            cols = lax.fori_loop(b * 8, (b + 1) * 8, functools.partial(step, *place(t, b)), cols)
        write_rows(psum, r_buf, (t,))
        write_cols(t, psum, cols)


def load_kernel(p_hbm, _, out, sem):
    copy = pltpu.make_async_copy(p_hbm.at[0, pl.ds(HEAD, 512 - HEAD), :], out, sem)
    copy.start()
    copy.wait()


def first_tile(t, srow, sources, hc_ref, out, usum, a_buf, r_buf, ready):
    s = slot_rows(srow)

    def step(p_ref, skip, g, cols):
        cols = list(cols)
        us = [[], []]
        r0 = pl.multiple_of(g * 16, 16)
        a = [a_buf[pl.ds(pl.multiple_of(t * 512 + r0 + 8 * h, 8), 8), :] for h in range(2)]
        for cb in range(SR):
            lanes = pl.ds(cb * L, L)
            c16 = hc_ref[t, pl.ds(r0, 16), lanes].astype(jnp.float32)
            for h in range(2):
                p = p_ref[pl.ds(pl.multiple_of(r0 + 8 * h - skip, 8), 8), lanes]
                hc = c16[8 * h : 8 * h + 8]
                u = jnp.minimum(jnp.maximum(((p - hc) - a[h]) - s[cb], 0.0), 1.0)
                out[t, pl.ds(pl.multiple_of(r0 + 8 * h, 8), 8), lanes] = u - hc
                us[h].append(u)
                cols[cb] = cols[cb] + u
        for h in range(2):
            r_buf[pl.ds(pl.multiple_of(t * 512 + r0 + 8 * h, 8), 8), :] = tree(us[h])
        return tuple(cols)

    cols = ZEROS()
    for b in range(NRB):
        ready(t, b)
        cols = lax.fori_loop(b * 8, (b + 1) * 8, functools.partial(step, *sources[b]), cols, unroll=2)
    write_cols(t, usum, cols)


def first_kernel(own_ids, rec, mine, other, bias, psum, hc_ref, head, rest, p_hbm, out, usum, msg, ids, p_ref, a_buf, r_buf, id_buf, p_sems, sem):
    def fetch(b):
        rows = pl.ds(b * RB, RB)
        return pltpu.make_async_copy(p_hbm.at[1, rows, :], p_ref.at[rows, :], p_sems.at[b])

    def ready(t, b):
        if t == 1:
            fetch(b).wait()

    for b in range(NRB):
        fetch(b).start()
    core = lax.axis_index("tiles") & 1
    id_buf[0:4, :] = mine[TS : TS + 4, :].astype(jnp.int32)
    id_buf[4:8, :] = other[TS : TS + 4, :].astype(jnp.int32)
    keep_ids = pltpu.make_async_copy(id_buf, ids, sem)
    keep_ids.start()
    slots = []
    for t in range(2):
        a, s = own_ids[t], own_ids[2 + t]
        arow = jnp.where((a & 1) == core, rows_of(rec, a, False), other[AR * t : AR * (t + 1), :])
        spread_half(arow, a_buf.at[pl.ds(t * 512, 512), :])
        slots.append(jnp.where((s & 1) == core, rows_of(rec, s, True), other[8 + SR * t : 8 + SR * (t + 1), :]))
    for t in range(2):
        sources = [(p_ref, 0) if t else (head, 0) if b * RB < HEAD else (rest, HEAD) for b in range(NRB)]
        first_tile(t, slots[t], sources, hc_ref, out, usum, a_buf, r_buf, ready)
    write_rows(usum, r_buf)
    data = jnp.concatenate([2.0 * usum[...] - psum[...], bias[...]], axis=0)
    for j in range(LINE):
        msg[j * MSG : (j + 1) * MSG, :] = data
    keep_ids.wait()


def write_flags(own_ids, mine, other, flags):
    me = lax.axis_index("tiles")
    core = me & 1
    lane = lax.broadcasted_iota(jnp.int32, (4, L), 1)
    row = lax.broadcasted_iota(jnp.int32, (4, L), 0)
    place = lane * 4 + jnp.where(row < 2, core, 1 - core) * 2 + (row & 1)

    def found(where):
        return jnp.max(jnp.where(where & (lane < CHIPS), 1, 0))

    for kind in range(2):
        rows = pl.ds(TS + 2 * kind, 2)
        ids = jnp.concatenate([mine[rows, :], other[rows, :]], axis=0).astype(jnp.int32)
        for k in range(2):
            i = own_ids[2 * kind + k]
            earlier = found((ids == i) & (place < me * 2 + k))
            flags[2 * kind + k] = jnp.where((i >= 0) & (earlier == 0), 1, 0)
        flags[4 + kind] = 1 - found(ids == me)


def users_kernel(own_ids, ids, mine, other, rec, out, flags, acc_a0, acc_a1, acc_s0, acc_s1):
    write_flags(own_ids, mine, other, flags)
    me = lax.axis_index("tiles")
    chip = me >> 1
    core = me & 1
    x = chip >> 4
    line = chip & 15

    def at(i):
        return pl.multiple_of(jnp.where(i < 0, BLOCKS, i) * 8, 8)

    wanted = []
    for j in range(PLANE):
        there = (x << 4) | j
        o = j * TS
        adv = [(ids[k, there], o + AR * k) for k in range(2)]
        slot = [(ids[2 + k, there], o + 8 + SR * k) for k in range(2)]
        wanted.append((adv, slot))
    zero = jnp.zeros((8, L), jnp.float32)
    for adv, slot in wanted:
        for i, _ in adv:
            acc_a0[pl.ds(at(i), 8), :] = zero
            acc_a1[pl.ds(at(i), 8), :] = zero
        for i, _ in slot:
            acc_s0[pl.ds(at(i), 8), :] = zero
            acc_s1[pl.ds(at(i), 8), :] = zero
    for j in range(LINE):
        source = ((j >> 1) << 4) | line
        side = 4 * ((j & 1) ^ core)
        o = j * MSG
        for k, acc in ((0, acc_a0), (1, acc_a1)):
            rows = pl.ds(at(ids[side + k, source]), AR)
            acc[rows, :] = acc[rows, :] + rec[o + AR * k : o + AR * (k + 1), :]
        for k, acc in ((0, acc_s0), (1, acc_s1)):
            rows = pl.ds(at(ids[side + 2 + k, source]), SR)
            acc[rows, :] = acc[rows, :] + rec[o + 8 + SR * k : o + 8 + SR * (k + 1), :]

    def bias(i, o, n):
        b = jnp.maximum(i, 0)
        here = ((b >> 1) & 15) == line
        return rec[pl.ds(((b >> 5) * 2 + (b & 1)) * MSG + o, n), :] * jnp.where(here, 1.0, 0.0)

    for adv, slot in wanted:
        for i, o in adv:
            rows = pl.ds(at(i), AR)
            out[o : o + AR, :] = (acc_a0[rows, :] + acc_a1[rows, :]) + bias(i, TS + SR, AR)
        for i, o in slot:
            rows = pl.ds(at(i), SR)
            out[o : o + SR, :] = (acc_s0[rows, :] + acc_s1[rows, :]) + bias(i, TS, SR)


def second_tile(t, srow, base, outs, usum, a_buf, r_buf, done):
    s = slot_rows(srow)

    def step(out, skip, g, cols):
        rows = pl.ds(pl.multiple_of(g * 8, 8), 8)
        wide = pl.ds(pl.multiple_of(t * 512 + g * 8, 8), 8)
        a = a_buf[wide, :]
        cols = list(cols)
        us = []
        for cb in range(SR):
            lanes = pl.ds(cb * L, L)
            u = jnp.minimum(jnp.maximum((base[t, rows, lanes] - a) - s[cb], 0.0), 1.0)
            out[pl.ds(pl.multiple_of(g * 8 - skip, 8), 8), lanes] = u
            cols[cb] = cols[cb] + u
            us.append(u)
        r_buf[wide, :] = tree(us)
        return tuple(cols)

    cols = ZEROS()
    for b in range(NRB):
        cols = lax.fori_loop(b * 16, (b + 1) * 16, functools.partial(step, *outs[b]), cols, unroll=4)
        done(t, b)
    write_cols(t, usum, cols)


def second_kernel(flags, rec, base, psum, primal, sums, tail, out, usum, a_buf, r_buf, sems):
    early = 1024 - TAIL

    def keep(t, b):
        n = t * NRB + b
        return pltpu.make_async_copy(out.at[pl.ds(n * RB, RB), :], primal.at[t, pl.ds(b * RB, RB), :], sems.at[n])

    def done(t, b):
        if (t * NRB + b) * RB < early:
            keep(t, b).start()

    total = jnp.maximum(tree([rec[j * TS : (j + 1) * TS, :] for j in range(PLANE)]), 0.0)
    adv = total[0:8] * (1.0 / 1024)
    slot = total[8:24] * (1.0 / 512)
    spread_half(adv, a_buf)
    for t in range(2):
        outs = [(out, -t * 512) if t * 512 + b * RB < early else (tail, early - t * 512) for b in range(NRB)]
        second_tile(t, slot[8 * t : 8 * t + 8], base, outs, usum, a_buf, r_buf, done)
    write_rows(usum, r_buf)
    for k, (o, n) in enumerate(((0, AR), (AR, AR), (8, SR), (8 + SR, SR))):
        rows = pl.ds(o, n)
        named = total[o : o + n] * jnp.where(flags[k] > 0, 1.0, 0.0)
        sums[rows, :] = named + (2.0 * usum[rows, :] - psum[rows, :])
    for n in range(early // RB):
        keep(*divmod(n, NRB)).wait()


def store_kernel(tail, _, primal, sem):
    copy = pltpu.make_async_copy(tail, primal.at[1, pl.ds(512 - TAIL, TAIL), :], sem)
    copy.start()
    copy.wait()


def owners_kernel(ids, mine, other, _, out):

    me = lax.axis_index("tiles")
    chip = me >> 1
    core = me & 1
    out[...] = jnp.zeros_like(out)
    for side, rec in ((0, mine), (4, other)):
        for k in range(2):
            for i, o, n, src in (
                (ids[side + k, chip], SR, AR, AR * k),
                (ids[side + 2 + k, chip], 0, SR, 8 + SR * k),
            ):

                @pl.when((i >= 0) & ((i & 1) == core))
                def _():
                    rows = pl.ds((i >> 1) * OUT + o, n)
                    out[rows, :] = out[rows, :] + rec[src : src + n, :]


def last_kernel(flags, rec, bias, bounds, adv_out, slot_out):
    n = 2 * OUT
    total = tree([rec[g * n : (g + 1) * n, :] for g in range(CHIPS // 2)])
    total = total[0:OUT] + total[OUT:n]
    unnamed = jnp.maximum(bias[...], 0.0)
    slot = total[0:SR] + unnamed[0:SR] * jnp.where(flags[5] > 0, 1.0, 0.0)
    adv = total[SR:OUT] + unnamed[SR:OUT] * jnp.where(flags[4] > 0, 1.0, 0.0)
    slot_out[...] = jnp.maximum((slot - bounds[0:SR, :]) * (1.0 / 512), 0.0)
    adv_out[...] = jnp.maximum((adv - bounds[SR:OUT, :]) * (1.0 / 1024), 0.0)


def f32(*shape):
    return jax.ShapeDtypeStruct(shape, jnp.float32)


def vmem(*shape):
    return pltpu.VMEM(shape, jnp.float32)


def in_vmem(x):
    return pltpu.with_memory_space_constraint(x, pltpu.VMEM)


def in_smem(x):
    return pltpu.with_memory_space_constraint(x, pltpu.SMEM)


def call(kernel, name, ins, outs, scratch=(), mib=4, aliases={}):
    return pl.pallas_call(
        kernel,
        in_specs=[s for _, s in ins],
        out_specs=[s for _, s in outs],
        out_shape=[o for o, _ in outs],
        scratch_shapes=list(scratch),
        compiler_params=pltpu.CompilerParams(vmem_limit_bytes=mib << 20),
        input_output_aliases=aliases,
        name=name,
    )(*[x for x, _ in ins])


def in_hbm(x):
    return pltpu.with_memory_space_constraint(x, pltpu.HBM)


def hbm_arg(x):
    return (in_hbm(x), pl.BlockSpec(memory_space=pl.ANY))


def smem_out(*shape):
    return (pltpu.SMEM(shape, jnp.int32), IN_SMEM)


def smem_arg(x):
    return (in_smem(x), IN_SMEM)


def vmem_arg(x):
    return (in_vmem(x), IN_VMEM)


def vmem_out(*shape):
    return (vmem(*shape), IN_VMEM)


def exchange(x, groups, rows):
    n = len(groups[0])
    x = lax.all_to_all(x.reshape(n, rows * L), "tiles", 0, 0, axis_index_groups=groups, tiled=True)
    return vmem_arg(x.reshape(n * rows, L))


def swap(x):
    return lax.ppermute(x, "tiles", PARTNERS)


def body(primal_start, cost, mask, tile_adv, tile_slot, adv_dual, slot_dual, spend_limit, capacity):
    tile = (2, 512, 1024)
    message, bias, bounds, row_ids, own_ids = call(
        own_kernel,
        "own",
        [(in_hbm(tile_adv), IN_SMEM), (in_hbm(tile_slot), IN_SMEM)]
        + [(in_hbm(x.reshape(-1, L)), IN_VMEM) for x in (adv_dual, slot_dual, spend_limit, capacity)],
        [vmem_out(CHIPS * OWN, L), vmem_out(OUT, L), vmem_out(OUT, L)]
        + [(pltpu.VMEM((8, L), jnp.int32), IN_VMEM), smem_out(4)],
    )
    table = exchange(message, CORE_GROUPS, OWN)
    hc, psum, head = call(
        prepare_kernel,
        "prepare",
        [smem_arg(own_ids), (in_hbm(mask.transpose(0, 2, 1)), IN_SMEM), hbm_arg(primal_start), hbm_arg(cost)],
        [(pltpu.VMEM(tile, jnp.bfloat16), IN_VMEM), vmem_out(TS, L), vmem_out(HEAD, 1024)],
        [vmem(1024 - HEAD, 1024), pltpu.VMEM(tile, jnp.bfloat16), vmem(512, L)] + [pltpu.SemaphoreType.DMA((2 * NRB,))] * 2,
        8,
    )
    (picked,) = call(pick_kernel, "pick", [vmem_arg(swap(row_ids)), table, vmem_arg(psum)], [vmem_out(SEL, L)])
    other = swap(picked)
    (rest,) = call(
        load_kernel,
        "load",
        [hbm_arg(primal_start), vmem_arg(picked)],
        [vmem_out(512 - HEAD, 1024)],
        [pltpu.SemaphoreType.DMA(())],
    )
    base, usum, message, ids = call(
        first_kernel,
        "first",
        [smem_arg(own_ids), table, vmem_arg(picked), vmem_arg(other), vmem_arg(bias), vmem_arg(psum), vmem_arg(hc)]
        + [vmem_arg(head), vmem_arg(rest), hbm_arg(primal_start)],
        [vmem_out(*tile), vmem_out(TS, L), vmem_out(LINE * MSG, L), smem_out(8, L)],
        [vmem(512, 1024), vmem(1024, L), vmem(1024, L), pltpu.VMEM((8, L), jnp.int32)]
        + [pltpu.SemaphoreType.DMA((NRB,)), pltpu.SemaphoreType.DMA(())],
        8,
    )
    part = exchange(message, LINE_GROUPS, MSG)
    message, flags = call(
        users_kernel,
        "users",
        [smem_arg(own_ids), smem_arg(ids), vmem_arg(picked), vmem_arg(other), part],
        [vmem_out(PLANE * TS, L), smem_out(6)],
        [vmem((BLOCKS + 1) * 8, L)] * 4,
    )
    primal, sums, tail = call(
        second_kernel,
        "second",
        [smem_arg(flags), exchange(message, PLANE_GROUPS, TS), vmem_arg(base), vmem_arg(usum)],
        [(f32(*tile), pl.BlockSpec(memory_space=pl.ANY))] + [vmem_out(TS, L), vmem_out(TAIL, 1024)],
        [vmem(1024 - TAIL, 1024), vmem(TS, L), vmem(1024, L), vmem(1024, L)]
        + [pltpu.SemaphoreType.DMA((2 * NRB - TAIL // RB,))],
        8,
    )
    (primal,) = call(
        store_kernel,
        "store",
        [vmem_arg(tail), hbm_arg(primal)],
        [(f32(*tile), pl.BlockSpec(memory_space=pl.ANY))],
        [pltpu.SemaphoreType.DMA(())],
        aliases={1: 0},
    )
    (message,) = call(
        owners_kernel,
        "owners",
        [smem_arg(ids), vmem_arg(sums), vmem_arg(swap(sums)), hbm_arg(primal)],
        [vmem_out(CHIPS * OUT, L)],
    )
    adv_out, slot_out = call(
        last_kernel,
        "last",
        [smem_arg(flags), exchange(message, CORE_GROUPS, OUT), vmem_arg(bias), vmem_arg(bounds)],
        [(f32(AR, L), IN_VMEM), (f32(SR, L), IN_VMEM)],
    )
    return primal, adv_out.reshape(1, 512), slot_out.reshape(1, 1024)


def solution(mesh):
    return jax.shard_map(
        body,
        mesh=mesh,
        in_specs=(
            P("tiles", None, None),
            P("tiles", None, None),
            P("tiles", None, None),
            P("tiles"),
            P("tiles"),
            P("tiles", None),
            P("tiles", None),
            P("tiles", None),
            P("tiles", None),
        ),
        out_specs=(P("tiles", None, None), P("tiles", None), P("tiles", None)),
        check_vma=False,
    )
```

```python
import functools

import jax
import jax.numpy as jnp
from jax import lax
from jax.experimental import pallas as pl
from jax.experimental.pallas import tpu as pltpu
from jax.sharding import Mesh
from jax.sharding import PartitionSpec as P

CHIPS = 64
BLOCKS = 128
L = 128
AR = 4
SR = 8
OWN = AR + SR + 1
SEL = 2 * (AR + SR) + 8
TS = 2 * (AR + SR)
MSG = TS + SR + AR
OUT = SR + AR
RB = 128
NRB = 4
BIG = 1e30
HEAD = 128
TAIL = 256

PLANE = 16
AXES = ("x", "z", "y", "core")
LINE = 8
LINE_GROUPS = [[(x * PLANE + j) * 2 + c for x in range(4) for c in range(2)] for j in range(PLANE)]
PARTNERS = [(i, i ^ 1) for i in range(2 * CHIPS)]


IN_VMEM = pl.BlockSpec(memory_space=pltpu.VMEM)
IN_SMEM = pl.BlockSpec(memory_space=pltpu.SMEM)


def device():
    x, z, y, core = (lax.axis_index(a) for a in AXES)
    return ((x * 4 + z) * 4 + y) * 2 + core


def own_kernel(adv_id, slot_id, adv, slot, limit, cap, out, bias, bounds, row_ids, ids):
    lane = lax.broadcasted_iota(jnp.int32, (8, L), 1)
    row = jnp.zeros((8, L), jnp.int32)
    for k, v in enumerate((adv_id[0], adv_id[1], slot_id[0], slot_id[1])):
        row = jnp.where(lane == k, v, row)
        ids[k] = v
    row_ids[...] = row
    data = jnp.concatenate([slot[...], adv[...], row[0:1].astype(jnp.float32)], axis=0)
    for j in range(CHIPS):
        out[j * OWN : (j + 1) * OWN, :] = data
    bias[0:SR, :] = slot[...] * 512.0 - cap[...]
    bias[SR:OUT, :] = adv[...] * 1024.0 - limit[...]
    bounds[0:SR, :] = cap[...]
    bounds[SR:OUT, :] = limit[...]


def rows_of(rec, i, slot):
    at = (jnp.maximum(i, 0) >> 1) * OWN
    return rec[pl.ds(at, SR), :] if slot else rec[pl.ds(at + SR, AR), :]


def pick_kernel(partner_ids, rec, _, out):

    lane = lax.broadcasted_iota(jnp.int32, (1, L), 1)
    row = partner_ids[0:1, :]
    wanted = [jnp.max(jnp.where(lane == k, row, -1)) for k in range(4)]
    for k in range(2):
        out[AR * k : AR * (k + 1), :] = rows_of(rec, wanted[k], False)
        out[8 + SR * k : 8 + SR * (k + 1), :] = rows_of(rec, wanted[2 + k], True)
    ids = rec[pl.ds(OWN - 1, CHIPS, stride=OWN), :]
    out[TS:SEL, :] = jnp.concatenate([ids, ids], axis=0).T[0:8, :]


def spread_half(rows, buf):
    for b in range(rows.shape[0]):
        block = jnp.broadcast_to(0.5 * rows[b : b + 1, :], (L, L))
        buf[b * L : (b + 1) * L, :] = block.T


def tree(xs):
    while len(xs) > 1:
        xs = [xs[i] + xs[i + 1] for i in range(0, len(xs), 2)]
    return xs[0]


def write_rows(sums, r_buf, tiles=(0, 1)):
    for n in range(len(tiles) * NRB):
        o = tiles[0] * AR + n
        sums[o : o + 1, :] = jnp.sum(r_buf[n * L : (n + 1) * L, :].T, axis=0, keepdims=True)


def write_cols(t, sums, cols):
    rows = [jnp.sum(c, axis=0, keepdims=True) for c in cols]
    sums[8 + t * SR : 8 + (t + 1) * SR, :] = jnp.concatenate(rows, axis=0)


def slot_rows(srow):
    return [jnp.broadcast_to(0.5 * srow[cb : cb + 1, :], (8, L)) for cb in range(SR)]


ZEROS = lambda: (jnp.zeros((8, L), jnp.float32),) * SR


def prepare_kernel(own_ids, mask, p_hbm, c_hbm, hc, psum, head, p_rest, c_ref, r_buf, p_sems, c_sems):
    def place(t, b):
        n = (t * NRB + b) * RB
        return (head, -t * 512) if n < HEAD else (p_rest, HEAD - t * 512)

    def fetch(t, b):
        rows = pl.ds(b * RB, RB)
        n = t * NRB + b
        p_ref, skip = place(t, b)
        return (
            pltpu.make_async_copy(p_hbm.at[t, rows, :], p_ref.at[pl.ds(b * RB - skip, RB), :], p_sems.at[n]),
            pltpu.make_async_copy(c_hbm.at[t, rows, :], c_ref.at[t, rows, :], c_sems.at[n]),
        )

    for t in range(2):
        for b in range(NRB):
            for copy in fetch(t, b):
                copy.start()
    for t in range(2):
        alive = jnp.where(own_ids[t] >= 0, 1, 0)

        def step(p_ref, skip, g, cols):
            r0 = pl.multiple_of(g * 16, 16)
            cols = list(cols)
            ps = [[], []]
            for cb in range(SR):
                lanes = pl.ds(cb * L, L)
                c16 = 0.5 * c_ref[t, pl.ds(r0, 16), lanes].astype(jnp.float32)
                halves = []
                for h in range(2):
                    here = jnp.full((8, L), mask[t, cb, g * 2 + h] * alive, jnp.int32) > 0
                    rows = pl.ds(pl.multiple_of(r0 + 8 * h - skip, 8), 8)
                    p = jnp.where(here, p_ref[rows, lanes], 0.0)
                    halves.append(jnp.where(here, c16[8 * h : 8 * h + 8], BIG))
                    ps[h].append(p)
                    cols[cb] = cols[cb] + p
                hc[t, pl.ds(r0, 16), lanes] = jnp.concatenate(halves, axis=0).astype(jnp.bfloat16)
            for h in range(2):
                r_buf[pl.ds(pl.multiple_of(r0 + 8 * h, 8), 8), :] = tree(ps[h])
            return tuple(cols)

        cols = ZEROS()
        for b in range(NRB):
            for copy in fetch(t, b):
                copy.wait()
            cols = lax.fori_loop(b * 8, (b + 1) * 8, functools.partial(step, *place(t, b)), cols)
        write_rows(psum, r_buf, (t,))
        write_cols(t, psum, cols)


def load_kernel(p_hbm, _, out, sem):
    copy = pltpu.make_async_copy(p_hbm.at[0, pl.ds(HEAD, 512 - HEAD), :], out, sem)
    copy.start()
    copy.wait()


def first_tile(t, srow, sources, hc_ref, out, usum, a_buf, r_buf, ready):
    s = slot_rows(srow)

    def step(p_ref, skip, g, cols):
        cols = list(cols)
        us = [[], []]
        r0 = pl.multiple_of(g * 16, 16)
        a = [a_buf[pl.ds(pl.multiple_of(t * 512 + r0 + 8 * h, 8), 8), :] for h in range(2)]
        for cb in range(SR):
            lanes = pl.ds(cb * L, L)
            c16 = hc_ref[t, pl.ds(r0, 16), lanes].astype(jnp.float32)
            for h in range(2):
                p = p_ref[pl.ds(pl.multiple_of(r0 + 8 * h - skip, 8), 8), lanes]
                hc = c16[8 * h : 8 * h + 8]
                u = jnp.minimum(jnp.maximum(((p - hc) - a[h]) - s[cb], 0.0), 1.0)
                out[t, pl.ds(pl.multiple_of(r0 + 8 * h, 8), 8), lanes] = u - hc
                us[h].append(u)
                cols[cb] = cols[cb] + u
        for h in range(2):
            r_buf[pl.ds(pl.multiple_of(t * 512 + r0 + 8 * h, 8), 8), :] = tree(us[h])
        return tuple(cols)

    cols = ZEROS()
    for b in range(NRB):
        ready(t, b)
        cols = lax.fori_loop(b * 8, (b + 1) * 8, functools.partial(step, *sources[b]), cols, unroll=2)
    write_cols(t, usum, cols)


def first_kernel(own_ids, rec, mine, other, bias, psum, hc_ref, head, rest, p_hbm, out, usum, msg, ids, p_ref, a_buf, r_buf, id_buf, p_sems, sem):
    def fetch(b):
        rows = pl.ds(b * RB, RB)
        return pltpu.make_async_copy(p_hbm.at[1, rows, :], p_ref.at[rows, :], p_sems.at[b])

    def ready(t, b):
        if t == 1:
            fetch(b).wait()

    for b in range(NRB):
        fetch(b).start()
    core = lax.axis_index("core")
    id_buf[0:4, :] = mine[TS : TS + 4, :].astype(jnp.int32)
    id_buf[4:8, :] = other[TS : TS + 4, :].astype(jnp.int32)
    keep_ids = pltpu.make_async_copy(id_buf, ids, sem)
    keep_ids.start()
    slots = []
    for t in range(2):
        a, s = own_ids[t], own_ids[2 + t]
        arow = jnp.where((a & 1) == core, rows_of(rec, a, False), other[AR * t : AR * (t + 1), :])
        spread_half(arow, a_buf.at[pl.ds(t * 512, 512), :])
        slots.append(jnp.where((s & 1) == core, rows_of(rec, s, True), other[8 + SR * t : 8 + SR * (t + 1), :]))
    for t in range(2):
        sources = [(p_ref, 0) if t else (head, 0) if b * RB < HEAD else (rest, HEAD) for b in range(NRB)]
        first_tile(t, slots[t], sources, hc_ref, out, usum, a_buf, r_buf, ready)
    write_rows(usum, r_buf)
    data = jnp.concatenate([2.0 * usum[...] - psum[...], bias[...]], axis=0)
    for j in range(LINE):
        msg[j * MSG : (j + 1) * MSG, :] = data
    keep_ids.wait()


def write_flags(own_ids, mine, other, flags):
    me = device()
    core = me & 1
    lane = lax.broadcasted_iota(jnp.int32, (4, L), 1)
    row = lax.broadcasted_iota(jnp.int32, (4, L), 0)
    place = lane * 4 + jnp.where(row < 2, core, 1 - core) * 2 + (row & 1)

    def found(where):
        return jnp.max(jnp.where(where & (lane < CHIPS), 1, 0))

    for kind in range(2):
        rows = pl.ds(TS + 2 * kind, 2)
        ids = jnp.concatenate([mine[rows, :], other[rows, :]], axis=0).astype(jnp.int32)
        for k in range(2):
            i = own_ids[2 * kind + k]
            earlier = found((ids == i) & (place < me * 2 + k))
            flags[2 * kind + k] = jnp.where((i >= 0) & (earlier == 0), 1, 0)
        flags[4 + kind] = 1 - found(ids == me)


def users_kernel(own_ids, ids, mine, other, rec, out, flags, acc_a0, acc_a1, acc_s0, acc_s1):
    write_flags(own_ids, mine, other, flags)
    me = device()
    chip = me >> 1
    core = me & 1
    x = chip >> 4
    line = chip & 15

    def at(i):
        return pl.multiple_of(jnp.where(i < 0, BLOCKS, i) * 8, 8)

    wanted = []
    for j in range(PLANE):
        there = (x << 4) | j
        o = j * TS
        adv = [(ids[k, there], o + AR * k) for k in range(2)]
        slot = [(ids[2 + k, there], o + 8 + SR * k) for k in range(2)]
        wanted.append((adv, slot))
    zero = jnp.zeros((8, L), jnp.float32)
    for adv, slot in wanted:
        for i, _ in adv:
            acc_a0[pl.ds(at(i), 8), :] = zero
            acc_a1[pl.ds(at(i), 8), :] = zero
        for i, _ in slot:
            acc_s0[pl.ds(at(i), 8), :] = zero
            acc_s1[pl.ds(at(i), 8), :] = zero
    for j in range(LINE):
        source = ((j >> 1) << 4) | line
        side = 4 * ((j & 1) ^ core)
        o = j * MSG
        for k, acc in ((0, acc_a0), (1, acc_a1)):
            rows = pl.ds(at(ids[side + k, source]), AR)
            acc[rows, :] = acc[rows, :] + rec[o + AR * k : o + AR * (k + 1), :]
        for k, acc in ((0, acc_s0), (1, acc_s1)):
            rows = pl.ds(at(ids[side + 2 + k, source]), SR)
            acc[rows, :] = acc[rows, :] + rec[o + 8 + SR * k : o + 8 + SR * (k + 1), :]

    def bias(i, o, n):
        b = jnp.maximum(i, 0)
        here = ((b >> 1) & 15) == line
        return rec[pl.ds(((b >> 5) * 2 + (b & 1)) * MSG + o, n), :] * jnp.where(here, 1.0, 0.0)

    for adv, slot in wanted:
        for i, o in adv:
            rows = pl.ds(at(i), AR)
            out[o : o + AR, :] = (acc_a0[rows, :] + acc_a1[rows, :]) + bias(i, TS + SR, AR)
        for i, o in slot:
            rows = pl.ds(at(i), SR)
            out[o : o + SR, :] = (acc_s0[rows, :] + acc_s1[rows, :]) + bias(i, TS, SR)


def second_tile(t, srow, base, outs, usum, a_buf, r_buf, done):
    s = slot_rows(srow)

    def step(out, skip, g, cols):
        rows = pl.ds(pl.multiple_of(g * 8, 8), 8)
        wide = pl.ds(pl.multiple_of(t * 512 + g * 8, 8), 8)
        a = a_buf[wide, :]
        cols = list(cols)
        us = []
        for cb in range(SR):
            lanes = pl.ds(cb * L, L)
            u = jnp.minimum(jnp.maximum((base[t, rows, lanes] - a) - s[cb], 0.0), 1.0)
            out[pl.ds(pl.multiple_of(g * 8 - skip, 8), 8), lanes] = u
            cols[cb] = cols[cb] + u
            us.append(u)
        r_buf[wide, :] = tree(us)
        return tuple(cols)

    cols = ZEROS()
    for b in range(NRB):
        cols = lax.fori_loop(b * 16, (b + 1) * 16, functools.partial(step, *outs[b]), cols, unroll=4)
        done(t, b)
    write_cols(t, usum, cols)


def second_kernel(flags, rec, base, psum, primal, sums, tail, out, usum, a_buf, r_buf, sems):
    early = 1024 - TAIL

    def keep(t, b):
        n = t * NRB + b
        return pltpu.make_async_copy(out.at[pl.ds(n * RB, RB), :], primal.at[t, pl.ds(b * RB, RB), :], sems.at[n])

    def done(t, b):
        if (t * NRB + b) * RB < early:
            keep(t, b).start()

    total = jnp.maximum(tree([rec[j * TS : (j + 1) * TS, :] for j in range(PLANE)]), 0.0)
    adv = total[0:8] * (1.0 / 1024)
    slot = total[8:24] * (1.0 / 512)
    spread_half(adv, a_buf)
    for t in range(2):
        outs = [(out, -t * 512) if t * 512 + b * RB < early else (tail, early - t * 512) for b in range(NRB)]
        second_tile(t, slot[8 * t : 8 * t + 8], base, outs, usum, a_buf, r_buf, done)
    write_rows(usum, r_buf)
    for k, (o, n) in enumerate(((0, AR), (AR, AR), (8, SR), (8 + SR, SR))):
        rows = pl.ds(o, n)
        named = total[o : o + n] * jnp.where(flags[k] > 0, 1.0, 0.0)
        sums[rows, :] = named + (2.0 * usum[rows, :] - psum[rows, :])
    for n in range(early // RB):
        keep(*divmod(n, NRB)).wait()


def store_kernel(tail, _, primal, sem):
    copy = pltpu.make_async_copy(tail, primal.at[1, pl.ds(512 - TAIL, TAIL), :], sem)
    copy.start()
    copy.wait()


def owners_kernel(ids, mine, other, _, out):

    me = device()
    chip = me >> 1
    core = me & 1
    out[...] = jnp.zeros_like(out)
    for side, rec in ((0, mine), (4, other)):
        for k in range(2):
            for i, o, n, src in (
                (ids[side + k, chip], SR, AR, AR * k),
                (ids[side + 2 + k, chip], 0, SR, 8 + SR * k),
            ):

                @pl.when((i >= 0) & ((i & 1) == core))
                def _():
                    rows = pl.ds((i >> 1) * OUT + o, n)
                    out[rows, :] = out[rows, :] + rec[src : src + n, :]


def last_kernel(flags, rec, bias, bounds, adv_out, slot_out):
    n = 2 * OUT
    total = tree([rec[g * n : (g + 1) * n, :] for g in range(CHIPS // 2)])
    total = total[0:OUT] + total[OUT:n]
    unnamed = jnp.maximum(bias[...], 0.0)
    slot = total[0:SR] + unnamed[0:SR] * jnp.where(flags[5] > 0, 1.0, 0.0)
    adv = total[SR:OUT] + unnamed[SR:OUT] * jnp.where(flags[4] > 0, 1.0, 0.0)
    slot_out[...] = jnp.maximum((slot - bounds[0:SR, :]) * (1.0 / 512), 0.0)
    adv_out[...] = jnp.maximum((adv - bounds[SR:OUT, :]) * (1.0 / 1024), 0.0)


def f32(*shape):
    return jax.ShapeDtypeStruct(shape, jnp.float32)


def vmem(*shape):
    return pltpu.VMEM(shape, jnp.float32)


def in_vmem(x):
    return pltpu.with_memory_space_constraint(x, pltpu.VMEM)


def in_smem(x):
    return pltpu.with_memory_space_constraint(x, pltpu.SMEM)


def call(kernel, name, ins, outs, scratch=(), mib=4, aliases={}):
    return pl.pallas_call(
        kernel,
        in_specs=[s for _, s in ins],
        out_specs=[s for _, s in outs],
        out_shape=[o for o, _ in outs],
        scratch_shapes=list(scratch),
        compiler_params=pltpu.CompilerParams(vmem_limit_bytes=mib << 20),
        input_output_aliases=aliases,
        name=name,
    )(*[x for x, _ in ins])


def in_hbm(x):
    return pltpu.with_memory_space_constraint(x, pltpu.HBM)


def hbm_arg(x):
    return (in_hbm(x), pl.BlockSpec(memory_space=pl.ANY))


def smem_out(*shape):
    return (pltpu.SMEM(shape, jnp.int32), IN_SMEM)


def smem_arg(x):
    return (in_smem(x), IN_SMEM)


def vmem_arg(x):
    return (in_vmem(x), IN_VMEM)


def vmem_out(*shape):
    return (vmem(*shape), IN_VMEM)


def exchange(x, axes, rows, groups=None):
    n = x.shape[0] // rows
    x = lax.all_to_all(x.reshape(n, rows * L), axes, 0, 0, axis_index_groups=groups, tiled=True)
    return vmem_arg(x.reshape(n * rows, L))


def swap(x):
    return lax.ppermute(x, AXES, PARTNERS)


def body(primal_start, cost, mask, tile_adv, tile_slot, adv_dual, slot_dual, spend_limit, capacity):
    tile = (2, 512, 1024)
    message, bias, bounds, row_ids, own_ids = call(
        own_kernel,
        "own",
        [(in_hbm(tile_adv), IN_SMEM), (in_hbm(tile_slot), IN_SMEM)]
        + [(in_hbm(x.reshape(-1, L)), IN_VMEM) for x in (adv_dual, slot_dual, spend_limit, capacity)],
        [vmem_out(CHIPS * OWN, L), vmem_out(OUT, L), vmem_out(OUT, L)]
        + [(pltpu.VMEM((8, L), jnp.int32), IN_VMEM), smem_out(4)],
    )
    table = exchange(message, AXES[:3], OWN)
    hc, psum, head = call(
        prepare_kernel,
        "prepare",
        [smem_arg(own_ids), (in_hbm(mask.transpose(0, 2, 1)), IN_SMEM), hbm_arg(primal_start), hbm_arg(cost)],
        [(pltpu.VMEM(tile, jnp.bfloat16), IN_VMEM), vmem_out(TS, L), vmem_out(HEAD, 1024)],
        [vmem(1024 - HEAD, 1024), pltpu.VMEM(tile, jnp.bfloat16), vmem(512, L)] + [pltpu.SemaphoreType.DMA((2 * NRB,))] * 2,
        8,
    )
    (picked,) = call(pick_kernel, "pick", [vmem_arg(swap(row_ids)), table, vmem_arg(psum)], [vmem_out(SEL, L)])
    other = swap(picked)
    (rest,) = call(
        load_kernel,
        "load",
        [hbm_arg(primal_start), vmem_arg(picked)],
        [vmem_out(512 - HEAD, 1024)],
        [pltpu.SemaphoreType.DMA(())],
    )
    base, usum, message, ids = call(
        first_kernel,
        "first",
        [smem_arg(own_ids), table, vmem_arg(picked), vmem_arg(other), vmem_arg(bias), vmem_arg(psum), vmem_arg(hc)]
        + [vmem_arg(head), vmem_arg(rest), hbm_arg(primal_start)],
        [vmem_out(*tile), vmem_out(TS, L), vmem_out(LINE * MSG, L), smem_out(8, L)],
        [vmem(512, 1024), vmem(1024, L), vmem(1024, L), pltpu.VMEM((8, L), jnp.int32)]
        + [pltpu.SemaphoreType.DMA((NRB,)), pltpu.SemaphoreType.DMA(())],
        8,
    )
    part = exchange(message, AXES, MSG, LINE_GROUPS)
    message, flags = call(
        users_kernel,
        "users",
        [smem_arg(own_ids), smem_arg(ids), vmem_arg(picked), vmem_arg(other), part],
        [vmem_out(PLANE * TS, L), smem_out(6)],
        [vmem((BLOCKS + 1) * 8, L)] * 4,
    )
    primal, sums, tail = call(
        second_kernel,
        "second",
        [smem_arg(flags), exchange(message, AXES[1:3], TS), vmem_arg(base), vmem_arg(usum)],
        [(f32(*tile), pl.BlockSpec(memory_space=pl.ANY))] + [vmem_out(TS, L), vmem_out(TAIL, 1024)],
        [vmem(1024 - TAIL, 1024), vmem(TS, L), vmem(1024, L), vmem(1024, L)]
        + [pltpu.SemaphoreType.DMA((2 * NRB - TAIL // RB,))],
        8,
    )
    (primal,) = call(
        store_kernel,
        "store",
        [vmem_arg(tail), hbm_arg(primal)],
        [(f32(*tile), pl.BlockSpec(memory_space=pl.ANY))],
        [pltpu.SemaphoreType.DMA(())],
        aliases={1: 0},
    )
    (message,) = call(
        owners_kernel,
        "owners",
        [smem_arg(ids), vmem_arg(sums), vmem_arg(swap(sums)), hbm_arg(primal)],
        [vmem_out(CHIPS * OUT, L)],
    )
    adv_out, slot_out = call(
        last_kernel,
        "last",
        [smem_arg(flags), exchange(message, AXES[:3], OUT), vmem_arg(bias), vmem_arg(bounds)],
        [(f32(AR, L), IN_VMEM), (f32(SR, L), IN_VMEM)],
    )
    return primal, adv_out.reshape(1, 512), slot_out.reshape(1, 1024)


def solution(mesh):
    return jax.shard_map(
        body,
        mesh=Mesh(mesh.devices.reshape(4, 4, 4, 2), AXES),
        in_specs=(
            P(AXES, None, None),
            P(AXES, None, None),
            P(AXES, None, None),
            P(AXES),
            P(AXES),
            P(AXES, None),
            P(AXES, None),
            P(AXES, None),
            P(AXES, None),
        ),
        out_specs=(P(AXES, None, None), P(AXES, None), P(AXES, None)),
        check_vma=False,
    )
```

```python
import functools

import jax
import jax.numpy as jnp
from jax import lax
from jax.experimental import pallas as pl
from jax.experimental.pallas import tpu as pltpu
from jax.sharding import Mesh
from jax.sharding import PartitionSpec as P

CHIPS = 64
BLOCKS = 128
L = 128
AR = 4
SR = 8
OWN = AR + SR + 1
SEL = 2 * (AR + SR) + 8
TS = 2 * (AR + SR)
MSG = TS + SR + AR
OUT = SR + AR
RB = 128
NRB = 4
BIG = 1e30
HEAD = 128
TAIL = 256

PLANE = 16
AXES = ("x", "z", "y", "core")
LINE = 8
LINE_GROUPS = [[(x * PLANE + j) * 2 + c for x in range(4) for c in range(2)] for j in range(PLANE)]
PARTNERS = [(i, i ^ 1) for i in range(2 * CHIPS)]


IN_VMEM = pl.BlockSpec(memory_space=pltpu.VMEM)
IN_SMEM = pl.BlockSpec(memory_space=pltpu.SMEM)


def device():
    x, z, y, core = (lax.axis_index(a) for a in AXES)
    return ((x * 4 + z) * 4 + y) * 2 + core


def own_kernel(adv_id, slot_id, adv, slot, limit, cap, out, bias, bounds, row_ids, ids):
    lane = lax.broadcasted_iota(jnp.int32, (8, L), 1)
    row = jnp.zeros((8, L), jnp.int32)
    for k, v in enumerate((adv_id[0], adv_id[1], slot_id[0], slot_id[1])):
        row = jnp.where(lane == k, v, row)
        ids[k] = v
    row_ids[...] = row
    data = jnp.concatenate([slot[...], adv[...], row[0:1].astype(jnp.float32)], axis=0)
    for j in range(CHIPS):
        out[j * OWN : (j + 1) * OWN, :] = data
    bias[0:SR, :] = slot[...] * 512.0 - cap[...]
    bias[SR:OUT, :] = adv[...] * 1024.0 - limit[...]
    bounds[0:SR, :] = cap[...]
    bounds[SR:OUT, :] = limit[...]


def rows_of(rec, i, slot):
    at = (jnp.maximum(i, 0) >> 1) * OWN
    return rec[pl.ds(at, SR), :] if slot else rec[pl.ds(at + SR, AR), :]


def pick_kernel(partner_ids, rec, _, out):

    lane = lax.broadcasted_iota(jnp.int32, (1, L), 1)
    row = partner_ids[0:1, :]
    wanted = [jnp.max(jnp.where(lane == k, row, -1)) for k in range(4)]
    for k in range(2):
        out[AR * k : AR * (k + 1), :] = rows_of(rec, wanted[k], False)
        out[8 + SR * k : 8 + SR * (k + 1), :] = rows_of(rec, wanted[2 + k], True)
    ids = rec[pl.ds(OWN - 1, CHIPS, stride=OWN), :]
    out[TS:SEL, :] = jnp.concatenate([ids, ids], axis=0).T[0:8, :]


def spread_half(rows, buf):
    for b in range(rows.shape[0]):
        block = jnp.broadcast_to(0.5 * rows[b : b + 1, :], (L, L))
        buf[b * L : (b + 1) * L, :] = block.T


def tree(xs):
    while len(xs) > 1:
        xs = [xs[i] + xs[i + 1] for i in range(0, len(xs), 2)]
    return xs[0]


def write_rows(sums, r_buf, tiles=(0, 1)):
    for n in range(len(tiles) * NRB):
        o = tiles[0] * AR + n
        sums[o : o + 1, :] = jnp.sum(r_buf[n * L : (n + 1) * L, :].T, axis=0, keepdims=True)


def write_cols(t, sums, cols):
    rows = [jnp.sum(c, axis=0, keepdims=True) for c in cols]
    sums[8 + t * SR : 8 + (t + 1) * SR, :] = jnp.concatenate(rows, axis=0)


def slot_rows(srow):
    return [jnp.broadcast_to(0.5 * srow[cb : cb + 1, :], (8, L)) for cb in range(SR)]


ZEROS = lambda: (jnp.zeros((8, L), jnp.float32),) * SR


def prepare_kernel(own_ids, mask, p_hbm, c_hbm, hc, psum, head, p_rest, c_ref, r_buf, p_sems, c_sems):
    def place(t, b):
        n = (t * NRB + b) * RB
        return (head, -t * 512) if n < HEAD else (p_rest, HEAD - t * 512)

    def fetch(t, b):
        rows = pl.ds(b * RB, RB)
        n = t * NRB + b
        p_ref, skip = place(t, b)
        return (
            pltpu.make_async_copy(p_hbm.at[t, rows, :], p_ref.at[pl.ds(b * RB - skip, RB), :], p_sems.at[n]),
            pltpu.make_async_copy(c_hbm.at[t, rows, :], c_ref.at[t, rows, :], c_sems.at[n]),
        )

    for t in range(2):
        for b in range(NRB):
            for copy in fetch(t, b):
                copy.start()
    for t in range(2):
        alive = jnp.where(own_ids[t] >= 0, 1, 0)

        def step(p_ref, skip, g, cols):
            r0 = pl.multiple_of(g * 16, 16)
            cols = list(cols)
            ps = [[], []]
            for cb in range(SR):
                lanes = pl.ds(cb * L, L)
                c16 = 0.5 * c_ref[t, pl.ds(r0, 16), lanes].astype(jnp.float32)
                halves = []
                for h in range(2):
                    here = jnp.full((8, L), mask[t, cb, g * 2 + h] * alive, jnp.int32) > 0
                    rows = pl.ds(pl.multiple_of(r0 + 8 * h - skip, 8), 8)
                    p = jnp.where(here, p_ref[rows, lanes], 0.0)
                    halves.append(jnp.where(here, c16[8 * h : 8 * h + 8], BIG))
                    ps[h].append(p)
                    cols[cb] = cols[cb] + p
                hc[t, pl.ds(r0, 16), lanes] = jnp.concatenate(halves, axis=0).astype(jnp.bfloat16)
            for h in range(2):
                r_buf[pl.ds(pl.multiple_of(r0 + 8 * h, 8), 8), :] = tree(ps[h])
            return tuple(cols)

        cols = ZEROS()
        for b in range(NRB):
            for copy in fetch(t, b):
                copy.wait()
            cols = lax.fori_loop(b * 8, (b + 1) * 8, functools.partial(step, *place(t, b)), cols)
        write_rows(psum, r_buf, (t,))
        write_cols(t, psum, cols)


def load_kernel(p_hbm, _, out, sem):
    copy = pltpu.make_async_copy(p_hbm.at[0, pl.ds(HEAD, 512 - HEAD), :], out, sem)
    copy.start()
    copy.wait()


def first_tile(t, srow, sources, hc_ref, out, usum, a_buf, r_buf, ready):
    s = slot_rows(srow)

    def step(p_ref, skip, g, cols):
        cols = list(cols)
        us = [[], []]
        r0 = pl.multiple_of(g * 16, 16)
        a = [a_buf[pl.ds(pl.multiple_of(t * 512 + r0 + 8 * h, 8), 8), :] for h in range(2)]
        for cb in range(SR):
            lanes = pl.ds(cb * L, L)
            c16 = hc_ref[t, pl.ds(r0, 16), lanes].astype(jnp.float32)
            for h in range(2):
                p = p_ref[pl.ds(pl.multiple_of(r0 + 8 * h - skip, 8), 8), lanes]
                hc = c16[8 * h : 8 * h + 8]
                u = jnp.minimum(jnp.maximum(((p - hc) - a[h]) - s[cb], 0.0), 1.0)
                out[t, pl.ds(pl.multiple_of(r0 + 8 * h, 8), 8), lanes] = u - hc
                us[h].append(u)
                cols[cb] = cols[cb] + u
        for h in range(2):
            r_buf[pl.ds(pl.multiple_of(t * 512 + r0 + 8 * h, 8), 8), :] = tree(us[h])
        return tuple(cols)

    cols = ZEROS()
    for b in range(NRB):
        ready(t, b)
        cols = lax.fori_loop(b * 8, (b + 1) * 8, functools.partial(step, *sources[b]), cols, unroll=2)
    write_cols(t, usum, cols)


def write_flags(own_ids, mine, other, flags):
    me = device()
    core = me & 1
    lane = lax.broadcasted_iota(jnp.int32, (4, L), 1)
    row = lax.broadcasted_iota(jnp.int32, (4, L), 0)
    place = lane * 4 + jnp.where(row < 2, core, 1 - core) * 2 + (row & 1)

    def found(where):
        return jnp.max(jnp.where(where & (lane < CHIPS), 1, 0))

    for kind in range(2):
        rows = pl.ds(TS + 2 * kind, 2)
        ids = jnp.concatenate([mine[rows, :], other[rows, :]], axis=0).astype(jnp.int32)
        for k in range(2):
            i = own_ids[2 * kind + k]
            earlier = found((ids == i) & (place < me * 2 + k))
            flags[2 * kind + k] = jnp.where((i >= 0) & (earlier == 0), 1, 0)
        flags[4 + kind] = 1 - found(ids == me)


def first_kernel(own_ids, rec, mine, other, bias, psum, hc_ref, head, rest, p_hbm, out, usum, msg, ids, flags, p_ref, a_buf, r_buf, id_buf, p_sems, sem):
    def fetch(b):
        rows = pl.ds(b * RB, RB)
        return pltpu.make_async_copy(p_hbm.at[1, rows, :], p_ref.at[rows, :], p_sems.at[b])

    def ready(t, b):
        if t == 1:
            fetch(b).wait()

    for b in range(NRB):
        fetch(b).start()
    core = lax.axis_index("core")
    id_buf[0:4, :] = mine[TS : TS + 4, :].astype(jnp.int32)
    id_buf[4:8, :] = other[TS : TS + 4, :].astype(jnp.int32)
    keep_ids = pltpu.make_async_copy(id_buf, ids, sem)
    keep_ids.start()
    write_flags(own_ids, mine, other, flags)
    slots = []
    for t in range(2):
        a, s = own_ids[t], own_ids[2 + t]
        arow = jnp.where((a & 1) == core, rows_of(rec, a, False), other[AR * t : AR * (t + 1), :])
        spread_half(arow, a_buf.at[pl.ds(t * 512, 512), :])
        slots.append(jnp.where((s & 1) == core, rows_of(rec, s, True), other[8 + SR * t : 8 + SR * (t + 1), :]))
    for t in range(2):
        sources = [(p_ref, 0) if t else (head, 0) if b * RB < HEAD else (rest, HEAD) for b in range(NRB)]
        first_tile(t, slots[t], sources, hc_ref, out, usum, a_buf, r_buf, ready)
    write_rows(usum, r_buf)
    data = jnp.concatenate([2.0 * usum[...] - psum[...], bias[...]], axis=0)
    for j in range(LINE):
        msg[j * MSG : (j + 1) * MSG, :] = data
    keep_ids.wait()


def users_kernel(ids, rec, out, acc_a0, acc_a1, acc_s0, acc_s1):
    me = device()
    chip = me >> 1
    core = me & 1
    x = chip >> 4
    line = chip & 15

    def at(i):
        return pl.multiple_of(jnp.where(i < 0, BLOCKS, i) * 8, 8)

    wanted = []
    for j in range(PLANE):
        there = (x << 4) | j
        o = j * TS
        adv = [(ids[k, there], o + AR * k) for k in range(2)]
        slot = [(ids[2 + k, there], o + 8 + SR * k) for k in range(2)]
        wanted.append((adv, slot))
    zero = jnp.zeros((8, L), jnp.float32)
    for adv, slot in wanted:
        for i, _ in adv:
            acc_a0[pl.ds(at(i), 8), :] = zero
            acc_a1[pl.ds(at(i), 8), :] = zero
        for i, _ in slot:
            acc_s0[pl.ds(at(i), 8), :] = zero
            acc_s1[pl.ds(at(i), 8), :] = zero
    for j in range(LINE):
        source = ((j >> 1) << 4) | line
        side = 4 * ((j & 1) ^ core)
        o = j * MSG
        for k, acc in ((0, acc_a0), (1, acc_a1)):
            rows = pl.ds(at(ids[side + k, source]), AR)
            acc[rows, :] = acc[rows, :] + rec[o + AR * k : o + AR * (k + 1), :]
        for k, acc in ((0, acc_s0), (1, acc_s1)):
            rows = pl.ds(at(ids[side + 2 + k, source]), SR)
            acc[rows, :] = acc[rows, :] + rec[o + 8 + SR * k : o + 8 + SR * (k + 1), :]

    def bias(i, o, n):
        b = jnp.maximum(i, 0)
        here = ((b >> 1) & 15) == line
        return rec[pl.ds(((b >> 5) * 2 + (b & 1)) * MSG + o, n), :] * jnp.where(here, 1.0, 0.0)

    for adv, slot in wanted:
        for i, o in adv:
            rows = pl.ds(at(i), AR)
            out[o : o + AR, :] = (acc_a0[rows, :] + acc_a1[rows, :]) + bias(i, TS + SR, AR)
        for i, o in slot:
            rows = pl.ds(at(i), SR)
            out[o : o + SR, :] = (acc_s0[rows, :] + acc_s1[rows, :]) + bias(i, TS, SR)


def second_tile(t, srow, base, outs, usum, a_buf, r_buf, done):
    s = slot_rows(srow)

    def step(out, skip, g, cols):
        rows = pl.ds(pl.multiple_of(g * 8, 8), 8)
        wide = pl.ds(pl.multiple_of(t * 512 + g * 8, 8), 8)
        a = a_buf[wide, :]
        cols = list(cols)
        us = []
        for cb in range(SR):
            lanes = pl.ds(cb * L, L)
            u = jnp.minimum(jnp.maximum((base[t, rows, lanes] - a) - s[cb], 0.0), 1.0)
            out[pl.ds(pl.multiple_of(g * 8 - skip, 8), 8), lanes] = u
            cols[cb] = cols[cb] + u
            us.append(u)
        r_buf[wide, :] = tree(us)
        return tuple(cols)

    cols = ZEROS()
    for b in range(NRB):
        cols = lax.fori_loop(b * 16, (b + 1) * 16, functools.partial(step, *outs[b]), cols, unroll=4)
        done(t, b)
    write_cols(t, usum, cols)


def second_kernel(flags, rec, base, psum, primal, sums, tail, out, usum, a_buf, r_buf, sems):
    early = 1024 - TAIL

    def keep(t, b):
        n = t * NRB + b
        return pltpu.make_async_copy(out.at[pl.ds(n * RB, RB), :], primal.at[t, pl.ds(b * RB, RB), :], sems.at[n])

    def done(t, b):
        if (t * NRB + b) * RB < early:
            keep(t, b).start()

    total = jnp.maximum(tree([rec[j * TS : (j + 1) * TS, :] for j in range(PLANE)]), 0.0)
    adv = total[0:8] * (1.0 / 1024)
    slot = total[8:24] * (1.0 / 512)
    spread_half(adv, a_buf)
    for t in range(2):
        outs = [(out, -t * 512) if t * 512 + b * RB < early else (tail, early - t * 512) for b in range(NRB)]
        second_tile(t, slot[8 * t : 8 * t + 8], base, outs, usum, a_buf, r_buf, done)
    write_rows(usum, r_buf)
    for k, (o, n) in enumerate(((0, AR), (AR, AR), (8, SR), (8 + SR, SR))):
        rows = pl.ds(o, n)
        named = total[o : o + n] * jnp.where(flags[k] > 0, 1.0, 0.0)
        sums[rows, :] = named + (2.0 * usum[rows, :] - psum[rows, :])
    for n in range(early // RB):
        keep(*divmod(n, NRB)).wait()


def store_kernel(tail, _, primal, sem):
    copy = pltpu.make_async_copy(tail, primal.at[1, pl.ds(512 - TAIL, TAIL), :], sem)
    copy.start()
    copy.wait()


def owners_kernel(ids, mine, other, _, out):

    me = device()
    chip = me >> 1
    core = me & 1
    out[...] = jnp.zeros_like(out)
    for side, rec in ((0, mine), (4, other)):
        for k in range(2):
            for i, o, n, src in (
                (ids[side + k, chip], SR, AR, AR * k),
                (ids[side + 2 + k, chip], 0, SR, 8 + SR * k),
            ):

                @pl.when((i >= 0) & ((i & 1) == core))
                def _():
                    rows = pl.ds((i >> 1) * OUT + o, n)
                    out[rows, :] = out[rows, :] + rec[src : src + n, :]


def last_kernel(flags, rec, bias, bounds, adv_out, slot_out):
    n = 2 * OUT
    total = tree([rec[g * n : (g + 1) * n, :] for g in range(CHIPS // 2)])
    total = total[0:OUT] + total[OUT:n]
    unnamed = jnp.maximum(bias[...], 0.0)
    slot = total[0:SR] + unnamed[0:SR] * jnp.where(flags[5] > 0, 1.0, 0.0)
    adv = total[SR:OUT] + unnamed[SR:OUT] * jnp.where(flags[4] > 0, 1.0, 0.0)
    slot_out[...] = jnp.maximum((slot - bounds[0:SR, :]) * (1.0 / 512), 0.0)
    adv_out[...] = jnp.maximum((adv - bounds[SR:OUT, :]) * (1.0 / 1024), 0.0)


def f32(*shape):
    return jax.ShapeDtypeStruct(shape, jnp.float32)


def vmem(*shape):
    return pltpu.VMEM(shape, jnp.float32)


def in_vmem(x):
    return pltpu.with_memory_space_constraint(x, pltpu.VMEM)


def in_smem(x):
    return pltpu.with_memory_space_constraint(x, pltpu.SMEM)


def call(kernel, name, ins, outs, scratch=(), mib=4, aliases={}):
    return pl.pallas_call(
        kernel,
        in_specs=[s for _, s in ins],
        out_specs=[s for _, s in outs],
        out_shape=[o for o, _ in outs],
        scratch_shapes=list(scratch),
        compiler_params=pltpu.CompilerParams(vmem_limit_bytes=mib << 20),
        input_output_aliases=aliases,
        name=name,
    )(*[x for x, _ in ins])


def in_hbm(x):
    return pltpu.with_memory_space_constraint(x, pltpu.HBM)


def hbm_arg(x):
    return (in_hbm(x), pl.BlockSpec(memory_space=pl.ANY))


def smem_out(*shape):
    return (pltpu.SMEM(shape, jnp.int32), IN_SMEM)


def smem_arg(x):
    return (in_smem(x), IN_SMEM)


def vmem_arg(x):
    return (in_vmem(x), IN_VMEM)


def vmem_out(*shape):
    return (vmem(*shape), IN_VMEM)


def exchange(x, axes, rows, groups=None):
    n = x.shape[0] // rows
    x = lax.all_to_all(x.reshape(n, rows * L), axes, 0, 0, axis_index_groups=groups, tiled=True)
    return vmem_arg(x.reshape(n * rows, L))


def swap(x):
    return lax.ppermute(x, AXES, PARTNERS)


def body(primal_start, cost, mask, tile_adv, tile_slot, adv_dual, slot_dual, spend_limit, capacity):
    tile = (2, 512, 1024)
    message, bias, bounds, row_ids, own_ids = call(
        own_kernel,
        "own",
        [(in_hbm(tile_adv), IN_SMEM), (in_hbm(tile_slot), IN_SMEM)]
        + [(in_hbm(x.reshape(-1, L)), IN_VMEM) for x in (adv_dual, slot_dual, spend_limit, capacity)],
        [vmem_out(CHIPS * OWN, L), vmem_out(OUT, L), vmem_out(OUT, L)]
        + [(pltpu.VMEM((8, L), jnp.int32), IN_VMEM), smem_out(4)],
    )
    table = exchange(message, AXES[:3], OWN)
    hc, psum, head = call(
        prepare_kernel,
        "prepare",
        [smem_arg(own_ids), (in_hbm(mask.transpose(0, 2, 1)), IN_SMEM), hbm_arg(primal_start), hbm_arg(cost)],
        [(pltpu.VMEM(tile, jnp.bfloat16), IN_VMEM), vmem_out(TS, L), vmem_out(HEAD, 1024)],
        [vmem(1024 - HEAD, 1024), pltpu.VMEM(tile, jnp.bfloat16), vmem(512, L)] + [pltpu.SemaphoreType.DMA((2 * NRB,))] * 2,
        8,
    )
    (picked,) = call(pick_kernel, "pick", [vmem_arg(swap(row_ids)), table, vmem_arg(psum)], [vmem_out(SEL, L)])
    other = swap(picked)
    (rest,) = call(
        load_kernel,
        "load",
        [hbm_arg(primal_start), vmem_arg(picked)],
        [vmem_out(512 - HEAD, 1024)],
        [pltpu.SemaphoreType.DMA(())],
    )
    base, usum, message, ids, flags = call(
        first_kernel,
        "first",
        [smem_arg(own_ids), table, vmem_arg(picked), vmem_arg(other), vmem_arg(bias), vmem_arg(psum), vmem_arg(hc)]
        + [vmem_arg(head), vmem_arg(rest), hbm_arg(primal_start)],
        [vmem_out(*tile), vmem_out(TS, L), vmem_out(LINE * MSG, L), smem_out(8, L), smem_out(6)],
        [vmem(512, 1024), vmem(1024, L), vmem(1024, L), pltpu.VMEM((8, L), jnp.int32)]
        + [pltpu.SemaphoreType.DMA((NRB,)), pltpu.SemaphoreType.DMA(())],
        8,
    )
    part = exchange(message, AXES, MSG, LINE_GROUPS)
    (message,) = call(
        users_kernel,
        "users",
        [smem_arg(ids), part],
        [vmem_out(PLANE * TS, L)],
        [vmem((BLOCKS + 1) * 8, L)] * 4,
    )
    primal, sums, tail = call(
        second_kernel,
        "second",
        [smem_arg(flags), exchange(message, AXES[1:3], TS), vmem_arg(base), vmem_arg(usum)],
        [(f32(*tile), pl.BlockSpec(memory_space=pl.ANY))] + [vmem_out(TS, L), vmem_out(TAIL, 1024)],
        [vmem(1024 - TAIL, 1024), vmem(TS, L), vmem(1024, L), vmem(1024, L)]
        + [pltpu.SemaphoreType.DMA((2 * NRB - TAIL // RB,))],
        8,
    )
    (primal,) = call(
        store_kernel,
        "store",
        [vmem_arg(tail), hbm_arg(primal)],
        [(f32(*tile), pl.BlockSpec(memory_space=pl.ANY))],
        [pltpu.SemaphoreType.DMA(())],
        aliases={1: 0},
    )
    (message,) = call(
        owners_kernel,
        "owners",
        [smem_arg(ids), vmem_arg(sums), vmem_arg(swap(sums)), hbm_arg(primal)],
        [vmem_out(CHIPS * OUT, L)],
    )
    adv_out, slot_out = call(
        last_kernel,
        "last",
        [smem_arg(flags), exchange(message, AXES[:3], OUT), vmem_arg(bias), vmem_arg(bounds)],
        [(f32(AR, L), IN_VMEM), (f32(SR, L), IN_VMEM)],
    )
    return primal, adv_out.reshape(1, 512), slot_out.reshape(1, 1024)


def solution(mesh):
    return jax.shard_map(
        body,
        mesh=Mesh(mesh.devices.reshape(4, 4, 4, 2), AXES),
        in_specs=(
            P(AXES, None, None),
            P(AXES, None, None),
            P(AXES, None, None),
            P(AXES),
            P(AXES),
            P(AXES, None),
            P(AXES, None),
            P(AXES, None),
            P(AXES, None),
        ),
        out_specs=(P(AXES, None, None), P(AXES, None), P(AXES, None)),
        check_vma=False,
    )
```

```python
import functools

import jax
import jax.numpy as jnp
from jax import lax
from jax.experimental import pallas as pl
from jax.experimental.pallas import tpu as pltpu
from jax.sharding import Mesh
from jax.sharding import PartitionSpec as P

CHIPS = 64
BLOCKS = 128
L = 128
AR = 4
SR = 8
OWN = AR + SR + 1
SEL = 2 * (AR + SR) + 8
TS = 2 * (AR + SR)
MSG = TS + SR + AR
OUT = SR + AR
RB = 128
NRB = 4
BIG = 1e30
HEAD = 128
TAIL = 256

PLANE = 16
AXES = ("x", "z", "y", "core")
LINE = 8
LINE_GROUPS = [[(x * PLANE + j) * 2 + c for x in range(4) for c in range(2)] for j in range(PLANE)]
PARTNERS = [(i, i ^ 1) for i in range(2 * CHIPS)]


IN_VMEM = pl.BlockSpec(memory_space=pltpu.VMEM)
IN_SMEM = pl.BlockSpec(memory_space=pltpu.SMEM)


def device():
    x, z, y, core = (lax.axis_index(a) for a in AXES)
    return ((x * 4 + z) * 4 + y) * 2 + core


def own_kernel(adv_id, slot_id, adv, slot, limit, cap, out, bias, bounds, row_ids, ids):
    lane = lax.broadcasted_iota(jnp.int32, (8, L), 1)
    row = jnp.zeros((8, L), jnp.int32)
    for k, v in enumerate((adv_id[0], adv_id[1], slot_id[0], slot_id[1])):
        row = jnp.where(lane == k, v, row)
        ids[k] = v
    row_ids[...] = row
    data = jnp.concatenate([slot[...], adv[...], row[0:1].astype(jnp.float32)], axis=0)
    for j in range(CHIPS):
        out[j * OWN : (j + 1) * OWN, :] = data
    bias[0:SR, :] = slot[...] * 512.0 - cap[...]
    bias[SR:OUT, :] = adv[...] * 1024.0 - limit[...]
    bounds[0:SR, :] = cap[...]
    bounds[SR:OUT, :] = limit[...]


def rows_of(rec, i, slot):
    at = (jnp.maximum(i, 0) >> 1) * OWN
    return rec[pl.ds(at, SR), :] if slot else rec[pl.ds(at + SR, AR), :]


def pick_kernel(partner_ids, rec, _, out):

    lane = lax.broadcasted_iota(jnp.int32, (1, L), 1)
    row = partner_ids[0:1, :]
    wanted = [jnp.max(jnp.where(lane == k, row, -1)) for k in range(4)]
    for k in range(2):
        out[AR * k : AR * (k + 1), :] = rows_of(rec, wanted[k], False)
        out[8 + SR * k : 8 + SR * (k + 1), :] = rows_of(rec, wanted[2 + k], True)
    ids = rec[pl.ds(OWN - 1, CHIPS, stride=OWN), :]
    out[TS:SEL, :] = jnp.concatenate([ids, ids], axis=0).T[0:8, :]


def spread_half(rows, buf):
    for b in range(rows.shape[0]):
        block = jnp.broadcast_to(0.5 * rows[b : b + 1, :], (L, L))
        buf[b * L : (b + 1) * L, :] = block.T


def tree(xs):
    while len(xs) > 1:
        xs = [xs[i] + xs[i + 1] for i in range(0, len(xs), 2)]
    return xs[0]


def write_rows(sums, r_buf, tiles=(0, 1)):
    for n in range(len(tiles) * NRB):
        o = tiles[0] * AR + n
        sums[o : o + 1, :] = jnp.sum(r_buf[n * L : (n + 1) * L, :].T, axis=0, keepdims=True)


def write_cols(t, sums, cols):
    rows = [jnp.sum(c, axis=0, keepdims=True) for c in cols]
    sums[8 + t * SR : 8 + (t + 1) * SR, :] = jnp.concatenate(rows, axis=0)


def slot_rows(srow):
    return [jnp.broadcast_to(0.5 * srow[cb : cb + 1, :], (8, L)) for cb in range(SR)]


ZEROS = lambda: (jnp.zeros((8, L), jnp.float32),) * SR


def prepare_kernel(own_ids, mask, p_hbm, c_hbm, hc, psum, head, p_rest, c_ref, r_buf, p_sems, c_sems):
    def place(t, b):
        n = (t * NRB + b) * RB
        return (head, -t * 512) if n < HEAD else (p_rest, HEAD - t * 512)

    def fetch(t, b):
        rows = pl.ds(b * RB, RB)
        n = t * NRB + b
        p_ref, skip = place(t, b)
        return (
            pltpu.make_async_copy(p_hbm.at[t, rows, :], p_ref.at[pl.ds(b * RB - skip, RB), :], p_sems.at[n]),
            pltpu.make_async_copy(c_hbm.at[t, rows, :], c_ref.at[t, rows, :], c_sems.at[n]),
        )

    for t in range(2):
        for b in range(NRB):
            for copy in fetch(t, b):
                copy.start()
    for t in range(2):
        alive = jnp.where(own_ids[t] >= 0, 1, 0)

        def step(p_ref, skip, g, cols):
            r0 = pl.multiple_of(g * 16, 16)
            cols = list(cols)
            ps = [[], []]
            for cb in range(SR):
                lanes = pl.ds(cb * L, L)
                c16 = 0.5 * c_ref[t, pl.ds(r0, 16), lanes].astype(jnp.float32)
                halves = []
                for h in range(2):
                    here = jnp.full((8, L), mask[t, cb, g * 2 + h] * alive, jnp.int32) > 0
                    rows = pl.ds(pl.multiple_of(r0 + 8 * h - skip, 8), 8)
                    p = jnp.where(here, p_ref[rows, lanes], 0.0)
                    halves.append(jnp.where(here, c16[8 * h : 8 * h + 8], BIG))
                    ps[h].append(p)
                    cols[cb] = cols[cb] + p
                hc[t, pl.ds(r0, 16), lanes] = jnp.concatenate(halves, axis=0).astype(jnp.bfloat16)
            for h in range(2):
                r_buf[pl.ds(pl.multiple_of(r0 + 8 * h, 8), 8), :] = tree(ps[h])
            return tuple(cols)

        cols = ZEROS()
        for b in range(NRB):
            for copy in fetch(t, b):
                copy.wait()
            cols = lax.fori_loop(b * 8, (b + 1) * 8, functools.partial(step, *place(t, b)), cols)
        write_rows(psum, r_buf, (t,))
        write_cols(t, psum, cols)


def load_kernel(p_hbm, _, out, sem):
    copy = pltpu.make_async_copy(p_hbm.at[0, pl.ds(HEAD, 512 - HEAD), :], out, sem)
    copy.start()
    copy.wait()


def first_tile(t, srow, sources, hc_ref, out, usum, a_buf, r_buf, ready):
    s = slot_rows(srow)

    def step(p_ref, skip, g, cols):
        cols = list(cols)
        us = [[], []]
        r0 = pl.multiple_of(g * 16, 16)
        a = [a_buf[pl.ds(pl.multiple_of(t * 512 + r0 + 8 * h, 8), 8), :] for h in range(2)]
        for cb in range(SR):
            lanes = pl.ds(cb * L, L)
            c16 = hc_ref[t, pl.ds(r0, 16), lanes].astype(jnp.float32)
            for h in range(2):
                p = p_ref[pl.ds(pl.multiple_of(r0 + 8 * h - skip, 8), 8), lanes]
                hc = c16[8 * h : 8 * h + 8]
                u = jnp.minimum(jnp.maximum(((p - hc) - a[h]) - s[cb], 0.0), 1.0)
                out[t, pl.ds(pl.multiple_of(r0 + 8 * h, 8), 8), lanes] = u - hc
                us[h].append(u)
                cols[cb] = cols[cb] + u
        for h in range(2):
            r_buf[pl.ds(pl.multiple_of(t * 512 + r0 + 8 * h, 8), 8), :] = tree(us[h])
        return tuple(cols)

    cols = ZEROS()
    for b in range(NRB):
        ready(t, b)
        cols = lax.fori_loop(b * 8, (b + 1) * 8, functools.partial(step, *sources[b]), cols, unroll=2)
    write_cols(t, usum, cols)


def first_kernel(own_ids, rec, mine, other, bias, psum, hc_ref, head, rest, p_hbm, out, usum, msg, ids, p_ref, a_buf, r_buf, id_buf, p_sems, sem):
    def fetch(b):
        rows = pl.ds(b * RB, RB)
        return pltpu.make_async_copy(p_hbm.at[1, rows, :], p_ref.at[rows, :], p_sems.at[b])

    def ready(t, b):
        if t == 1:
            fetch(b).wait()

    for b in range(NRB):
        fetch(b).start()
    core = lax.axis_index("core")
    id_buf[0:4, :] = mine[TS : TS + 4, :].astype(jnp.int32)
    id_buf[4:8, :] = other[TS : TS + 4, :].astype(jnp.int32)
    keep_ids = pltpu.make_async_copy(id_buf, ids, sem)
    keep_ids.start()
    for t in range(2):
        a, s = own_ids[t], own_ids[2 + t]
        part = pl.ds(t * 512, 512)
        arow = jnp.where((a & 1) == core, rows_of(rec, a, False), other[AR * t : AR * (t + 1), :])
        srow = jnp.where((s & 1) == core, rows_of(rec, s, True), other[8 + SR * t : 8 + SR * (t + 1), :])
        spread_half(arow, a_buf.at[part, :])
        sources = [(p_ref, 0) if t else (head, 0) if b * RB < HEAD else (rest, HEAD) for b in range(NRB)]
        first_tile(t, srow, sources, hc_ref, out, usum, a_buf, r_buf, ready)
        write_rows(usum, r_buf.at[part, :], (t,))
    data = jnp.concatenate([2.0 * usum[...] - psum[...], bias[...]], axis=0)
    for j in range(LINE):
        msg[j * MSG : (j + 1) * MSG, :] = data
    keep_ids.wait()


def write_flags(own_ids, mine, other, flags):
    me = device()
    core = me & 1
    lane = lax.broadcasted_iota(jnp.int32, (4, L), 1)
    row = lax.broadcasted_iota(jnp.int32, (4, L), 0)
    place = lane * 4 + jnp.where(row < 2, core, 1 - core) * 2 + (row & 1)

    def found(where):
        return jnp.max(jnp.where(where & (lane < CHIPS), 1, 0))

    for kind in range(2):
        rows = pl.ds(TS + 2 * kind, 2)
        ids = jnp.concatenate([mine[rows, :], other[rows, :]], axis=0).astype(jnp.int32)
        for k in range(2):
            i = own_ids[2 * kind + k]
            earlier = found((ids == i) & (place < me * 2 + k))
            flags[2 * kind + k] = jnp.where((i >= 0) & (earlier == 0), 1, 0)
        flags[4 + kind] = 1 - found(ids == me)


def users_kernel(own_ids, ids, mine, other, rec, out, flags, acc_a0, acc_a1, acc_s0, acc_s1):
    write_flags(own_ids, mine, other, flags)
    me = device()
    chip = me >> 1
    core = me & 1
    x = chip >> 4
    line = chip & 15

    def at(i):
        return pl.multiple_of(jnp.where(i < 0, BLOCKS, i) * 8, 8)

    wanted = []
    for j in range(PLANE):
        there = (x << 4) | j
        o = j * TS
        adv = [(ids[k, there], o + AR * k) for k in range(2)]
        slot = [(ids[2 + k, there], o + 8 + SR * k) for k in range(2)]
        wanted.append((adv, slot))
    zero = jnp.zeros((8, L), jnp.float32)
    for adv, slot in wanted:
        for i, _ in adv:
            acc_a0[pl.ds(at(i), 8), :] = zero
            acc_a1[pl.ds(at(i), 8), :] = zero
        for i, _ in slot:
            acc_s0[pl.ds(at(i), 8), :] = zero
            acc_s1[pl.ds(at(i), 8), :] = zero
    for j in range(LINE):
        source = ((j >> 1) << 4) | line
        side = 4 * ((j & 1) ^ core)
        o = j * MSG
        for k, acc in ((0, acc_a0), (1, acc_a1)):
            rows = pl.ds(at(ids[side + k, source]), AR)
            acc[rows, :] = acc[rows, :] + rec[o + AR * k : o + AR * (k + 1), :]
        for k, acc in ((0, acc_s0), (1, acc_s1)):
            rows = pl.ds(at(ids[side + 2 + k, source]), SR)
            acc[rows, :] = acc[rows, :] + rec[o + 8 + SR * k : o + 8 + SR * (k + 1), :]

    def bias(i, o, n):
        b = jnp.maximum(i, 0)
        here = ((b >> 1) & 15) == line
        return rec[pl.ds(((b >> 5) * 2 + (b & 1)) * MSG + o, n), :] * jnp.where(here, 1.0, 0.0)

    for adv, slot in wanted:
        for i, o in adv:
            rows = pl.ds(at(i), AR)
            out[o : o + AR, :] = (acc_a0[rows, :] + acc_a1[rows, :]) + bias(i, TS + SR, AR)
        for i, o in slot:
            rows = pl.ds(at(i), SR)
            out[o : o + SR, :] = (acc_s0[rows, :] + acc_s1[rows, :]) + bias(i, TS, SR)


def second_tile(t, srow, base, outs, usum, a_buf, r_buf, done):
    s = slot_rows(srow)

    def step(out, skip, g, cols):
        rows = pl.ds(pl.multiple_of(g * 8, 8), 8)
        wide = pl.ds(pl.multiple_of(t * 512 + g * 8, 8), 8)
        a = a_buf[wide, :]
        cols = list(cols)
        us = []
        for cb in range(SR):
            lanes = pl.ds(cb * L, L)
            u = jnp.minimum(jnp.maximum((base[t, rows, lanes] - a) - s[cb], 0.0), 1.0)
            out[pl.ds(pl.multiple_of(g * 8 - skip, 8), 8), lanes] = u
            cols[cb] = cols[cb] + u
            us.append(u)
        r_buf[wide, :] = tree(us)
        return tuple(cols)

    cols = ZEROS()
    for b in range(NRB):
        cols = lax.fori_loop(b * 16, (b + 1) * 16, functools.partial(step, *outs[b]), cols, unroll=4)
        done(t, b)
    write_cols(t, usum, cols)


def second_kernel(flags, rec, base, psum, primal, sums, tail, out, usum, a_buf, r_buf, sems):
    early = 1024 - TAIL

    def keep(t, b):
        n = t * NRB + b
        return pltpu.make_async_copy(out.at[pl.ds(n * RB, RB), :], primal.at[t, pl.ds(b * RB, RB), :], sems.at[n])

    def done(t, b):
        if (t * NRB + b) * RB < early:
            keep(t, b).start()

    total = jnp.maximum(tree([rec[j * TS : (j + 1) * TS, :] for j in range(PLANE)]), 0.0)
    adv = total[0:8] * (1.0 / 1024)
    slot = total[8:24] * (1.0 / 512)
    for t in range(2):
        outs = [(out, -t * 512) if t * 512 + b * RB < early else (tail, early - t * 512) for b in range(NRB)]
        part = pl.ds(t * 512, 512)
        spread_half(adv[4 * t : 4 * t + 4], a_buf.at[part, :])
        second_tile(t, slot[8 * t : 8 * t + 8], base, outs, usum, a_buf, r_buf, done)
        write_rows(usum, r_buf.at[part, :], (t,))
    for k, (o, n) in enumerate(((0, AR), (AR, AR), (8, SR), (8 + SR, SR))):
        rows = pl.ds(o, n)
        named = total[o : o + n] * jnp.where(flags[k] > 0, 1.0, 0.0)
        sums[rows, :] = named + (2.0 * usum[rows, :] - psum[rows, :])
    for n in range(early // RB):
        keep(*divmod(n, NRB)).wait()


def store_kernel(tail, _, primal, sem):
    copy = pltpu.make_async_copy(tail, primal.at[1, pl.ds(512 - TAIL, TAIL), :], sem)
    copy.start()
    copy.wait()


def owners_kernel(ids, mine, other, _, out):

    me = device()
    chip = me >> 1
    core = me & 1
    out[...] = jnp.zeros_like(out)
    for side, rec in ((0, mine), (4, other)):
        for k in range(2):
            for i, o, n, src in (
                (ids[side + k, chip], SR, AR, AR * k),
                (ids[side + 2 + k, chip], 0, SR, 8 + SR * k),
            ):

                @pl.when((i >= 0) & ((i & 1) == core))
                def _():
                    rows = pl.ds((i >> 1) * OUT + o, n)
                    out[rows, :] = out[rows, :] + rec[src : src + n, :]


def last_kernel(flags, rec, bias, bounds, adv_out, slot_out):
    n = 2 * OUT
    total = tree([rec[g * n : (g + 1) * n, :] for g in range(CHIPS // 2)])
    total = total[0:OUT] + total[OUT:n]
    unnamed = jnp.maximum(bias[...], 0.0)
    slot = total[0:SR] + unnamed[0:SR] * jnp.where(flags[5] > 0, 1.0, 0.0)
    adv = total[SR:OUT] + unnamed[SR:OUT] * jnp.where(flags[4] > 0, 1.0, 0.0)
    slot_out[...] = jnp.maximum((slot - bounds[0:SR, :]) * (1.0 / 512), 0.0)
    adv_out[...] = jnp.maximum((adv - bounds[SR:OUT, :]) * (1.0 / 1024), 0.0)


def f32(*shape):
    return jax.ShapeDtypeStruct(shape, jnp.float32)


def vmem(*shape):
    return pltpu.VMEM(shape, jnp.float32)


def in_vmem(x):
    return pltpu.with_memory_space_constraint(x, pltpu.VMEM)


def in_smem(x):
    return pltpu.with_memory_space_constraint(x, pltpu.SMEM)


def call(kernel, name, ins, outs, scratch=(), mib=4, aliases={}):
    return pl.pallas_call(
        kernel,
        in_specs=[s for _, s in ins],
        out_specs=[s for _, s in outs],
        out_shape=[o for o, _ in outs],
        scratch_shapes=list(scratch),
        compiler_params=pltpu.CompilerParams(vmem_limit_bytes=mib << 20),
        input_output_aliases=aliases,
        name=name,
    )(*[x for x, _ in ins])


def in_hbm(x):
    return pltpu.with_memory_space_constraint(x, pltpu.HBM)


def hbm_arg(x):
    return (in_hbm(x), pl.BlockSpec(memory_space=pl.ANY))


def smem_out(*shape):
    return (pltpu.SMEM(shape, jnp.int32), IN_SMEM)


def smem_arg(x):
    return (in_smem(x), IN_SMEM)


def vmem_arg(x):
    return (in_vmem(x), IN_VMEM)


def vmem_out(*shape):
    return (vmem(*shape), IN_VMEM)


def exchange(x, axes, rows, groups=None):
    n = x.shape[0] // rows
    x = lax.all_to_all(x.reshape(n, rows * L), axes, 0, 0, axis_index_groups=groups, tiled=True)
    return vmem_arg(x.reshape(n * rows, L))


def swap(x):
    return lax.ppermute(x, AXES, PARTNERS)


def body(primal_start, cost, mask, tile_adv, tile_slot, adv_dual, slot_dual, spend_limit, capacity):
    tile = (2, 512, 1024)
    message, bias, bounds, row_ids, own_ids = call(
        own_kernel,
        "own",
        [(in_hbm(tile_adv), IN_SMEM), (in_hbm(tile_slot), IN_SMEM)]
        + [(in_hbm(x.reshape(-1, L)), IN_VMEM) for x in (adv_dual, slot_dual, spend_limit, capacity)],
        [vmem_out(CHIPS * OWN, L), vmem_out(OUT, L), vmem_out(OUT, L)]
        + [(pltpu.VMEM((8, L), jnp.int32), IN_VMEM), smem_out(4)],
    )
    table = exchange(message, AXES[:3], OWN)
    hc, psum, head = call(
        prepare_kernel,
        "prepare",
        [smem_arg(own_ids), (in_hbm(mask.transpose(0, 2, 1)), IN_SMEM), hbm_arg(primal_start), hbm_arg(cost)],
        [(pltpu.VMEM(tile, jnp.bfloat16), IN_VMEM), vmem_out(TS, L), vmem_out(HEAD, 1024)],
        [vmem(1024 - HEAD, 1024), pltpu.VMEM(tile, jnp.bfloat16), vmem(512, L)] + [pltpu.SemaphoreType.DMA((2 * NRB,))] * 2,
        8,
    )
    (picked,) = call(pick_kernel, "pick", [vmem_arg(swap(row_ids)), table, vmem_arg(psum)], [vmem_out(SEL, L)])
    other = swap(picked)
    (rest,) = call(
        load_kernel,
        "load",
        [hbm_arg(primal_start), vmem_arg(picked)],
        [vmem_out(512 - HEAD, 1024)],
        [pltpu.SemaphoreType.DMA(())],
    )
    base, usum, message, ids = call(
        first_kernel,
        "first",
        [smem_arg(own_ids), table, vmem_arg(picked), vmem_arg(other), vmem_arg(bias), vmem_arg(psum), vmem_arg(hc)]
        + [vmem_arg(head), vmem_arg(rest), hbm_arg(primal_start)],
        [vmem_out(*tile), vmem_out(TS, L), vmem_out(LINE * MSG, L), smem_out(8, L)],
        [vmem(512, 1024), vmem(1024, L), vmem(1024, L), pltpu.VMEM((8, L), jnp.int32)]
        + [pltpu.SemaphoreType.DMA((NRB,)), pltpu.SemaphoreType.DMA(())],
        8,
    )
    part = exchange(message, AXES, MSG, LINE_GROUPS)
    message, flags = call(
        users_kernel,
        "users",
        [smem_arg(own_ids), smem_arg(ids), vmem_arg(picked), vmem_arg(other), part],
        [vmem_out(PLANE * TS, L), smem_out(6)],
        [vmem((BLOCKS + 1) * 8, L)] * 4,
    )
    primal, sums, tail = call(
        second_kernel,
        "second",
        [smem_arg(flags), exchange(message, AXES[1:3], TS), vmem_arg(base), vmem_arg(usum)],
        [(f32(*tile), pl.BlockSpec(memory_space=pl.ANY))] + [vmem_out(TS, L), vmem_out(TAIL, 1024)],
        [vmem(1024 - TAIL, 1024), vmem(TS, L), vmem(1024, L), vmem(1024, L)]
        + [pltpu.SemaphoreType.DMA((2 * NRB - TAIL // RB,))],
        8,
    )
    (primal,) = call(
        store_kernel,
        "store",
        [vmem_arg(tail), hbm_arg(primal)],
        [(f32(*tile), pl.BlockSpec(memory_space=pl.ANY))],
        [pltpu.SemaphoreType.DMA(())],
        aliases={1: 0},
    )
    (message,) = call(
        owners_kernel,
        "owners",
        [smem_arg(ids), vmem_arg(sums), vmem_arg(swap(sums)), hbm_arg(primal)],
        [vmem_out(CHIPS * OUT, L)],
    )
    adv_out, slot_out = call(
        last_kernel,
        "last",
        [smem_arg(flags), exchange(message, AXES[:3], OUT), vmem_arg(bias), vmem_arg(bounds)],
        [(f32(AR, L), IN_VMEM), (f32(SR, L), IN_VMEM)],
    )
    return primal, adv_out.reshape(1, 512), slot_out.reshape(1, 1024)


def solution(mesh):
    return jax.shard_map(
        body,
        mesh=Mesh(mesh.devices.reshape(4, 4, 4, 2), AXES),
        in_specs=(
            P(AXES, None, None),
            P(AXES, None, None),
            P(AXES, None, None),
            P(AXES),
            P(AXES),
            P(AXES, None),
            P(AXES, None),
            P(AXES, None),
            P(AXES, None),
        ),
        out_specs=(P(AXES, None, None), P(AXES, None), P(AXES, None)),
        check_vma=False,
    )
```

```python
import functools

import jax
import jax.numpy as jnp
from jax import lax
from jax.experimental import pallas as pl
from jax.experimental.pallas import tpu as pltpu
from jax.sharding import Mesh
from jax.sharding import PartitionSpec as P

CHIPS = 64
BLOCKS = 128
L = 128
AR = 4
SR = 8
OWN = AR + SR + 1
SEL = 2 * (AR + SR) + 8
TS = 2 * (AR + SR)
MSG = TS + SR + AR
OUT = SR + AR
RB = 128
NRB = 4
BIG = 1e30
HEAD = 128
TAIL = 384

PLANE = 16
AXES = ("x", "z", "y", "core")
LINE = 8
LINE_GROUPS = [[(x * PLANE + j) * 2 + c for x in range(4) for c in range(2)] for j in range(PLANE)]
PARTNERS = [(i, i ^ 1) for i in range(2 * CHIPS)]


IN_VMEM = pl.BlockSpec(memory_space=pltpu.VMEM)
IN_SMEM = pl.BlockSpec(memory_space=pltpu.SMEM)


def device():
    x, z, y, core = (lax.axis_index(a) for a in AXES)
    return ((x * 4 + z) * 4 + y) * 2 + core


def own_kernel(adv_id, slot_id, adv, slot, limit, cap, out, bias, bounds, row_ids, ids):
    lane = lax.broadcasted_iota(jnp.int32, (8, L), 1)
    row = jnp.zeros((8, L), jnp.int32)
    for k, v in enumerate((adv_id[0], adv_id[1], slot_id[0], slot_id[1])):
        row = jnp.where(lane == k, v, row)
        ids[k] = v
    row_ids[...] = row
    data = jnp.concatenate([slot[...], adv[...], row[0:1].astype(jnp.float32)], axis=0)
    for j in range(CHIPS):
        out[j * OWN : (j + 1) * OWN, :] = data
    bias[0:SR, :] = slot[...] * 512.0 - cap[...]
    bias[SR:OUT, :] = adv[...] * 1024.0 - limit[...]
    bounds[0:SR, :] = cap[...]
    bounds[SR:OUT, :] = limit[...]


def rows_of(rec, i, slot):
    at = (jnp.maximum(i, 0) >> 1) * OWN
    return rec[pl.ds(at, SR), :] if slot else rec[pl.ds(at + SR, AR), :]


def pick_kernel(partner_ids, rec, _, out):

    lane = lax.broadcasted_iota(jnp.int32, (1, L), 1)
    row = partner_ids[0:1, :]
    wanted = [jnp.max(jnp.where(lane == k, row, -1)) for k in range(4)]
    for k in range(2):
        out[AR * k : AR * (k + 1), :] = rows_of(rec, wanted[k], False)
        out[8 + SR * k : 8 + SR * (k + 1), :] = rows_of(rec, wanted[2 + k], True)
    ids = rec[pl.ds(OWN - 1, CHIPS, stride=OWN), :]
    out[TS:SEL, :] = jnp.concatenate([ids, ids], axis=0).T[0:8, :]


def spread_half(rows, buf):
    for b in range(rows.shape[0]):
        block = jnp.broadcast_to(0.5 * rows[b : b + 1, :], (L, L))
        buf[b * L : (b + 1) * L, :] = block.T


def tree(xs):
    while len(xs) > 1:
        xs = [xs[i] + xs[i + 1] for i in range(0, len(xs), 2)]
    return xs[0]


def write_rows(sums, r_buf, tiles=(0, 1)):
    for n in range(len(tiles) * NRB):
        o = tiles[0] * AR + n
        sums[o : o + 1, :] = jnp.sum(r_buf[n * L : (n + 1) * L, :].T, axis=0, keepdims=True)


def write_cols(t, sums, cols):
    rows = [jnp.sum(c, axis=0, keepdims=True) for c in cols]
    sums[8 + t * SR : 8 + (t + 1) * SR, :] = jnp.concatenate(rows, axis=0)


def slot_rows(srow):
    return [jnp.broadcast_to(0.5 * srow[cb : cb + 1, :], (8, L)) for cb in range(SR)]


ZEROS = lambda: (jnp.zeros((8, L), jnp.float32),) * SR


def prepare_kernel(own_ids, mask, p_hbm, c_hbm, hc, psum, head, p_rest, c_ref, r_buf, p_sems, c_sems):
    def place(t, b):
        n = (t * NRB + b) * RB
        return (head, -t * 512) if n < HEAD else (p_rest, HEAD - t * 512)

    def fetch(t, b):
        rows = pl.ds(b * RB, RB)
        n = t * NRB + b
        p_ref, skip = place(t, b)
        return (
            pltpu.make_async_copy(p_hbm.at[t, rows, :], p_ref.at[pl.ds(b * RB - skip, RB), :], p_sems.at[n]),
            pltpu.make_async_copy(c_hbm.at[t, rows, :], c_ref.at[t, rows, :], c_sems.at[n]),
        )

    for t in range(2):
        for b in range(NRB):
            for copy in fetch(t, b):
                copy.start()
    for t in range(2):
        alive = jnp.where(own_ids[t] >= 0, 1, 0)

        def step(p_ref, skip, g, cols):
            r0 = pl.multiple_of(g * 16, 16)
            cols = list(cols)
            ps = [[], []]
            for cb in range(SR):
                lanes = pl.ds(cb * L, L)
                c16 = 0.5 * c_ref[t, pl.ds(r0, 16), lanes].astype(jnp.float32)
                halves = []
                for h in range(2):
                    here = jnp.full((8, L), mask[t, cb, g * 2 + h] * alive, jnp.int32) > 0
                    rows = pl.ds(pl.multiple_of(r0 + 8 * h - skip, 8), 8)
                    p = jnp.where(here, p_ref[rows, lanes], 0.0)
                    halves.append(jnp.where(here, c16[8 * h : 8 * h + 8], BIG))
                    ps[h].append(p)
                    cols[cb] = cols[cb] + p
                hc[t, pl.ds(r0, 16), lanes] = jnp.concatenate(halves, axis=0).astype(jnp.bfloat16)
            for h in range(2):
                r_buf[pl.ds(pl.multiple_of(r0 + 8 * h, 8), 8), :] = tree(ps[h])
            return tuple(cols)

        cols = ZEROS()
        for b in range(NRB):
            for copy in fetch(t, b):
                copy.wait()
            cols = lax.fori_loop(b * 8, (b + 1) * 8, functools.partial(step, *place(t, b)), cols)
        write_rows(psum, r_buf, (t,))
        write_cols(t, psum, cols)


def load_kernel(p_hbm, _, out, sem):
    copy = pltpu.make_async_copy(p_hbm.at[0, pl.ds(HEAD, 512 - HEAD), :], out, sem)
    copy.start()
    copy.wait()


def first_tile(t, srow, sources, hc_ref, out, usum, a_buf, r_buf, ready):
    s = slot_rows(srow)

    def step(p_ref, skip, g, cols):
        cols = list(cols)
        us = [[], []]
        r0 = pl.multiple_of(g * 16, 16)
        a = [a_buf[pl.ds(pl.multiple_of(t * 512 + r0 + 8 * h, 8), 8), :] for h in range(2)]
        for cb in range(SR):
            lanes = pl.ds(cb * L, L)
            c16 = hc_ref[t, pl.ds(r0, 16), lanes].astype(jnp.float32)
            for h in range(2):
                p = p_ref[pl.ds(pl.multiple_of(r0 + 8 * h - skip, 8), 8), lanes]
                hc = c16[8 * h : 8 * h + 8]
                u = jnp.minimum(jnp.maximum(((p - hc) - a[h]) - s[cb], 0.0), 1.0)
                out[t, pl.ds(pl.multiple_of(r0 + 8 * h, 8), 8), lanes] = u - hc
                us[h].append(u)
                cols[cb] = cols[cb] + u
        for h in range(2):
            r_buf[pl.ds(pl.multiple_of(t * 512 + r0 + 8 * h, 8), 8), :] = tree(us[h])
        return tuple(cols)

    cols = ZEROS()
    for b in range(NRB):
        ready(t, b)
        cols = lax.fori_loop(b * 8, (b + 1) * 8, functools.partial(step, *sources[b]), cols, unroll=2)
    write_cols(t, usum, cols)


def first_kernel(own_ids, rec, mine, other, bias, psum, hc_ref, head, rest, p_hbm, out, usum, msg, ids, p_ref, a_buf, r_buf, id_buf, p_sems, sem):
    def fetch(b):
        rows = pl.ds(b * RB, RB)
        return pltpu.make_async_copy(p_hbm.at[1, rows, :], p_ref.at[rows, :], p_sems.at[b])

    def ready(t, b):
        if t == 1:
            fetch(b).wait()

    for b in range(NRB):
        fetch(b).start()
    core = lax.axis_index("core")
    id_buf[0:4, :] = mine[TS : TS + 4, :].astype(jnp.int32)
    id_buf[4:8, :] = other[TS : TS + 4, :].astype(jnp.int32)
    keep_ids = pltpu.make_async_copy(id_buf, ids, sem)
    keep_ids.start()
    for t in range(2):
        a, s = own_ids[t], own_ids[2 + t]
        part = pl.ds(t * 512, 512)
        arow = jnp.where((a & 1) == core, rows_of(rec, a, False), other[AR * t : AR * (t + 1), :])
        srow = jnp.where((s & 1) == core, rows_of(rec, s, True), other[8 + SR * t : 8 + SR * (t + 1), :])
        spread_half(arow, a_buf.at[part, :])
        sources = [(p_ref, 0) if t else (head, 0) if b * RB < HEAD else (rest, HEAD) for b in range(NRB)]
        first_tile(t, srow, sources, hc_ref, out, usum, a_buf, r_buf, ready)
        write_rows(usum, r_buf.at[part, :], (t,))
    data = jnp.concatenate([2.0 * usum[...] - psum[...], bias[...]], axis=0)
    for j in range(LINE):
        msg[j * MSG : (j + 1) * MSG, :] = data
    keep_ids.wait()


def write_flags(own_ids, mine, other, flags):
    me = device()
    core = me & 1
    lane = lax.broadcasted_iota(jnp.int32, (4, L), 1)
    row = lax.broadcasted_iota(jnp.int32, (4, L), 0)
    place = lane * 4 + jnp.where(row < 2, core, 1 - core) * 2 + (row & 1)

    def found(where):
        return jnp.max(jnp.where(where & (lane < CHIPS), 1, 0))

    for kind in range(2):
        rows = pl.ds(TS + 2 * kind, 2)
        ids = jnp.concatenate([mine[rows, :], other[rows, :]], axis=0).astype(jnp.int32)
        for k in range(2):
            i = own_ids[2 * kind + k]
            earlier = found((ids == i) & (place < me * 2 + k))
            flags[2 * kind + k] = jnp.where((i >= 0) & (earlier == 0), 1, 0)
        flags[4 + kind] = 1 - found(ids == me)


def users_kernel(own_ids, ids, mine, other, rec, out, flags, acc_a0, acc_a1, acc_s0, acc_s1):
    write_flags(own_ids, mine, other, flags)
    me = device()
    chip = me >> 1
    core = me & 1
    x = chip >> 4
    line = chip & 15

    def at(i):
        return pl.multiple_of(jnp.where(i < 0, BLOCKS, i) * 8, 8)

    wanted = []
    for j in range(PLANE):
        there = (x << 4) | j
        o = j * TS
        adv = [(ids[k, there], o + AR * k) for k in range(2)]
        slot = [(ids[2 + k, there], o + 8 + SR * k) for k in range(2)]
        wanted.append((adv, slot))
    zero = jnp.zeros((8, L), jnp.float32)
    for adv, slot in wanted:
        for i, _ in adv:
            acc_a0[pl.ds(at(i), 8), :] = zero
            acc_a1[pl.ds(at(i), 8), :] = zero
        for i, _ in slot:
            acc_s0[pl.ds(at(i), 8), :] = zero
            acc_s1[pl.ds(at(i), 8), :] = zero
    for j in range(LINE):
        source = ((j >> 1) << 4) | line
        side = 4 * ((j & 1) ^ core)
        o = j * MSG
        for k, acc in ((0, acc_a0), (1, acc_a1)):
            rows = pl.ds(at(ids[side + k, source]), AR)
            acc[rows, :] = acc[rows, :] + rec[o + AR * k : o + AR * (k + 1), :]
        for k, acc in ((0, acc_s0), (1, acc_s1)):
            rows = pl.ds(at(ids[side + 2 + k, source]), SR)
            acc[rows, :] = acc[rows, :] + rec[o + 8 + SR * k : o + 8 + SR * (k + 1), :]

    def bias(i, o, n):
        b = jnp.maximum(i, 0)
        here = ((b >> 1) & 15) == line
        return rec[pl.ds(((b >> 5) * 2 + (b & 1)) * MSG + o, n), :] * jnp.where(here, 1.0, 0.0)

    for adv, slot in wanted:
        for i, o in adv:
            rows = pl.ds(at(i), AR)
            out[o : o + AR, :] = (acc_a0[rows, :] + acc_a1[rows, :]) + bias(i, TS + SR, AR)
        for i, o in slot:
            rows = pl.ds(at(i), SR)
            out[o : o + SR, :] = (acc_s0[rows, :] + acc_s1[rows, :]) + bias(i, TS, SR)


def second_tile(t, srow, base, outs, usum, a_buf, r_buf, done):
    s = slot_rows(srow)

    def step(out, skip, g, cols):
        rows = pl.ds(pl.multiple_of(g * 8, 8), 8)
        wide = pl.ds(pl.multiple_of(t * 512 + g * 8, 8), 8)
        a = a_buf[wide, :]
        cols = list(cols)
        us = []
        for cb in range(SR):
            lanes = pl.ds(cb * L, L)
            u = jnp.minimum(jnp.maximum((base[t, rows, lanes] - a) - s[cb], 0.0), 1.0)
            out[pl.ds(pl.multiple_of(g * 8 - skip, 8), 8), lanes] = u
            cols[cb] = cols[cb] + u
            us.append(u)
        r_buf[wide, :] = tree(us)
        return tuple(cols)

    cols = ZEROS()
    for b in range(NRB):
        cols = lax.fori_loop(b * 16, (b + 1) * 16, functools.partial(step, *outs[b]), cols, unroll=4)
        done(t, b)
    write_cols(t, usum, cols)


def second_kernel(flags, rec, base, psum, primal, sums, tail, out, usum, a_buf, r_buf, sems):
    early = 1024 - TAIL

    def keep(t, b):
        n = t * NRB + b
        return pltpu.make_async_copy(out.at[pl.ds(n * RB, RB), :], primal.at[t, pl.ds(b * RB, RB), :], sems.at[n])

    def done(t, b):
        if (t * NRB + b) * RB < early:
            keep(t, b).start()

    total = jnp.maximum(tree([rec[j * TS : (j + 1) * TS, :] for j in range(PLANE)]), 0.0)
    adv = total[0:8] * (1.0 / 1024)
    slot = total[8:24] * (1.0 / 512)
    for t in range(2):
        outs = [(out, -t * 512) if t * 512 + b * RB < early else (tail, early - t * 512) for b in range(NRB)]
        part = pl.ds(t * 512, 512)
        spread_half(adv[4 * t : 4 * t + 4], a_buf.at[part, :])
        second_tile(t, slot[8 * t : 8 * t + 8], base, outs, usum, a_buf, r_buf, done)
        write_rows(usum, r_buf.at[part, :], (t,))
    for k, (o, n) in enumerate(((0, AR), (AR, AR), (8, SR), (8 + SR, SR))):
        rows = pl.ds(o, n)
        named = total[o : o + n] * jnp.where(flags[k] > 0, 1.0, 0.0)
        sums[rows, :] = named + (2.0 * usum[rows, :] - psum[rows, :])
    for n in range(early // RB):
        keep(*divmod(n, NRB)).wait()


def store_kernel(tail, _, primal, sem):
    copy = pltpu.make_async_copy(tail, primal.at[1, pl.ds(512 - TAIL, TAIL), :], sem)
    copy.start()
    copy.wait()


def owners_kernel(ids, mine, other, _, out):

    me = device()
    chip = me >> 1
    core = me & 1
    out[...] = jnp.zeros_like(out)
    for side, rec in ((0, mine), (4, other)):
        for k in range(2):
            for i, o, n, src in (
                (ids[side + k, chip], SR, AR, AR * k),
                (ids[side + 2 + k, chip], 0, SR, 8 + SR * k),
            ):

                @pl.when((i >= 0) & ((i & 1) == core))
                def _():
                    rows = pl.ds((i >> 1) * OUT + o, n)
                    out[rows, :] = out[rows, :] + rec[src : src + n, :]


def last_kernel(flags, rec, bias, bounds, adv_out, slot_out):
    n = 2 * OUT
    total = tree([rec[g * n : (g + 1) * n, :] for g in range(CHIPS // 2)])
    total = total[0:OUT] + total[OUT:n]
    unnamed = jnp.maximum(bias[...], 0.0)
    slot = total[0:SR] + unnamed[0:SR] * jnp.where(flags[5] > 0, 1.0, 0.0)
    adv = total[SR:OUT] + unnamed[SR:OUT] * jnp.where(flags[4] > 0, 1.0, 0.0)
    slot_out[...] = jnp.maximum((slot - bounds[0:SR, :]) * (1.0 / 512), 0.0)
    adv_out[...] = jnp.maximum((adv - bounds[SR:OUT, :]) * (1.0 / 1024), 0.0)


def f32(*shape):
    return jax.ShapeDtypeStruct(shape, jnp.float32)


def vmem(*shape):
    return pltpu.VMEM(shape, jnp.float32)


def in_vmem(x):
    return pltpu.with_memory_space_constraint(x, pltpu.VMEM)


def in_smem(x):
    return pltpu.with_memory_space_constraint(x, pltpu.SMEM)


def call(kernel, name, ins, outs, scratch=(), mib=4, aliases={}):
    return pl.pallas_call(
        kernel,
        in_specs=[s for _, s in ins],
        out_specs=[s for _, s in outs],
        out_shape=[o for o, _ in outs],
        scratch_shapes=list(scratch),
        compiler_params=pltpu.CompilerParams(vmem_limit_bytes=mib << 20),
        input_output_aliases=aliases,
        name=name,
    )(*[x for x, _ in ins])


def in_hbm(x):
    return pltpu.with_memory_space_constraint(x, pltpu.HBM)


def hbm_arg(x):
    return (in_hbm(x), pl.BlockSpec(memory_space=pl.ANY))


def smem_out(*shape):
    return (pltpu.SMEM(shape, jnp.int32), IN_SMEM)


def smem_arg(x):
    return (in_smem(x), IN_SMEM)


def vmem_arg(x):
    return (in_vmem(x), IN_VMEM)


def vmem_out(*shape):
    return (vmem(*shape), IN_VMEM)


def exchange(x, axes, rows, groups=None):
    n = x.shape[0] // rows
    x = lax.all_to_all(x.reshape(n, rows * L), axes, 0, 0, axis_index_groups=groups, tiled=True)
    return vmem_arg(x.reshape(n * rows, L))


def swap(x):
    return lax.ppermute(x, AXES, PARTNERS)


def body(primal_start, cost, mask, tile_adv, tile_slot, adv_dual, slot_dual, spend_limit, capacity):
    tile = (2, 512, 1024)
    message, bias, bounds, row_ids, own_ids = call(
        own_kernel,
        "own",
        [(in_hbm(tile_adv), IN_SMEM), (in_hbm(tile_slot), IN_SMEM)]
        + [(in_hbm(x.reshape(-1, L)), IN_VMEM) for x in (adv_dual, slot_dual, spend_limit, capacity)],
        [vmem_out(CHIPS * OWN, L), vmem_out(OUT, L), vmem_out(OUT, L)]
        + [(pltpu.VMEM((8, L), jnp.int32), IN_VMEM), smem_out(4)],
    )
    table = exchange(message, AXES[:3], OWN)
    hc, psum, head = call(
        prepare_kernel,
        "prepare",
        [smem_arg(own_ids), (in_hbm(mask.transpose(0, 2, 1)), IN_SMEM), hbm_arg(primal_start), hbm_arg(cost)],
        [(pltpu.VMEM(tile, jnp.bfloat16), IN_VMEM), vmem_out(TS, L), vmem_out(HEAD, 1024)],
        [vmem(1024 - HEAD, 1024), pltpu.VMEM(tile, jnp.bfloat16), vmem(512, L)] + [pltpu.SemaphoreType.DMA((2 * NRB,))] * 2,
        8,
    )
    (picked,) = call(pick_kernel, "pick", [vmem_arg(swap(row_ids)), table, vmem_arg(psum)], [vmem_out(SEL, L)])
    other = swap(picked)
    (rest,) = call(
        load_kernel,
        "load",
        [hbm_arg(primal_start), vmem_arg(picked)],
        [vmem_out(512 - HEAD, 1024)],
        [pltpu.SemaphoreType.DMA(())],
    )
    base, usum, message, ids = call(
        first_kernel,
        "first",
        [smem_arg(own_ids), table, vmem_arg(picked), vmem_arg(other), vmem_arg(bias), vmem_arg(psum), vmem_arg(hc)]
        + [vmem_arg(head), vmem_arg(rest), hbm_arg(primal_start)],
        [vmem_out(*tile), vmem_out(TS, L), vmem_out(LINE * MSG, L), smem_out(8, L)],
        [vmem(512, 1024), vmem(1024, L), vmem(1024, L), pltpu.VMEM((8, L), jnp.int32)]
        + [pltpu.SemaphoreType.DMA((NRB,)), pltpu.SemaphoreType.DMA(())],
        8,
    )
    part = exchange(message, AXES, MSG, LINE_GROUPS)
    message, flags = call(
        users_kernel,
        "users",
        [smem_arg(own_ids), smem_arg(ids), vmem_arg(picked), vmem_arg(other), part],
        [vmem_out(PLANE * TS, L), smem_out(6)],
        [vmem((BLOCKS + 1) * 8, L)] * 4,
    )
    primal, sums, tail = call(
        second_kernel,
        "second",
        [smem_arg(flags), exchange(message, AXES[1:3], TS), vmem_arg(base), vmem_arg(usum)],
        [(f32(*tile), pl.BlockSpec(memory_space=pl.ANY))] + [vmem_out(TS, L), vmem_out(TAIL, 1024)],
        [vmem(1024 - TAIL, 1024), vmem(TS, L), vmem(1024, L), vmem(1024, L)]
        + [pltpu.SemaphoreType.DMA((2 * NRB - TAIL // RB,))],
        8,
    )
    (primal,) = call(
        store_kernel,
        "store",
        [vmem_arg(tail), hbm_arg(primal)],
        [(f32(*tile), pl.BlockSpec(memory_space=pl.ANY))],
        [pltpu.SemaphoreType.DMA(())],
        aliases={1: 0},
    )
    (message,) = call(
        owners_kernel,
        "owners",
        [smem_arg(ids), vmem_arg(sums), vmem_arg(swap(sums)), hbm_arg(primal)],
        [vmem_out(CHIPS * OUT, L)],
    )
    adv_out, slot_out = call(
        last_kernel,
        "last",
        [smem_arg(flags), exchange(message, AXES[:3], OUT), vmem_arg(bias), vmem_arg(bounds)],
        [(f32(AR, L), IN_VMEM), (f32(SR, L), IN_VMEM)],
    )
    return primal, adv_out.reshape(1, 512), slot_out.reshape(1, 1024)


def solution(mesh):
    return jax.shard_map(
        body,
        mesh=Mesh(mesh.devices.reshape(4, 4, 4, 2), AXES),
        in_specs=(
            P(AXES, None, None),
            P(AXES, None, None),
            P(AXES, None, None),
            P(AXES),
            P(AXES),
            P(AXES, None),
            P(AXES, None),
            P(AXES, None),
            P(AXES, None),
        ),
        out_specs=(P(AXES, None, None), P(AXES, None), P(AXES, None)),
        check_vma=False,
    )
```
